32 devices in a mesh: rep: 4 (over y, x), shard: 8 (over z, core).
Axes of the slice: x: 2, y: 2, z: 4, core: 2. Of those that a mesh axis runs over, the one named last changes fastest.
Arguments:
- tokens: bfloat16 [8192, 2048], P(('rep', 'shard')), may hold values from -6 to 6
- lengths: int32 [32], P(('rep', 'shard')), may hold values from 128 to 256, as said below
- routes: int32 [8192, 8], P(('rep', 'shard')), may hold values from 0 to 15, all different within a row; in each aligned block of 256 rows (0 to 255, 256 to 511, ...) at most 144 rows name the same one
- gain_attn: float32 [2048], replicated, may hold values from 0.1 to 1.9
- gain_query: float32 [128], replicated, may hold values from 0.1 to 1.9
- gain_key: float32 [128], replicated, may hold values from 0.1 to 1.9
- w_query: bfloat16 [2048, 2048], P(None, 'shard'), may hold values from -0.125 to 0.125
- w_key: bfloat16 [2048, 2048], P(None, 'shard'), may hold values from -0.125 to 0.125
- w_value: bfloat16 [2048, 2048], P(None, 'shard'), may hold values from -0.125 to 0.125
- w_out: bfloat16 [2048, 2048], P('shard'), may hold values from -0.75 to 0.75
- gain_moe: float32 [2048], replicated, may hold values from 0.1 to 1.9
- w_router: bfloat16 [2048, 16], replicated, may hold values from -0.0625 to 0.0625
- w_gate: bfloat16 [16, 2048, 1024], P('shard'), may hold values from -0.125 to 0.125
- w_up: bfloat16 [16, 2048, 1024], P('shard'), may hold values from -0.125 to 0.125
- w_down: bfloat16 [16, 1024, 2048], P('shard'), may hold values from -1.5 to 1.5
- out_grad: bfloat16 [8192, 2048], P(('rep', 'shard')), may hold values from -6 to 6
Outputs:
- output: bfloat16 [8192, 2048], P(('rep', 'shard'))
- input_grad: float32 [8192, 2048], P(('rep', 'shard'))
- grad_gain_attn: float32 [2048], replicated
- grad_gain_query: float32 [128], replicated
- grad_gain_key: float32 [128], replicated
- grad_w_query: float32 [2048, 2048], P(None, 'shard')
- grad_w_key: float32 [2048, 2048], P(None, 'shard')
- grad_w_value: float32 [2048, 2048], P(None, 'shard')
- grad_w_out: float32 [2048, 2048], P('shard')
- grad_gain_moe: float32 [2048], replicated
- grad_w_router: float32 [2048, 16], replicated
- grad_w_gate: float32 [16, 2048, 1024], P('shard')
- grad_w_up: float32 [16, 2048, 1024], P('shard')
- grad_w_down: float32 [16, 1024, 2048], P('shard')
The draws below stay inside these ranges and needn't reach their ends.
Inputs may be any that keep to these rules, and one draw needn't show every extreme that they name: `lengths`: valid tokens of each sequence; some sequence is full. `routes`: each row names 8 different experts; among the 256 rows of one sequence no expert is named by more than 144 rows, a bound that some block reaches.
All inputs are finite; a program needn't handle non-finite values.
Results may differ from the reference program's by a relative error of at most 0.024.
Values may be sent and summed in bfloat16 or wider, within the bound.
A program may use at most 320 MiB of HBM per device.

```python
import math
import jax
import jax.numpy as jnp
import numpy as np
from jax import lax

D = 2048
HD = 128
F = 1024
TOPK = 8
EXPERTS = 16
TOK_DEV = 256
CAP = 144
SEQS = 32
TOKENS = 8192
N_REP = 4
N_SHARD = 8


def draw_lengths(key, part):
    key_vals, key_spot = jax.random.split(key)
    drawn = jax.random.randint(key_vals, (SEQS,), TOK_DEV // 2, TOK_DEV + 1, dtype=jnp.int32)
    full_spot = jax.random.randint(key_spot, (), 0, SEQS, dtype=jnp.int32)
    return drawn.at[full_spot].set(TOK_DEV)


def shard_levels(own_key, shape, shards, low, top_value):
    def one(dim, shards_of):
        draws = jax.random.uniform(jax.random.fold_in(jax.random.fold_in(own_key, 6), dim), (shards_of,), jnp.float32, low / len(shards), top_value / len(shards))
        return jnp.repeat(jnp.exp(draws), shape[dim] // shards_of).reshape((-1,) + (1,) * (len(shape) - dim - 1))

    level = one(*shards[0])
    for cut in shards[1:]:
        level = level * one(*cut)
    return level


def shared_out(own_key, own, number, rows, number_of, top, most, slope):
    sequence = jax.random.permutation(own_key, number_of)
    crowded, usual = load_shares(number_of, rows * top, most, slope, True), load_shares(number_of, rows * top, most, slope, False)
    places = jnp.arange(number_of)

    def named(sizes, offset_by):
        used = int((sizes > 0).sum())
        fixed = max(1, used // 4)
        passed = fixed + (places - fixed + offset_by * (used - fixed)) % max(1, number_of - fixed)
        return jnp.zeros((number_of,), jnp.int32).at[sequence[jnp.where(places < fixed, places, passed)]].set(jnp.asarray(sizes, jnp.int32))

    sizes = jnp.where(number % 4 == 0, named(crowded, number // 4), named(usual, number - number // 4 - 1))
    mixed = jax.random.permutation(jax.random.fold_in(own, 3), number_of)
    donor, receiver = mixed[0:number_of // 2 * 2:2], mixed[1:number_of // 2 * 2:2]
    margin = jnp.minimum(sizes[donor] - 1, most - sizes[receiver]) // 2
    margin = jnp.where((donor == sequence[0]) | (receiver == sequence[0]) | (sizes[receiver] == 0), 0, jnp.maximum(margin, 0))
    passed = jax.random.randint(jax.random.fold_in(own, 4), (number_of // 2,), 0, 1 << 20) % (margin + 1)
    sizes = sizes.at[donor].add(-passed).at[receiver].add(passed)
    items = jnp.searchsorted(jnp.cumsum(sizes), jnp.arange(rows * top), side="right").astype(jnp.int32)
    grid = items.reshape(top, rows).T
    grid = grid[jax.random.permutation(jax.random.fold_in(own, 1), rows)]
    offset_by = jax.random.randint(jax.random.fold_in(own, 2), (rows, 1), 0, top)
    return jnp.take_along_axis(grid, (jnp.arange(top)[None, :] + offset_by) % top, axis=1)


def load_shares(number_of, total, most, skew, full):
    portions = [(1 << 20) // math.isqrt(rank ** skew) + 1 for rank in range(1, number_of + 1)]
    largest = most if full else min(most, max(-(-total // number_of), total * portions[0] // sum(portions)))
    least = 1 if total - largest >= number_of - 1 else 0
    counts, surplus = [largest] + [least] * (number_of - 1), total - largest - least * (number_of - 1)
    while surplus > 0:
        candidates = [i for i in range(1, number_of) if counts[i] < largest] or [i for i in range(1, number_of) if counts[i] < most]
        whole, remaining = sum([portions[i] for i in candidates]), surplus
        for i in candidates:
            extra = min(most - counts[i], max(1, remaining * portions[i] // whole), surplus)
            counts[i] = counts[i] + extra
            surplus = surplus - extra
    return np.array(counts)


def noise(stream_key, shape, deviation, limit, cuts=(), kind=jnp.bfloat16):
    loudness = shard_levels(stream_key, shape, cuts, -0.22, 0.18) if cuts else 1.0
    array = jax.random.normal(stream_key, shape, jnp.float32) * deviation * loudness
    return jnp.minimum(jnp.maximum(array, -limit), limit).astype(kind)


def setup_inputs(seed: int = 0) -> dict:
    arg_keys = jax.random.split(jax.random.key(seed), 17)
    tokens = noise(arg_keys[0], (TOKENS, D), 1.0, 6.0, ((0, 32),))
    lengths = draw_lengths(jax.random.fold_in(arg_keys[16], 71), 0)
    routes_keys = jax.random.split(jax.random.fold_in(arg_keys[2], 1), TOKENS // TOK_DEV)
    routes_turns = jax.random.permutation(jax.random.fold_in(arg_keys[2], 3), TOKENS // TOK_DEV)
    routes = jax.vmap(lambda own, number: shared_out(jax.random.fold_in(arg_keys[2], 2), own, number, TOK_DEV, EXPERTS, TOPK, CAP, 2))(routes_keys, routes_turns).reshape((TOKENS, TOPK))
    gain_attn = jnp.clip(1.0 + 0.18 * jax.random.normal(arg_keys[3], (D,), jnp.float32), 0.1, 1.9)
    gain_query = jnp.clip(1.0 + 0.18 * jax.random.normal(arg_keys[4], (HD,), jnp.float32), 0.1, 1.9)
    gain_key = jnp.clip(1.0 + 0.18 * jax.random.normal(arg_keys[5], (HD,), jnp.float32), 0.1, 1.9)
    w_query = noise(arg_keys[6], (D, D), D ** -0.5, 0.125, ((1, 8),))
    w_key = noise(arg_keys[7], (D, D), D ** -0.5, 0.125, ((1, 8),))
    w_value = noise(arg_keys[8], (D, D), D ** -0.5, 0.125, ((1, 8),))
    w_out = noise(arg_keys[9], (D, D), (D // 32) ** -0.5, 0.75, ((0, 8),))
    gain_moe = jnp.clip(1.0 + 0.18 * jax.random.normal(arg_keys[10], (D,), jnp.float32), 0.1, 1.9)
    w_router = noise(arg_keys[11], (D, EXPERTS), (4 * D) ** -0.5, 0.0625)
    w_gate = noise(arg_keys[12], (EXPERTS, D, F), D ** -0.5, 0.125, ((0, 8),))
    w_up = noise(arg_keys[13], (EXPERTS, D, F), D ** -0.5, 0.125, ((0, 8),))
    w_down = noise(arg_keys[14], (EXPERTS, F, D), (max(F // 64, 1)) ** -0.5, 1.5, ((0, 8),))
    out_grad = noise(arg_keys[15], (TOKENS, D), 1.0, 6.0, ((0, 32),))
    return {"tokens": tokens, "lengths": lengths, "routes": routes, "gain_attn": gain_attn, "gain_query": gain_query, "gain_key": gain_key, "w_query": w_query, "w_key": w_key, "w_value": w_value, "w_out": w_out, "gain_moe": gain_moe, "w_router": w_router, "w_gate": w_gate, "w_up": w_up, "w_down": w_down, "out_grad": out_grad}


EPS_NORM = 1e-06
ROPE_BASE = 50000.0
MASKED = -1e+30

@jax.custom_vjp
def low(v):
    return lax.optimization_barrier(v.astype(jnp.bfloat16)).astype(jnp.float32)

@jax.custom_vjp
def low_back(v):
    return v

def low_keep(v):
    return (low(v), None)

def low_pass(kept, grad):
    return (grad,)

def back_keep(v):
    return (v, None)

def back_low(kept, grad):
    return (low(grad),)
low.defvjp(low_keep, low_pass)
low_back.defvjp(back_keep, back_low)

def rms_scale(values, gain_vec):
    return values * lax.rsqrt(lax.optimization_barrier(jnp.mean(values * values, axis=-1, keepdims=True)) + EPS_NORM) * gain_vec

def rope_tables(seq_len, head_dim):
    half_dim = head_dim // 2
    places = jnp.arange(seq_len, dtype=jnp.float32)
    freqs = ROPE_BASE ** (-jnp.arange(half_dim, dtype=jnp.float32) * (2.0 / head_dim))
    angles = places[:, None] * freqs[None, :]
    cos_tab = jnp.concatenate([jnp.cos(angles), jnp.cos(angles)], axis=-1)
    sine_tab = jnp.concatenate([jnp.sin(angles), jnp.sin(angles)], axis=-1)
    return (cos_tab, sine_tab)

def rotate_half(values, cos_tab, sine_tab):
    half_dim = values.shape[-1] // 2
    turned = jnp.concatenate([-values[..., half_dim:], values[..., :half_dim]], axis=-1)
    return values * cos_tab[:, None, :] + turned * sine_tab[:, None, :]

def head_prepare(raw_proj, gain_vec, cos_tab, sine_tab):
    return rotate_half(rms_scale(raw_proj, gain_vec), cos_tab, sine_tab)

def soft_max(logit_vals):
    upper = lax.optimization_barrier(jnp.max(logit_vals, axis=-1, keepdims=True))
    expo = jnp.exp(logit_vals - upper)
    return expo / lax.optimization_barrier(jnp.sum(expo, axis=-1, keepdims=True))

def slot_table(route_rows):
    flat_ids = route_rows.reshape(-1).astype(jnp.int32)
    one_hot = (flat_ids[:, None] == jnp.arange(EXPERTS, dtype=jnp.int32)[None, :]).astype(jnp.int32)
    before = jnp.cumsum(one_hot, axis=0) - one_hot
    ranks = lax.optimization_barrier(jnp.sum(before * one_hot, axis=1))
    return (flat_ids * CAP + ranks).astype(jnp.int32)

def layer_forward(params, inputs, seq_lens, route_rows):
    gain_attn, gain_query, gain_key, w_query, w_key, w_value, w_out, gain_moe, w_router, w_gate, w_up, w_down = params
    group_size, seq_len, model_width = inputs.shape
    head_dim = gain_query.shape[0]
    head_count = model_width // head_dim
    four_shape = (group_size, seq_len, head_count, head_dim)
    cos_tab, sine_tab = rope_tables(seq_len, head_dim)
    highest = lax.Precision.HIGHEST
    normed = low(rms_scale(inputs, gain_attn))

    def project(weight_mat):
        return jnp.einsum('gtd,de->gte', normed, weight_mat, precision=highest)
    query_raw = low_back(project(w_query)).reshape(four_shape)
    key_raw = low_back(project(w_key)).reshape(four_shape)
    value_low = low_back(low(project(w_value))).reshape(four_shape)
    query_rot = low(head_prepare(query_raw, gain_query, cos_tab, sine_tab))
    key_rot = low(head_prepare(key_raw, gain_key, cos_tab, sine_tab))
    scores = jnp.einsum('gqhd,gkhd->ghqk', query_rot, key_rot, precision=highest) * head_dim ** (-0.5)
    key_valid = jnp.arange(seq_len, dtype=jnp.int32)[None, :] < seq_lens[:, None]
    scores = low_back(jnp.where(key_valid[:, None, None, :], scores, MASKED))
    weights = low(soft_max(scores))
    attended = low_back(low(jnp.einsum('ghqk,gkhd->gqhd', weights, value_low, precision=highest)))
    attended = attended.reshape(group_size, seq_len, model_width)
    branch = low_back(jnp.einsum('gtd,de->gte', attended, w_out, precision=highest))
    hidden = inputs + branch
    normed_moe = low(rms_scale(hidden, gain_moe))
    router_probs = soft_max(jnp.einsum('gtd,de->gte', normed_moe, w_router, precision=highest))
    expert_ids = jnp.arange(EXPERTS, dtype=jnp.int32)
    route_hot = (route_rows[..., None] == expert_ids).astype(jnp.float32)
    gate_vals = lax.optimization_barrier(jnp.sum(router_probs[:, :, None, :] * route_hot, axis=-1))
    slot_ids = jax.vmap(slot_table)(route_rows)
    copies = jnp.repeat(normed_moe, TOPK, axis=1)

    def place(slot_row, copy_rows):
        return jnp.zeros((EXPERTS * CAP, model_width), jnp.float32).at[slot_row].set(copy_rows)
    buffer = low_back(jax.vmap(place)(slot_ids, copies)).reshape(group_size, EXPERTS, CAP, model_width)
    gate_act = low_back(jnp.einsum('gecd,edf->gecf', buffer, w_gate, precision=highest))
    up_act = low_back(jnp.einsum('gecd,edf->gecf', buffer, w_up, precision=highest))
    joined = low(gate_act * jax.nn.sigmoid(gate_act) * up_act)
    expert_out = low_back(low(jnp.einsum('gecf,efd->gecd', joined, w_down, precision=highest)))
    expert_out = expert_out.reshape(group_size, EXPERTS * CAP, model_width)
    picked = jnp.take_along_axis(expert_out, slot_ids[:, :, None], axis=1)
    picked = picked.reshape(group_size, seq_len, TOPK, model_width)
    mixture = lax.optimization_barrier(jnp.sum(picked * gate_vals[..., None], axis=2))
    return hidden + mixture

def reference(tokens, lengths, routes, gain_attn, gain_query, gain_key, w_query, w_key, w_value, w_out, gain_moe, w_router, w_gate, w_up, w_down, out_grad):
    seq_count = N_REP * N_SHARD
    group_size = math.gcd(seq_count, max(1, 2048 // TOK_DEV))
    step_count = seq_count // group_size
    params = tuple((weight_arr.astype(jnp.float32) for weight_arr in (gain_attn, gain_query, gain_key, w_query, w_key, w_value, w_out, gain_moe, w_router, w_gate, w_up, w_down)))
    block_inputs = tokens.astype(jnp.float32).reshape(step_count, group_size, TOK_DEV, D)
    block_lengths = lengths.astype(jnp.int32).reshape(step_count, group_size)
    block_routes = routes.astype(jnp.int32).reshape(step_count, group_size, TOK_DEV, TOPK)
    block_grads = out_grad.astype(jnp.float32).reshape(step_count, group_size, TOK_DEV, D)
    zero_grads = jax.tree.map(jnp.zeros_like, params)

    def add_up(running, fresh):
        return running + fresh

    def one_step(carry, batch):
        step_in, step_lens, step_routes, step_dy = batch

        def inner(param_set, layer_in):
            return layer_forward(param_set, layer_in, step_lens, step_routes)
        out_vals, pull_back = jax.vjp(inner, params, step_in)
        valid = (jnp.arange(TOK_DEV, dtype=jnp.int32)[None, :] < step_lens[:, None]).astype(jnp.float32)
        param_grads, input_grad = pull_back(step_dy * valid[..., None])
        carry = jax.tree.map(add_up, carry, param_grads)
        return (carry, (out_vals, input_grad))
    totals, (outs_all, grads_all) = lax.scan(one_step, zero_grads, (block_inputs, block_lengths, block_routes, block_grads))
    return (outs_all.reshape(TOKENS, D).astype(jnp.bfloat16), grads_all.reshape(TOKENS, D), totals[0], totals[1], totals[2], totals[3], totals[4], totals[5], totals[6], totals[7], totals[8], totals[9], totals[10], totals[11])
```

```python
import functools

import jax
import jax.numpy as jnp
from jax import lax
from jax.experimental import pallas as pl
from jax.experimental.pallas import tpu as pltpu
from jax.sharding import PartitionSpec as P

CAP = 144
LINES = 16
EPS_NORM = 1e-06
ROPE_BASE = 50000.0
MASKED = -1e30
VMEM_BYTES = 60 * 1024 * 1024
LOW = jnp.bfloat16
WIDE = jnp.float32
COST = pl.CostEstimate(flops=1 << 20, bytes_accessed=1 << 16, transcendentals=0)


def dot_nn(a, b):
    return lax.dot_general(a, b, (((1,), (0,)), ((), ())), preferred_element_type=WIDE)


def dot_nt(a, b):
    return lax.dot_general(a, b, (((1,), (1,)), ((), ())), preferred_element_type=WIDE)


def dot_tn(a, b):
    return lax.dot_general(a, b, (((0,), (0,)), ((), ())), preferred_element_type=WIDE)


def rope_tables(seq_len, head_dim):
    half_dim = head_dim // 2
    places = jnp.arange(seq_len, dtype=WIDE)
    freqs = ROPE_BASE ** (-jnp.arange(half_dim, dtype=WIDE) * (2.0 / head_dim))
    angles = places[:, None] * freqs[None, :]
    cosine, sine = (jnp.cos(angles), jnp.sin(angles))
    return (
        jnp.concatenate([cosine, cosine], axis=-1),
        jnp.concatenate([-sine, sine], axis=-1),
    )


def head_forward(raw, gain, cos_tab, sin_tab):
    scale = lax.rsqrt(jnp.mean(raw * raw, axis=-1, keepdims=True) + EPS_NORM)
    plain = raw * scale
    scaled = plain * gain
    turned = pltpu.roll(scaled, raw.shape[-1] // 2, axis=1)
    return (scaled * cos_tab + turned * sin_tab, plain, scale)


def head_backward(grad, plain, scale, gain, cos_tab, sin_tab):
    back = grad * cos_tab + pltpu.roll(grad * sin_tab, grad.shape[-1] // 2, axis=1)
    gain_grad = jnp.sum(back * plain, axis=0, keepdims=True)
    back = back * gain
    raw_grad = scale * (back - plain * jnp.mean(back * plain, axis=-1, keepdims=True))
    return (raw_grad, gain_grad)


def soft_weights(query, key, length, score_scale):
    scores = dot_nt(query, key) * score_scale
    places = lax.broadcasted_iota(jnp.int32, scores.shape, 1).astype(WIDE)
    scores = jnp.where(places < length, scores, MASKED)
    expo = jnp.exp(scores - jnp.max(scores, axis=-1, keepdims=True))
    return expo / jnp.sum(expo, axis=-1, keepdims=True)


def attend_block(normed, length, wq, wk, wv, wo, gq, gk, cos_tab, sin_tab, keep):
    head_dim = gq.shape[-1]
    query_raw, key_raw = (dot_nn(normed, wq[...]), dot_nn(normed, wk[...]))
    value = dot_nn(normed, wv[...]).astype(LOW)
    heads = []
    for head in range(query_raw.shape[-1] // head_dim):
        span = slice(head * head_dim, (head + 1) * head_dim)
        query = head_forward(query_raw[:, span], gq, cos_tab, sin_tab)[0].astype(LOW)
        key = head_forward(key_raw[:, span], gk, cos_tab, sin_tab)[0].astype(LOW)
        weights = soft_weights(query, key, length, head_dim**-0.5).astype(LOW)
        heads.append(dot_nn(weights, value[:, span]).astype(LOW))
    joined = heads[0] if len(heads) == 1 else jnp.concatenate(heads, axis=-1)
    keep(query_raw, key_raw, value, joined)
    return dot_nn(joined, wo[...]).astype(LOW)


def attend_kernel(
    pk_ref, wq, wk, wv, wo, gq, gk, cos_ref, sin_ref, part_ref, qr_ref, kr_ref, v_ref, o_ref
):
    rows = pk_ref.shape[1] - LINES
    length = pk_ref[0, rows:, rows : rows + 128].astype(WIDE)[0:1, 0:1]

    def keep(query_raw, key_raw, value, joined):
        qr_ref[0], kr_ref[0], v_ref[0], o_ref[0] = (query_raw, key_raw, value, joined)

    part_ref[0] = attend_block(
        pk_ref[0, :rows], length, wq, wk, wv, wo, gq[...], gk[...], cos_ref[...], sin_ref[...], keep
    )


def whole_spec(array):
    return pl.BlockSpec(array.shape, lambda *_: (0,) * array.ndim, pipeline_mode=pl.Buffered(1))


def first_spec(array):
    return pl.BlockSpec((1,) + array.shape[1:], lambda i: (i,) + (0,) * (array.ndim - 1))


def attend_forward(packets, wq, wk, wv, wo, gq, gk, cos_tab, sin_tab):
    count, lines, width = packets.shape
    rows, wide = (lines - LINES, wq.shape[1])
    fixed = (wq, wk, wv, wo, gq, gk, cos_tab, sin_tab)
    out = (
        jax.ShapeDtypeStruct((count, rows, width), LOW),
        jax.ShapeDtypeStruct((count, rows, wide), WIDE),
        jax.ShapeDtypeStruct((count, rows, wide), WIDE),
        jax.ShapeDtypeStruct((count, rows, wide), LOW),
        jax.ShapeDtypeStruct((count, rows, wide), LOW),
    )
    return pl.pallas_call(
        attend_kernel,
        grid=(count,),
        in_specs=[first_spec(packets)] + [whole_spec(array) for array in fixed],
        out_specs=[first_spec(array) for array in out],
        out_shape=out,
        compiler_params=pltpu.CompilerParams(vmem_limit_bytes=VMEM_BYTES),
        cost_estimate=COST,
        name="attend_forward",
    )(packets, *fixed)


def attend_back_kernel(
    da_ref, pk_ref, qr_ref, kr_ref, v_ref, o_ref,
    wq, wk, wv, wo, gq, gk, cos_ref, sin_ref,
    part_ref, gw_in, gw_out, gain_q, gain_k, gain_n,
):
    rows = pk_ref.shape[1] - LINES
    head_dim = gq.shape[-1]
    length = pk_ref[0, rows:, rows : rows + 128].astype(WIDE)[0:1, 0:1]
    cos_tab, sin_tab = (cos_ref[...], sin_ref[...])
    score_scale = head_dim**-0.5

    @pl.when(pl.program_id(0) == 0)
    def _():
        for ref in (gw_in, gw_out, gain_q, gain_k, gain_n):
            ref[...] = jnp.zeros_like(ref)

    upper = da_ref[0]
    grad_joined = dot_nt(upper, wo[...]).astype(LOW)
    gw_out[...] += dot_tn(o_ref[0], upper)
    grads_q, grads_k, grads_v = ([], [], [])
    for head in range(qr_ref.shape[-1] // head_dim):
        span = slice(head * head_dim, (head + 1) * head_dim)
        query, plain_q, scale_q = head_forward(qr_ref[0, :, span], gq[...], cos_tab, sin_tab)
        key, plain_k, scale_k = head_forward(kr_ref[0, :, span], gk[...], cos_tab, sin_tab)
        query, key, value = (query.astype(LOW), key.astype(LOW), v_ref[0, :, span])
        probs = soft_weights(query, key, length, score_scale)
        grad_out = grad_joined[:, span]
        grads_v.append(dot_tn(probs.astype(LOW), grad_out).astype(LOW))
        grad_probs = dot_nt(grad_out, value)
        inner = jnp.sum(probs * grad_probs, axis=-1, keepdims=True)
        grad_scores = (probs * (grad_probs - inner)).astype(LOW)
        grad_q, head_gain_q = head_backward(
            dot_nn(grad_scores, key) * score_scale, plain_q, scale_q, gq[...], cos_tab, sin_tab
        )
        grad_k, head_gain_k = head_backward(
            dot_tn(grad_scores, query) * score_scale, plain_k, scale_k, gk[...], cos_tab, sin_tab
        )
        gain_q[...] += head_gain_q
        gain_k[...] += head_gain_k
        grads_q.append(grad_q.astype(LOW))
        grads_k.append(grad_k.astype(LOW))
    wide = qr_ref.shape[-1]
    grads = jnp.concatenate(grads_q + grads_k + grads_v, axis=-1)
    part = (
        dot_nt(grads[:, :wide], wq[...])
        + dot_nt(grads[:, wide : 2 * wide], wk[...])
        + dot_nt(grads[:, 2 * wide :], wv[...])
    )
    normed = pk_ref[0, :rows]
    part_ref[0] = part.astype(LOW)
    gain_n[...] += jnp.sum(part * normed.astype(WIDE), axis=0, keepdims=True)
    gw_in[...] += dot_tn(normed, grads)


def attend_backward(upper, packets, kept, wq, wk, wv, wo, gq, gk, cos_tab, sin_tab):
    count, lines, width = packets.shape
    rows, wide = (lines - LINES, wq.shape[1])
    blocks = (upper, packets) + tuple(kept)
    fixed = (wq, wk, wv, wo, gq, gk, cos_tab, sin_tab)
    sums = tuple(
        jax.ShapeDtypeStruct(shape, WIDE)
        for shape in ((width, 3 * wide), wo.shape, gq.shape, gk.shape, (1, width))
    )
    return pl.pallas_call(
        attend_back_kernel,
        grid=(count,),
        in_specs=[first_spec(array) for array in blocks] + [whole_spec(array) for array in fixed],
        out_specs=[first_spec(upper)] + [whole_spec(array) for array in sums],
        out_shape=(jax.ShapeDtypeStruct((count, rows, width), LOW),) + sums,
        compiler_params=pltpu.CompilerParams(vmem_limit_bytes=VMEM_BYTES),
        cost_estimate=COST,
        name="attend_backward",
    )(*blocks, *fixed)


def slot_spots(table, expert):
    row_count = table.shape[1]
    slots = lax.broadcasted_iota(jnp.int32, (CAP, row_count), 0).astype(WIDE) + 1.0
    mine = lax.broadcasted_iota(jnp.int32, table.shape, 0) == expert
    ranks = jnp.sum(jnp.where(mine, table, 0.0), axis=0, keepdims=True)
    return (slots == ranks).astype(LOW)


def expert_kernel(counts, batch, ex_ref, wg, wu, wd, wr, *refs):
    sources = len(counts)
    rows_in, cots_in = (refs[:sources], refs[sources : 2 * sources])
    x_ref, y_ref, m_ref, dg_ref, du_ref, dgate_ref, rows_buf, cots_buf, sems = refs[2 * sources :]
    steps = sum(counts) // batch
    turn = pl.program_id(0) * steps + pl.program_id(1)
    slot = lax.rem(turn, 2)
    row_count = rows_buf.shape[2]

    def copies(source, offset, place):
        span = pl.ds(offset, batch)
        return (
            pltpu.make_async_copy(rows_in[source].at[span], rows_buf.at[place], sems.at[0, place]),
            pltpu.make_async_copy(cots_in[source].at[span], cots_buf.at[place], sems.at[1, place]),
        )

    def fetch(step, place):
        begin = 0
        for source, count in enumerate(counts):
            size = count // batch

            @pl.when((step >= begin) & (step < begin + size))
            def _(source=source, begin=begin):
                for copy in copies(source, (step - begin) * batch, place):
                    copy.start()

            begin += size

    @pl.when(turn == 0)
    def _():
        fetch(turn, slot)

    @pl.when(turn + 1 < pl.num_programs(0) * steps)
    def _():
        fetch(lax.rem(turn + 1, steps), 1 - slot)

    for copy in copies(0, 0, slot):
        copy.wait()
    hidden = wg.shape[-1]
    expert = ex_ref[pl.program_id(0)]
    for seq in range(batch):
        table = cots_buf[slot, seq, row_count:, :row_count].astype(WIDE)
        spots = slot_spots(table, expert)
        span = pl.ds(seq * CAP, CAP)
        x_ref[0, span] = dot_nn(spots, rows_buf[slot, seq]).astype(LOW)
        y_ref[0, span] = dot_nn(spots, cots_buf[slot, seq, :row_count]).astype(LOW)
    x_all, y_all = (x_ref[0], y_ref[0])
    logits = dot_nn(x_all, wr[...])
    expo = jnp.exp(logits - jnp.max(logits, axis=-1, keepdims=True))
    chosen = lax.broadcasted_iota(jnp.int32, expo.shape, 1) == expert
    gates = jnp.sum(jnp.where(chosen, expo, 0.0), axis=-1, keepdims=True) / jnp.sum(
        expo, axis=-1, keepdims=True
    )
    step = min(256, hidden)
    dgate = jnp.zeros((x_all.shape[0], 1), WIDE)
    for start in range(0, hidden, step):
        span = slice(start, start + step)
        gate_act, up_act = (dot_nn(x_all, wg[0, :, span]), dot_nn(x_all, wu[0, :, span]))
        plain_grad = dot_nt(y_all, wd[0, span, :])
        sig = jax.nn.sigmoid(gate_act)
        silu = gate_act * sig
        joined = silu * up_act
        dgate += jnp.sum(joined * plain_grad, axis=-1, keepdims=True)
        grad = plain_grad * gates
        m_ref[0, :, span] = (joined * gates).astype(LOW)
        dg_ref[0, :, span] = (grad * up_act * (sig + silu * (1.0 - sig))).astype(LOW)
        du_ref[0, :, span] = (grad * silu).astype(LOW)
    dgate_ref[0] = jnp.broadcast_to(dgate, dgate_ref.shape[1:])


def expert_acts(ids, rows, cots, wg, wu, wd, wr, batch=4):
    row_count, width = rows[0].shape[1:]
    counts = tuple(array.shape[0] for array in rows)
    count = sum(counts)
    own, _, hidden = wg.shape
    out_rows = batch * CAP

    def acts(cols, kind=LOW):
        return jax.ShapeDtypeStruct((own, count * CAP, cols), kind)

    def act_spec(cols):
        return pl.BlockSpec((1, out_rows, cols), lambda e, i: (e, i, 0))

    def weight_spec(array):
        return pl.BlockSpec(
            (1,) + array.shape[1:], lambda e, i: (e, 0, 0), pipeline_mode=pl.Buffered(1)
        )

    any_spec = pl.BlockSpec(memory_space=pl.ANY)
    columns = (width, width, hidden, hidden, hidden, 128)
    return pl.pallas_call(
        functools.partial(expert_kernel, counts, batch),
        grid=(own, count // batch),
        in_specs=[
            pl.BlockSpec(memory_space=pltpu.SMEM),
            weight_spec(wg),
            weight_spec(wu),
            weight_spec(wd),
            pl.BlockSpec(wr.shape, lambda e, i: (0, 0)),
        ]
        + [any_spec] * (2 * len(counts)),
        out_specs=[act_spec(cols) for cols in columns],
        out_shape=tuple(acts(cols) for cols in columns[:5]) + (acts(128, WIDE),),
        scratch_shapes=[
            pltpu.VMEM((2, batch) + rows[0].shape[1:], LOW),
            pltpu.VMEM((2, batch) + cots[0].shape[1:], LOW),
            pltpu.SemaphoreType.DMA((2, 2)),
        ],
        compiler_params=pltpu.CompilerParams(vmem_limit_bytes=VMEM_BYTES),
        cost_estimate=COST,
        name="expert_acts",
    )(ids, wg, wu, wd, wr, *rows, *cots)


def pull_kernel(ex_ref, rows_ref, cot_ref, dg_ref, du_ref, dgate_ref, wg, wu, wr, part_ref, router):
    batch, row_count, _ = rows_ref.shape
    own = wg.shape[0]

    @pl.when(pl.program_id(0) == 0)
    def _():
        router[...] = jnp.zeros_like(router)

    backs = [
        (dot_nt(dg_ref[e], wg[e]) + dot_nt(du_ref[e], wu[e])).astype(LOW) for e in range(own)
    ]
    for seq in range(batch):
        table = cot_ref[seq, :, :row_count].astype(WIDE)
        logits = dot_nn(rows_ref[seq], wr[...])
        expo = jnp.exp(logits - jnp.max(logits, axis=-1, keepdims=True))
        probs = expo / jnp.sum(expo, axis=-1, keepdims=True)
        columns = lax.broadcasted_iota(jnp.int32, probs.shape, 1)
        grad_logits = jnp.zeros_like(probs)
        span = slice(seq * CAP, (seq + 1) * CAP)
        total = jnp.zeros(part_ref.shape[1:], WIDE)
        for e in range(own):
            spots = slot_spots(table, ex_ref[e])
            total += dot_tn(spots, backs[e][span])
            dgate = dgate_ref[e, span]
            high = dgate.astype(LOW)
            rest = (dgate - high.astype(WIDE)).astype(LOW)
            at_rows = (dot_tn(spots, high) + dot_tn(spots, rest))[:, : probs.shape[1]]
            chosen = (columns == ex_ref[e]).astype(WIDE)
            prob = jnp.sum(probs * chosen, axis=-1, keepdims=True)
            grad_logits += at_rows * prob * (chosen - probs)
        low_logits = grad_logits.astype(LOW)
        part_ref[seq] = (total + dot_nt(low_logits, wr[...])).astype(LOW)
        router[...] += dot_tn(rows_ref[seq], low_logits)


def mix_kernel(ex_ref, cot_ref, m_ref, wd, part_ref):
    batch, row_count, _ = part_ref.shape
    own = wd.shape[0]
    outs = [dot_nn(m_ref[e], wd[e]).astype(LOW) for e in range(own)]
    for seq in range(batch):
        table = cot_ref[seq, :, :row_count].astype(WIDE)
        span = slice(seq * CAP, (seq + 1) * CAP)
        total = sum(dot_tn(slot_spots(table, ex_ref[e]), outs[e][span]) for e in range(own))
        part_ref[seq] = total.astype(LOW)


def spread_call(kernel, name, ids, by_seq, cots, by_slot, fixed, router_shape, batch=2):
    count, lines, width = cots.shape
    row_count = lines - LINES
    part = jax.ShapeDtypeStruct((count, row_count, width), LOW)

    def seq_spec(array):
        return pl.BlockSpec((batch,) + array.shape[1:], lambda i: (i, 0, 0))

    def slot_spec(array):
        return pl.BlockSpec((array.shape[0], batch * CAP, array.shape[2]), lambda i: (0, i, 0))

    return pl.pallas_call(
        kernel,
        grid=(count // batch,),
        in_specs=[pl.BlockSpec(memory_space=pltpu.SMEM)]
        + [seq_spec(array) for array in by_seq]
        + [pl.BlockSpec((batch, LINES, width), lambda i: (i, row_count // LINES, 0))]
        + [slot_spec(array) for array in by_slot]
        + [whole_spec(array) for array in fixed],
        out_specs=[seq_spec(part)] + [whole_spec(shape) for shape in router_shape],
        out_shape=[part] + list(router_shape),
        compiler_params=pltpu.CompilerParams(vmem_limit_bytes=VMEM_BYTES),
        cost_estimate=COST,
        name=name,
    )(ids, *by_seq, cots, *by_slot, *fixed)


def weight_grad(lefts, rights):
    own, _, left_cols = lefts[0].shape
    right_cols = rights[0].shape[-1]
    sets = len(lefts)
    left_tile, right_tile = (min(512, left_cols), min(1024, right_cols))

    def kernel(*refs):
        refs[2 * sets][0] = sum(dot_tn(refs[i][0], refs[sets + i][0]) for i in range(sets))

    return pl.pallas_call(
        kernel,
        grid=(own, right_cols // right_tile, left_cols // left_tile),
        in_specs=[
            pl.BlockSpec((1, array.shape[1], left_tile), lambda e, r, l: (e, 0, l))
            for array in lefts
        ]
        + [
            pl.BlockSpec((1, array.shape[1], right_tile), lambda e, r, l: (e, 0, r))
            for array in rights
        ],
        out_specs=pl.BlockSpec((1, left_tile, right_tile), lambda e, r, l: (e, l, r)),
        out_shape=jax.ShapeDtypeStruct((own, left_cols, right_cols), WIDE),
        compiler_params=pltpu.CompilerParams(vmem_limit_bytes=VMEM_BYTES),
        cost_estimate=COST,
        name="weight_grad",
    )(*lefts, *rights)


def rms_parts(values):
    scale = lax.rsqrt(jnp.mean(values * values, axis=-1, keepdims=True) + EPS_NORM)
    return (values * scale, scale)


def rms_back(plain, scale, gain, grad):
    back = grad * gain
    return scale * (back - plain * jnp.mean(back * plain, axis=-1, keepdims=True))


def local(
    tokens, lengths, routes, gain_attn, gain_query, gain_key,
    w_query, w_key, w_value, w_out, gain_moe, w_router,
    w_gate, w_up, w_down, out_grad,
):
    row_count, width = tokens.shape
    head_dim = gain_query.shape[0]
    groups, replicas = (lax.axis_size("shard"), lax.axis_size("rep"))
    expert_count, own = (w_router.shape[1], w_gate.shape[0])
    wide = w_query.shape[1]
    after = lax.optimization_barrier
    gain_q, gain_k = (gain_query.reshape(1, -1), gain_key.reshape(1, -1))
    cos_tab, sin_tab = rope_tables(row_count, head_dim)
    ids = lax.axis_index("shard") * own + jnp.arange(own, dtype=jnp.int32)

    def flip_replica(values, bits):
        return lax.ppermute(values, "rep", [(i, i ^ bits) for i in range(replicas)])

    def flip_shard(values, bits):
        return lax.ppermute(values, "shard", [(i, i ^ bits) for i in range(groups)])

    def own_rail(blocks):
        pairs = blocks.reshape((groups // 2, 2) + blocks.shape[1:])
        return lax.dynamic_index_in_dim(pairs, lax.axis_index("shard") % 2, axis=1, keepdims=False)

    def foreign(blocks):
        rail = own_rail(blocks)
        mine = [flip_replica(rail, bits) for bits in (1, 2, 3)]
        return mine + [flip_shard(values, 1) for values in mine]

    def scatter_sum(parts):
        return lax.psum_scatter(
            parts.reshape(-1, width), "shard", scatter_dimension=0, tiled=True
        ).astype(WIDE)

    inputs = tokens.astype(WIDE)
    row_mask = (jnp.arange(row_count, dtype=jnp.int32) < lengths[0])[:, None]
    named = jnp.any(
        routes[None, :, :] == jnp.arange(expert_count, dtype=jnp.int32)[:, None, None], axis=-1
    )
    upto = (jnp.arange(row_count)[:, None] <= jnp.arange(row_count)[None, :]).astype(LOW)
    ranks = jnp.where(named, dot_nn(named.astype(LOW), upto), 0.0).astype(LOW)
    lines = jnp.concatenate(
        [ranks, jnp.broadcast_to(lengths[0].astype(LOW), (expert_count, width - row_count))], axis=1
    )
    plain_in, scale_in = rms_parts(inputs)
    packet = jnp.concatenate([(plain_in * gain_attn).astype(LOW), lines], axis=0)
    packets = lax.all_gather(packet, "shard", axis=0)
    cot_low = jnp.where(row_mask, out_grad, 0.0)
    cot_packet = jnp.concatenate([cot_low, lines], axis=0)
    cot_packet, packets = after((cot_packet, packets))
    cots = lax.all_gather(cot_packet, "shard", axis=0)

    heads = (w_query, w_key, w_value, w_out, gain_q, gain_k, cos_tab, sin_tab)
    part, *kept = attend_forward(packets, *heads)
    hidden = inputs + scatter_sum(part)
    plain_mid, scale_mid = rms_parts(hidden)
    moe_low = (plain_mid * gain_moe).astype(LOW)
    rows_all = lax.all_gather(moe_low, "shard", axis=0)

    share = replicas == 4
    acts = [expert_acts(ids, [rows_all], [cots], w_gate, w_up, w_down, w_router)]
    if share:
        far_rows, far_cots = (foreign(rows_all), foreign(cots))
    _, _, gated, grad_gate_act, grad_up_act, dgates = acts[0]
    router_shape = (jax.ShapeDtypeStruct(w_router.shape, WIDE),)
    pull_part, grad_router = spread_call(
        pull_kernel, "expert_pull", ids, (rows_all,), cots,
        (grad_gate_act, grad_up_act, dgates), (w_gate, w_up, w_router), router_shape,
    )
    grad_moe_in = scatter_sum(pull_part)
    gated, pull_part = after((gated, pull_part))
    (mix_part,) = spread_call(mix_kernel, "expert_mix", ids, (), cots, (gated,), (w_down,), ())
    if share:
        near, far_cots[0:2], mix_part = after((far_rows[0:2], far_cots[0:2], mix_part))
        acts.append(expert_acts(ids, near, far_cots[0:2], w_gate, w_up, w_down, w_router))
        grad_moe_in, acts = after((grad_moe_in, acts))

    grad_out = cot_low.astype(WIDE)
    grad_hidden = grad_out + rms_back(plain_mid, scale_mid, gain_moe, grad_moe_in)
    gain_moe_sum = jnp.sum(grad_moe_in * plain_mid, axis=0)
    branch_low = grad_hidden.astype(LOW)
    upper = lax.all_gather(branch_low, "shard", axis=0)
    if share:
        rest, branch_low = after((far_rows[2:], branch_low))
        acts.append(expert_acts(ids, rest, far_cots[2:], w_gate, w_up, w_down, w_router))
        upper, acts = after((upper, acts))
    part, gw_in, gw_out, sum_q, sum_k, sum_n = attend_backward(upper, packets, kept, *heads)
    mix_part, upper = after((mix_part, upper))
    mixture = scatter_sum(mix_part)
    output = (hidden + mixture).astype(LOW)

    acts, part = after((acts, part))
    grad_normed = scatter_sum(part)
    grad_input = grad_hidden + rms_back(plain_in, scale_in, gain_attn, grad_normed)

    def replica_sum(values):
        if replicas != 4:
            return lax.psum(values.astype(LOW), "rep")
        me = lax.axis_index("rep")
        pieces = values.astype(LOW).reshape((replicas, -1) + values.shape[1:])

        def piece(place):
            return lax.dynamic_index_in_dim(pieces, place, axis=0, keepdims=False)

        total = piece(me).astype(WIDE)
        for bits in (1, 2, 3):
            total = total + flip_replica(piece(me ^ bits), bits).astype(WIDE)
        low = total.astype(LOW)
        found = jnp.stack([low] + [flip_replica(low, bits) for bits in (1, 2, 3)])
        order = me ^ jnp.arange(replicas, dtype=jnp.int32)
        return jnp.take(found, order, axis=0).reshape(values.shape)

    sum_in, sum_out = (replica_sum(gw_in).astype(WIDE), replica_sum(gw_out).astype(WIDE))
    small = jnp.concatenate(
        [sum_n[0] / gain_attn, sum_q[0], sum_k[0], gain_moe_sum, grad_router.reshape(-1)]
    )
    for axis, size, flip in (("rep", replicas, flip_replica), ("shard", groups, flip_shard)):
        if size & (size - 1):
            small = lax.psum(small, axis)
        else:
            bits = 1
            while bits < size:
                small = small + flip(small, bits)
                bits *= 2
    edges = [0, width, width + head_dim, width + 2 * head_dim, 2 * width + 2 * head_dim]
    grad_gain_attn, grad_gain_query, grad_gain_key, grad_gain_moe = (
        small[a:b] for a, b in zip(edges[:-1], edges[1:])
    )
    grad_router = small[edges[-1] :].reshape(w_router.shape)

    def sets(place):
        return [act[place] for act in acts]

    grad_gate_w = weight_grad(sets(0), sets(3))
    grad_up_w = weight_grad(sets(0), sets(4))
    grad_down = weight_grad(sets(2), sets(1))
    if not share:
        grad_gate_w, grad_up_w, grad_down = (
            lax.psum(values.astype(LOW), "rep").astype(WIDE)
            for values in (grad_gate_w, grad_up_w, grad_down)
        )
    return (
        output, grad_input, grad_gain_attn, grad_gain_query, grad_gain_key,
        sum_in[:, :wide], sum_in[:, wide : 2 * wide], sum_in[:, 2 * wide :], sum_out,
        grad_gain_moe, grad_router, grad_gate_w, grad_up_w, grad_down,
    )


def solution(mesh):
    rows, flat, cols = (P(("rep", "shard"), None), P(), P(None, "shard"))
    lead, experts = (P("shard", None), P("shard", None, None))
    return jax.shard_map(
        local,
        mesh=mesh,
        in_specs=(
            rows, P(("rep", "shard")), rows, flat, flat, flat, cols, cols, cols, lead,
            flat, flat, experts, experts, experts, rows,
        ),
        out_specs=(
            rows, rows, flat, flat, flat, cols, cols, cols, lead,
            flat, flat, experts, experts, experts,
        ),
        check_vma=False,
    )
```

```python
import functools

import jax
import jax.numpy as jnp
from jax import lax
from jax.experimental import pallas as pl
from jax.experimental.pallas import tpu as pltpu
from jax.sharding import PartitionSpec as P

CAP = 144
LINES = 16
EPS_NORM = 1e-06
ROPE_BASE = 50000.0
MASKED = -1e30
VMEM_BYTES = 60 * 1024 * 1024
LOW = jnp.bfloat16
WIDE = jnp.float32
COST = pl.CostEstimate(flops=1 << 20, bytes_accessed=1 << 16, transcendentals=0)


def dot_nn(a, b):
    return lax.dot_general(a, b, (((1,), (0,)), ((), ())), preferred_element_type=WIDE)


def dot_nt(a, b):
    return lax.dot_general(a, b, (((1,), (1,)), ((), ())), preferred_element_type=WIDE)


def dot_tn(a, b):
    return lax.dot_general(a, b, (((0,), (0,)), ((), ())), preferred_element_type=WIDE)


def rope_tables(seq_len, head_dim):
    half_dim = head_dim // 2
    places = jnp.arange(seq_len, dtype=WIDE)
    freqs = ROPE_BASE ** (-jnp.arange(half_dim, dtype=WIDE) * (2.0 / head_dim))
    angles = places[:, None] * freqs[None, :]
    cosine, sine = (jnp.cos(angles), jnp.sin(angles))
    return (
        jnp.concatenate([cosine, cosine], axis=-1),
        jnp.concatenate([-sine, sine], axis=-1),
    )


def head_forward(raw, gain, cos_tab, sin_tab):
    scale = lax.rsqrt(jnp.mean(raw * raw, axis=-1, keepdims=True) + EPS_NORM)
    plain = raw * scale
    scaled = plain * gain
    turned = pltpu.roll(scaled, raw.shape[-1] // 2, axis=1)
    return (scaled * cos_tab + turned * sin_tab, plain, scale)


def head_backward(grad, plain, scale, gain, cos_tab, sin_tab):
    back = grad * cos_tab + pltpu.roll(grad * sin_tab, grad.shape[-1] // 2, axis=1)
    gain_grad = jnp.sum(back * plain, axis=0, keepdims=True)
    back = back * gain
    raw_grad = scale * (back - plain * jnp.mean(back * plain, axis=-1, keepdims=True))
    return (raw_grad, gain_grad)


def soft_weights(query, key, length, score_scale):
    scores = dot_nt(query, key) * score_scale
    places = lax.broadcasted_iota(jnp.int32, scores.shape, 1).astype(WIDE)
    scores = jnp.where(places < length, scores, MASKED)
    expo = jnp.exp(scores - jnp.max(scores, axis=-1, keepdims=True))
    return expo / jnp.sum(expo, axis=-1, keepdims=True)


def attend_block(normed, length, wq, wk, wv, wo, gq, gk, cos_tab, sin_tab, keep):
    head_dim = gq.shape[-1]
    query_raw, key_raw = (dot_nn(normed, wq[...]), dot_nn(normed, wk[...]))
    value = dot_nn(normed, wv[...]).astype(LOW)
    heads = []
    for head in range(query_raw.shape[-1] // head_dim):
        span = slice(head * head_dim, (head + 1) * head_dim)
        query = head_forward(query_raw[:, span], gq, cos_tab, sin_tab)[0].astype(LOW)
        key = head_forward(key_raw[:, span], gk, cos_tab, sin_tab)[0].astype(LOW)
        weights = soft_weights(query, key, length, head_dim**-0.5).astype(LOW)
        heads.append(dot_nn(weights, value[:, span]).astype(LOW))
    joined = heads[0] if len(heads) == 1 else jnp.concatenate(heads, axis=-1)
    keep(query_raw, key_raw, value, joined)
    return dot_nn(joined, wo[...]).astype(LOW)


def attend_kernel(
    pk_ref, wq, wk, wv, wo, gq, gk, cos_ref, sin_ref, part_ref, qr_ref, kr_ref, v_ref, o_ref
):
    rows = pk_ref.shape[1] - LINES
    length = pk_ref[0, rows:, rows : rows + 128].astype(WIDE)[0:1, 0:1]

    def keep(query_raw, key_raw, value, joined):
        qr_ref[0], kr_ref[0], v_ref[0], o_ref[0] = (query_raw, key_raw, value, joined)

    part_ref[0] = attend_block(
        pk_ref[0, :rows], length, wq, wk, wv, wo, gq[...], gk[...], cos_ref[...], sin_ref[...], keep
    )


def whole_spec(array):
    return pl.BlockSpec(array.shape, lambda *_: (0,) * array.ndim, pipeline_mode=pl.Buffered(1))


def first_spec(array):
    return pl.BlockSpec((1,) + array.shape[1:], lambda i: (i,) + (0,) * (array.ndim - 1))


def attend_forward(packets, wq, wk, wv, wo, gq, gk, cos_tab, sin_tab):
    count, lines, width = packets.shape
    rows, wide = (lines - LINES, wq.shape[1])
    fixed = (wq, wk, wv, wo, gq, gk, cos_tab, sin_tab)
    out = (
        jax.ShapeDtypeStruct((count, rows, width), LOW),
        jax.ShapeDtypeStruct((count, rows, wide), WIDE),
        jax.ShapeDtypeStruct((count, rows, wide), WIDE),
        jax.ShapeDtypeStruct((count, rows, wide), LOW),
        jax.ShapeDtypeStruct((count, rows, wide), LOW),
    )
    return pl.pallas_call(
        attend_kernel,
        grid=(count,),
        in_specs=[first_spec(packets)] + [whole_spec(array) for array in fixed],
        out_specs=[first_spec(array) for array in out],
        out_shape=out,
        compiler_params=pltpu.CompilerParams(vmem_limit_bytes=VMEM_BYTES),
        cost_estimate=COST,
        name="attend_forward",
    )(packets, *fixed)


def attend_back_kernel(
    da_ref, pk_ref, qr_ref, kr_ref, v_ref, o_ref,
    wq, wk, wv, wo, gq, gk, cos_ref, sin_ref,
    part_ref, gw_in, gw_out, gain_q, gain_k, gain_n,
):
    rows = pk_ref.shape[1] - LINES
    head_dim = gq.shape[-1]
    length = pk_ref[0, rows:, rows : rows + 128].astype(WIDE)[0:1, 0:1]
    cos_tab, sin_tab = (cos_ref[...], sin_ref[...])
    score_scale = head_dim**-0.5

    @pl.when(pl.program_id(0) == 0)
    def _():
        for ref in (gw_in, gw_out, gain_q, gain_k, gain_n):
            ref[...] = jnp.zeros_like(ref)

    upper = da_ref[0]
    grad_joined = dot_nt(upper, wo[...]).astype(LOW)
    gw_out[...] += dot_tn(o_ref[0], upper)
    grads_q, grads_k, grads_v = ([], [], [])
    for head in range(qr_ref.shape[-1] // head_dim):
        span = slice(head * head_dim, (head + 1) * head_dim)
        query, plain_q, scale_q = head_forward(qr_ref[0, :, span], gq[...], cos_tab, sin_tab)
        key, plain_k, scale_k = head_forward(kr_ref[0, :, span], gk[...], cos_tab, sin_tab)
        query, key, value = (query.astype(LOW), key.astype(LOW), v_ref[0, :, span])
        probs = soft_weights(query, key, length, score_scale)
        grad_out = grad_joined[:, span]
        grads_v.append(dot_tn(probs.astype(LOW), grad_out).astype(LOW))
        grad_probs = dot_nt(grad_out, value)
        inner = jnp.sum(probs * grad_probs, axis=-1, keepdims=True)
        grad_scores = (probs * (grad_probs - inner)).astype(LOW)
        grad_q, head_gain_q = head_backward(
            dot_nn(grad_scores, key) * score_scale, plain_q, scale_q, gq[...], cos_tab, sin_tab
        )
        grad_k, head_gain_k = head_backward(
            dot_tn(grad_scores, query) * score_scale, plain_k, scale_k, gk[...], cos_tab, sin_tab
        )
        gain_q[...] += head_gain_q
        gain_k[...] += head_gain_k
        grads_q.append(grad_q.astype(LOW))
        grads_k.append(grad_k.astype(LOW))
    wide = qr_ref.shape[-1]
    grads = jnp.concatenate(grads_q + grads_k + grads_v, axis=-1)
    part = (
        dot_nt(grads[:, :wide], wq[...])
        + dot_nt(grads[:, wide : 2 * wide], wk[...])
        + dot_nt(grads[:, 2 * wide :], wv[...])
    )
    normed = pk_ref[0, :rows]
    part_ref[0] = part.astype(LOW)
    gain_n[...] += jnp.sum(part * normed.astype(WIDE), axis=0, keepdims=True)
    gw_in[...] += dot_tn(normed, grads)


def attend_backward(upper, packets, kept, wq, wk, wv, wo, gq, gk, cos_tab, sin_tab):
    count, lines, width = packets.shape
    rows, wide = (lines - LINES, wq.shape[1])
    blocks = (upper, packets) + tuple(kept)
    fixed = (wq, wk, wv, wo, gq, gk, cos_tab, sin_tab)
    sums = tuple(
        jax.ShapeDtypeStruct(shape, WIDE)
        for shape in ((width, 3 * wide), wo.shape, gq.shape, gk.shape, (1, width))
    )
    return pl.pallas_call(
        attend_back_kernel,
        grid=(count,),
        in_specs=[first_spec(array) for array in blocks] + [whole_spec(array) for array in fixed],
        out_specs=[first_spec(upper)] + [whole_spec(array) for array in sums],
        out_shape=(jax.ShapeDtypeStruct((count, rows, width), LOW),) + sums,
        compiler_params=pltpu.CompilerParams(vmem_limit_bytes=VMEM_BYTES),
        cost_estimate=COST,
        name="attend_backward",
    )(*blocks, *fixed)


def slot_spots(table, expert):
    row_count = table.shape[1]
    slots = lax.broadcasted_iota(jnp.int32, (CAP, row_count), 0).astype(WIDE) + 1.0
    mine = lax.broadcasted_iota(jnp.int32, table.shape, 0) == expert
    ranks = jnp.sum(jnp.where(mine, table, 0.0), axis=0, keepdims=True)
    return (slots == ranks).astype(LOW)


UNIT = 2


def expert_kernel(row_counts, cot_counts, batch, ex_ref, wg, wu, wd, wr, *refs):
    first, second = (len(row_counts), len(row_counts) + len(cot_counts))
    rows_in, cots_in = (refs[:first], refs[first:second])
    x_ref, y_ref, m_ref, dg_ref, du_ref, dgate_ref, rows_buf, cots_buf, sems = refs[second:]
    steps, units = (sum(row_counts) // batch, batch // UNIT)
    turn = pl.program_id(0) * steps + pl.program_id(1)
    slot = lax.rem(turn, 2)
    row_count = rows_buf.shape[2]

    def copy(kind, source, offset, place, part):
        buffer = (rows_buf, cots_buf)[kind]
        return pltpu.make_async_copy(
            source.at[pl.ds(offset, UNIT)],
            buffer.at[place, pl.ds(part * UNIT, UNIT)],
            sems.at[kind, place, part],
        )

    def fetch(step, place):
        for part in range(units):
            unit = step * units + part
            for kind, sources, counts in ((0, rows_in, row_counts), (1, cots_in, cot_counts)):
                begin = 0
                for source, count in zip(sources, counts):
                    size = count // UNIT

                    @pl.when((unit >= begin) & (unit < begin + size))
                    def _(source=source, begin=begin):
                        copy(kind, source, (unit - begin) * UNIT, place, part).start()

                    begin += size

    @pl.when(turn == 0)
    def _():
        fetch(turn, slot)

    @pl.when(turn + 1 < pl.num_programs(0) * steps)
    def _():
        fetch(lax.rem(turn + 1, steps), 1 - slot)

    for part in range(units):
        copy(0, rows_in[0], 0, slot, part).wait()
        copy(1, cots_in[0], 0, slot, part).wait()
    hidden = wg.shape[-1]
    expert = ex_ref[pl.program_id(0)]
    for seq in range(batch):
        table = cots_buf[slot, seq, row_count:, :row_count].astype(WIDE)
        spots = slot_spots(table, expert)
        span = pl.ds(seq * CAP, CAP)
        x_ref[0, span] = dot_nn(spots, rows_buf[slot, seq]).astype(LOW)
        y_ref[0, span] = dot_nn(spots, cots_buf[slot, seq, :row_count]).astype(LOW)
    x_all, y_all = (x_ref[0], y_ref[0])
    logits = dot_nn(x_all, wr[...])
    expo = jnp.exp(logits - jnp.max(logits, axis=-1, keepdims=True))
    chosen = lax.broadcasted_iota(jnp.int32, expo.shape, 1) == expert
    gates = jnp.sum(jnp.where(chosen, expo, 0.0), axis=-1, keepdims=True) / jnp.sum(
        expo, axis=-1, keepdims=True
    )
    step = min(256, hidden)
    dgate = jnp.zeros((x_all.shape[0], 1), WIDE)
    for start in range(0, hidden, step):
        span = slice(start, start + step)
        gate_act, up_act = (dot_nn(x_all, wg[0, :, span]), dot_nn(x_all, wu[0, :, span]))
        plain_grad = dot_nt(y_all, wd[0, span, :])
        sig = jax.nn.sigmoid(gate_act)
        silu = gate_act * sig
        joined = silu * up_act
        dgate += jnp.sum(joined * plain_grad, axis=-1, keepdims=True)
        grad = plain_grad * gates
        m_ref[0, :, span] = (joined * gates).astype(LOW)
        dg_ref[0, :, span] = (grad * up_act * (sig + silu * (1.0 - sig))).astype(LOW)
        du_ref[0, :, span] = (grad * silu).astype(LOW)
    dgate_ref[0] = jnp.broadcast_to(dgate, dgate_ref.shape[1:])


def expert_acts(ids, rows, cots, wg, wu, wd, wr, batch=4):
    row_count, width = rows[0].shape[1:]
    row_counts, cot_counts = ([array.shape[0] for array in arrays] for arrays in (rows, cots))
    count = sum(row_counts)
    own, _, hidden = wg.shape
    out_rows = batch * CAP

    def acts(cols, kind=LOW):
        return jax.ShapeDtypeStruct((own, count * CAP, cols), kind)

    def act_spec(cols):
        return pl.BlockSpec((1, out_rows, cols), lambda e, i: (e, i, 0))

    def weight_spec(array):
        return pl.BlockSpec(
            (1,) + array.shape[1:], lambda e, i: (e, 0, 0), pipeline_mode=pl.Buffered(1)
        )

    any_spec = pl.BlockSpec(memory_space=pl.ANY)
    columns = (width, width, hidden, hidden, hidden, 128)
    return pl.pallas_call(
        functools.partial(expert_kernel, row_counts, cot_counts, batch),
        grid=(own, count // batch),
        in_specs=[
            pl.BlockSpec(memory_space=pltpu.SMEM),
            weight_spec(wg),
            weight_spec(wu),
            weight_spec(wd),
            pl.BlockSpec(wr.shape, lambda e, i: (0, 0)),
        ]
        + [any_spec] * (len(rows) + len(cots)),
        out_specs=[act_spec(cols) for cols in columns],
        out_shape=tuple(acts(cols) for cols in columns[:5]) + (acts(128, WIDE),),
        scratch_shapes=[
            pltpu.VMEM((2, batch) + rows[0].shape[1:], LOW),
            pltpu.VMEM((2, batch) + cots[0].shape[1:], LOW),
            pltpu.SemaphoreType.DMA((2, 2, batch // UNIT)),
        ],
        compiler_params=pltpu.CompilerParams(vmem_limit_bytes=VMEM_BYTES),
        cost_estimate=COST,
        name="expert_acts",
    )(ids, wg, wu, wd, wr, *rows, *cots)


def pull_kernel(ex_ref, rows_ref, cot_ref, dg_ref, du_ref, dgate_ref, wg, wu, wr, part_ref, router):
    batch, row_count, _ = rows_ref.shape
    own = wg.shape[0]

    @pl.when(pl.program_id(0) == 0)
    def _():
        router[...] = jnp.zeros_like(router)

    backs = [
        (dot_nt(dg_ref[e], wg[e]) + dot_nt(du_ref[e], wu[e])).astype(LOW) for e in range(own)
    ]
    for seq in range(batch):
        table = cot_ref[seq, :, :row_count].astype(WIDE)
        logits = dot_nn(rows_ref[seq], wr[...])
        expo = jnp.exp(logits - jnp.max(logits, axis=-1, keepdims=True))
        probs = expo / jnp.sum(expo, axis=-1, keepdims=True)
        columns = lax.broadcasted_iota(jnp.int32, probs.shape, 1)
        grad_logits = jnp.zeros_like(probs)
        span = slice(seq * CAP, (seq + 1) * CAP)
        total = jnp.zeros(part_ref.shape[1:], WIDE)
        for e in range(own):
            spots = slot_spots(table, ex_ref[e])
            total += dot_tn(spots, backs[e][span])
            dgate = dgate_ref[e, span]
            high = dgate.astype(LOW)
            rest = (dgate - high.astype(WIDE)).astype(LOW)
            at_rows = (dot_tn(spots, high) + dot_tn(spots, rest))[:, : probs.shape[1]]
            chosen = (columns == ex_ref[e]).astype(WIDE)
            prob = jnp.sum(probs * chosen, axis=-1, keepdims=True)
            grad_logits += at_rows * prob * (chosen - probs)
        low_logits = grad_logits.astype(LOW)
        part_ref[seq] = (total + dot_nt(low_logits, wr[...])).astype(LOW)
        router[...] += dot_tn(rows_ref[seq], low_logits)


def mix_kernel(ex_ref, cot_ref, m_ref, wd, part_ref):
    batch, row_count, _ = part_ref.shape
    own = wd.shape[0]
    outs = [dot_nn(m_ref[e], wd[e]).astype(LOW) for e in range(own)]
    for seq in range(batch):
        table = cot_ref[seq, :, :row_count].astype(WIDE)
        span = slice(seq * CAP, (seq + 1) * CAP)
        total = sum(dot_tn(slot_spots(table, ex_ref[e]), outs[e][span]) for e in range(own))
        part_ref[seq] = total.astype(LOW)


def spread_call(kernel, name, ids, by_seq, cots, by_slot, fixed, router_shape, batch=2):
    count, lines, width = cots.shape
    row_count = lines - LINES
    part = jax.ShapeDtypeStruct((count, row_count, width), LOW)

    def seq_spec(array):
        return pl.BlockSpec((batch,) + array.shape[1:], lambda i: (i, 0, 0))

    def slot_spec(array):
        return pl.BlockSpec((array.shape[0], batch * CAP, array.shape[2]), lambda i: (0, i, 0))

    return pl.pallas_call(
        kernel,
        grid=(count // batch,),
        in_specs=[pl.BlockSpec(memory_space=pltpu.SMEM)]
        + [seq_spec(array) for array in by_seq]
        + [pl.BlockSpec((batch, LINES, width), lambda i: (i, row_count // LINES, 0))]
        + [slot_spec(array) for array in by_slot]
        + [whole_spec(array) for array in fixed],
        out_specs=[seq_spec(part)] + [whole_spec(shape) for shape in router_shape],
        out_shape=[part] + list(router_shape),
        compiler_params=pltpu.CompilerParams(vmem_limit_bytes=VMEM_BYTES),
        cost_estimate=COST,
        name=name,
    )(ids, *by_seq, cots, *by_slot, *fixed)


def weight_grad(lefts, rights):
    own, _, left_cols = lefts[0].shape
    right_cols = rights[0].shape[-1]
    sets = len(lefts)
    left_tile, right_tile = (min(512, left_cols), min(1024, right_cols))

    def kernel(*refs):
        refs[2 * sets][0] = sum(dot_tn(refs[i][0], refs[sets + i][0]) for i in range(sets))

    return pl.pallas_call(
        kernel,
        grid=(own, right_cols // right_tile, left_cols // left_tile),
        in_specs=[
            pl.BlockSpec((1, array.shape[1], left_tile), lambda e, r, l: (e, 0, l))
            for array in lefts
        ]
        + [
            pl.BlockSpec((1, array.shape[1], right_tile), lambda e, r, l: (e, 0, r))
            for array in rights
        ],
        out_specs=pl.BlockSpec((1, left_tile, right_tile), lambda e, r, l: (e, l, r)),
        out_shape=jax.ShapeDtypeStruct((own, left_cols, right_cols), WIDE),
        compiler_params=pltpu.CompilerParams(vmem_limit_bytes=VMEM_BYTES),
        cost_estimate=COST,
        name="weight_grad",
    )(*lefts, *rights)


CHUNKS = 4
NEAR_LINES = 128


def front_kernel(
    replicas, groups,
    packet, cot, tokens, wq, wk, wv, wo, gq, gk, cos_ref, sin_ref, gain_ref,
    packets, qr_ref, kr_ref, v_ref, o_ref, hidden, rows_all, cots, fx, fy, fd, px, py, pd,
    nb, mine, pair_out, pair_in, line_r, line_l, low,
    n1_send, n1_recv, n1_pair, n2_send, n2_recv, n2_pair, cz_send, cz_recv, cz_pair,
    xy_send, xy_recv, dg_send, dg_recv, fl_send, fl_recv,
    po_send, po_recv, lr_send, lr_recv, ll_send, ll_recv, keep_sem, own_sem,
):
    rail = groups // 2
    rep, shard = (lax.axis_index("rep"), lax.axis_index("shard"))
    place, core = (shard // 2, shard % 2)
    rows = tokens.shape[0]
    step_rows = rows // CHUNKS
    last = rail - 1
    right, left, partner = ((rep, shard + 2), (rep, shard - 2), (rep, shard + 1 - 2 * core))
    over_x = (rep + 1 - 2 * (rep % 2), shard)
    over_y = ((rep + 2) % replicas, shard)

    def remote(source, target, send, recv, device):
        return pltpu.make_async_remote_copy(
            source, target, send, recv, device_id=device, device_id_type=pl.DeviceIdType.MESH
        )

    def each(size, body):
        def step(i, carry):
            body(i)
            return carry

        lax.fori_loop(0, size, step, 0)

    class Flood:
        def __init__(self, view, send, recv, pair, own):
            self.view, self.send, self.recv, self.pair, self.own = (view, send, recv, pair, own)

        def copy(self, way, q, own=False):
            slot = 2 * q + core
            source = self.own if own else self.view.at[slot]
            recv = self.pair.at[q] if way == 2 else self.recv.at[q]
            device = (right, left, partner)[way]
            return remote(source, self.view.at[slot], self.send.at[way, q], recv, device)

        def start_line(self):
            @pl.when(place < last)
            def _():
                self.copy(0, place, True).start()

            @pl.when(place > 0)
            def _():
                self.copy(1, place, True).start()

        def start_pair(self):
            self.copy(2, place, True).start()

        def onward(self, d, more=None):
            @pl.when((d > 0) & (place - d >= 0))
            def _():
                q = place - d
                self.copy(0, q).wait_recv()

                @pl.when(place < last)
                def _():
                    self.copy(0, q).start()

                self.copy(2, q).start()
                if more is not None:
                    more(q)

            @pl.when((d > 0) & (place + d <= last))
            def _():
                q = place + d
                self.copy(1, q).wait_recv()

                @pl.when(place > 0)
                def _():
                    self.copy(1, q).start()

                self.copy(2, q).start()
                if more is not None:
                    more(q)

        def wait_pair(self, q):
            slot = 2 * q + 1 - core
            remote(
                self.view.at[slot], self.view.at[slot], self.send.at[2, q], self.pair.at[q], partner
            ).wait_recv()

        def finish(self, pairs):
            def body(q):
                @pl.when((place < last) & (q <= place))
                def _():
                    self.copy(0, q).wait_send()

                @pl.when((place > 0) & (q >= place))
                def _():
                    self.copy(1, q).wait_send()

                self.copy(2, q).wait_send()
                if pairs:
                    self.wait_pair(q)

            each(rail, body)

    flood_n1 = Flood(nb, n1_send, n1_recv, n1_pair, packet)
    flood_n2 = Flood(rows_all, n2_send, n2_recv, n2_pair, low)
    flood_cot = Flood(cots, cz_send, cz_recv, cz_pair, cot)

    def cross(way, q, own=False):
        source = cot if own else cots.at[2 * q + core]
        target, device = ((fx, over_x), (fy, over_y))[way]
        return remote(source, target.at[q], xy_send.at[way, q], xy_recv.at[way, q], device)

    def cross_both(q):
        cross(0, q).start()
        cross(1, q).start()

    def diagonal(way, q):
        source, device = ((fx, over_y), (fy, over_x))[way]
        span = (pl.ds(0, NEAR_LINES), pl.ds(NEAR_LINES, cot.shape[0] - NEAR_LINES))[way]
        return remote(
            source.at[q, span], fd.at[q, span], dg_send.at[way, q], dg_recv.at[way, q], device
        )

    def flip(which, q):
        source, target = ((fx, px), (fy, py), (fd, pd))[which]
        return remote(
            source.at[q], target.at[q], fl_send.at[which, q], fl_recv.at[which, q], partner
        )

    def at_distance(d, body):
        if d < 0 or d > last:
            return
        if d == 0:
            body(place)
            return

        @pl.when(place - d >= 0)
        def _():
            body(place - d)

        @pl.when(place + d <= last)
        def _():
            body(place + d)

    def take_cross(q):
        for way in (0, 1):
            cross(way, q).wait_recv()
            diagonal(way, q).start()
            flip(way, q).start()

    def take_diagonal(q):
        for way in (0, 1):
            diagonal(way, q).wait_recv()
        flip(2, q).start()

    def event(d):
        if 1 <= d <= last:
            flood_cot.onward(d, cross_both)
        at_distance(d - 1, take_cross)
        at_distance(d - 2, take_diagonal)

    barrier = pltpu.get_barrier_semaphore()

    def greet(device):
        pl.semaphore_signal(
            barrier, inc=1, device_id=device, device_id_type=pl.DeviceIdType.MESH
        )

    for device in (partner, over_x, over_y):
        greet(device)

    @pl.when(place < last)
    def _():
        greet(right)

    @pl.when(place > 0)
    def _():
        greet(left)

    inner = (place > 0) & (place < last)

    @pl.when(inner)
    def _():
        pl.semaphore_wait(barrier, 5)

    @pl.when(jnp.logical_not(inner))
    def _():
        pl.semaphore_wait(barrier, 4)

    flood_n1.start_line()
    flood_n1.start_pair()
    own_block = pltpu.make_async_copy(packet, nb.at[shard], own_sem.at[0])
    own_block.start()
    own_cot = pltpu.make_async_copy(cot, cots.at[shard], own_sem.at[1])
    own_cot.start()
    cross(0, place, True).start()
    cross(1, place, True).start()
    flood_cot.start_pair()
    own_block.wait()

    def partial_out(q):
        return remote(
            pair_out.at[q], pair_in.at[q], po_send.at[q], po_recv.at[q], partner
        )

    def line(q, chunk, to_right):
        span = pl.ds(pl.multiple_of(chunk * step_rows, step_rows), step_rows)
        target, send, recv, device = (
            (line_r, lr_send, lr_recv, right) if to_right else (line_l, ll_send, ll_recv, left)
        )
        return remote(
            mine.at[q, span], target.at[q, span], send.at[q, chunk], recv.at[q, chunk], device
        )

    def add_up(q, chunk, extras):
        span = pl.ds(pl.multiple_of(chunk * step_rows, step_rows), step_rows)
        total = mine[q, span].astype(WIDE) + pair_in[q, span].astype(WIDE)
        for extra in extras:
            total = total + extra[q, span].astype(WIDE)
        return total

    def forward_line(q, to_right, first):
        partial_out(q).wait_recv()

        def body(chunk):
            extras = []
            if not first:
                line(q, chunk, to_right).wait_recv()
                extras = [line_r if to_right else line_l]
            span = pl.ds(pl.multiple_of(chunk * step_rows, step_rows), step_rows)
            mine[q, span] = add_up(q, chunk, extras).astype(LOW)
            line(q, chunk, to_right).start()

        each(CHUNKS, body)

    def keep_copy(slot):
        return pltpu.make_async_copy(nb.at[slot], packets.at[slot], keep_sem.at[slot])

    def one_distance(d):
        flood_n1.onward(d)

        def one_block(k):
            side, other = (k % 2, k // 2)
            q = place + (2 * side - 1) * d

            @pl.when((q >= 0) & (q <= last) & ((d > 0) | (side == 0)))
            def _():
                @pl.when(other == 1)
                def _():
                    flood_n1.wait_pair(q)

                slot = 2 * q + core + other * (1 - 2 * core)
                keep_copy(slot).start()
                length = nb[slot, rows:, rows : rows + 128].astype(WIDE)[0:1, 0:1]

                def keep(query_raw, key_raw, value, joined):
                    qr_ref[slot], kr_ref[slot] = (query_raw, key_raw)
                    v_ref[slot], o_ref[slot] = (value, joined)

                part = attend_block(
                    nb[slot, :rows], length, wq, wk, wv, wo, gq[...], gk[...],
                    cos_ref[...], sin_ref[...], keep,
                )

                @pl.when(other == 0)
                def _():
                    mine[q] = part

                @pl.when(other == 1)
                def _():
                    pair_out[q] = part
                    partial_out(q).start()

        each(4, one_block)

        @pl.when((place == 0) & (d > 0))
        def _():
            forward_line(d, True, True)

        @pl.when((place == last) & (d > 0))
        def _():
            forward_line(last - d, False, True)

    each(rail, one_distance)
    flood_cot.start_line()

    def rest_right():
        def body(j):
            @pl.when((place > 0) & (place + j <= last))
            def _():
                forward_line(place + j, True, False)

        each(last, lambda i: body(i + 1))

    def rest_left():
        def body(j):
            @pl.when((place < last) & (place - j >= 0))
            def _():
                forward_line(place - j, False, False)

        each(last, lambda i: body(i + 1))

    near_end = place < rail // 2
    pl.when(near_end)(rest_right)
    pl.when(jnp.logical_not(near_end))(rest_left)
    event(1)
    pl.when(near_end)(rest_left)
    pl.when(jnp.logical_not(near_end))(rest_right)

    partial_out(place).wait_recv()

    def finish_rows(chunk):
        @pl.when(place > 0)
        def _():
            line(place, chunk, True).wait_recv()

        @pl.when(place < last)
        def _():
            line(place, chunk, False).wait_recv()

        span = pl.ds(pl.multiple_of(chunk * step_rows, step_rows), step_rows)
        total = tokens[span].astype(WIDE) + add_up(place, chunk, [])
        from_left = jnp.where(place > 0, line_r[place, span].astype(WIDE), 0.0)
        from_right = jnp.where(place < last, line_l[place, span].astype(WIDE), 0.0)
        total = total + from_left + from_right
        hidden[span] = total
        scale = lax.rsqrt(jnp.mean(total * total, axis=-1, keepdims=True) + EPS_NORM)
        low[span] = (total * scale * gain_ref[...]).astype(LOW)

    each(CHUNKS, finish_rows)
    flood_n2.start_line()
    flood_n2.start_pair()
    own_low = pltpu.make_async_copy(low, rows_all.at[shard], own_sem.at[2])
    own_low.start()

    event(2)
    for d in range(1, rail):
        flood_n2.onward(d)
        event(d + 2)

    flood_n1.finish(False)
    flood_n2.finish(True)
    flood_cot.finish(True)
    own_cot.wait()
    own_low.wait()

    def settle(q):
        keep_copy(2 * q).wait()
        keep_copy(2 * q + 1).wait()
        partial_out(q).wait_send()
        for way in (0, 1):
            cross(way, q).wait_send()
            diagonal(way, q).wait_send()
        for which in (0, 1, 2):
            flip(which, q).wait_send()
            flip(which, q).wait_recv()

        def chunk_sends(chunk):
            @pl.when((place < last) & (q > place))
            def _():
                line(q, chunk, True).wait_send()

            @pl.when((place > 0) & (q < place))
            def _():
                line(q, chunk, False).wait_send()

        each(CHUNKS, chunk_sends)

    each(rail, settle)


def front(replicas, groups, packet, cot, tokens, wq, wk, wv, wo, gq, gk, cos_tab, sin_tab, gain):
    lines, width = packet.shape
    rows, wide, rail = (tokens.shape[0], wq.shape[1], groups // 2)
    any_spec, fast = (pl.BlockSpec(memory_space=pl.ANY), pl.BlockSpec(memory_space=pltpu.VMEM))

    def shape(*dims, kind=LOW):
        return jax.ShapeDtypeStruct(dims, kind)

    far = [shape(rail, lines, width)] * 6
    block = pltpu.VMEM((rail, rows, width), LOW)
    dma = pltpu.SemaphoreType.DMA
    return pl.pallas_call(
        functools.partial(front_kernel, replicas, groups),
        in_specs=[any_spec] * 2 + [fast] * 10,
        out_specs=[any_spec] + [fast] * 5 + [any_spec] * 8,
        out_shape=[
            shape(groups, lines, width),
            shape(groups, rows, wide, kind=WIDE),
            shape(groups, rows, wide, kind=WIDE),
            shape(groups, rows, wide),
            shape(groups, rows, wide),
            shape(rows, width, kind=WIDE),
            shape(groups, rows, width),
            shape(groups, lines, width),
        ]
        + far,
        scratch_shapes=[
            pltpu.VMEM((groups, lines, width), LOW),
            block, block, block, block, block,
            pltpu.VMEM((rows, width), LOW),
        ]
        + [dma((3, rail)), dma((rail,)), dma((rail,))] * 3
        + [dma((2, rail))] * 4
        + [dma((3, rail))] * 2
        + [dma((rail,))] * 2
        + [dma((rail, CHUNKS))] * 4
        + [dma((groups,)), dma((3,))],
        compiler_params=pltpu.CompilerParams(
            vmem_limit_bytes=VMEM_BYTES, collective_id=0, has_side_effects=True
        ),
        cost_estimate=COST,
        name="front",
    )(packet, cot, tokens, wq, wk, wv, wo, gq, gk, cos_tab, sin_tab, gain)


def rms_parts(values):
    scale = lax.rsqrt(jnp.mean(values * values, axis=-1, keepdims=True) + EPS_NORM)
    return (values * scale, scale)


def rms_back(plain, scale, gain, grad):
    back = grad * gain
    return scale * (back - plain * jnp.mean(back * plain, axis=-1, keepdims=True))


def local(
    tokens, lengths, routes, gain_attn, gain_query, gain_key,
    w_query, w_key, w_value, w_out, gain_moe, w_router,
    w_gate, w_up, w_down, out_grad,
):
    row_count, width = tokens.shape
    head_dim = gain_query.shape[0]
    groups, replicas = (lax.axis_size("shard"), lax.axis_size("rep"))
    expert_count, own = (w_router.shape[1], w_gate.shape[0])
    wide = w_query.shape[1]
    after = lax.optimization_barrier
    gain_q, gain_k = (gain_query.reshape(1, -1), gain_key.reshape(1, -1))
    cos_tab, sin_tab = rope_tables(row_count, head_dim)
    ids = lax.axis_index("shard") * own + jnp.arange(own, dtype=jnp.int32)

    def flip_replica(values, bits):
        return lax.ppermute(values, "rep", [(i, i ^ bits) for i in range(replicas)])

    def flip_shard(values, bits):
        return lax.ppermute(values, "shard", [(i, i ^ bits) for i in range(groups)])

    def scatter_sum(parts):
        return lax.psum_scatter(
            parts.reshape(-1, width), "shard", scatter_dimension=0, tiled=True
        ).astype(WIDE)

    inputs = tokens.astype(WIDE)
    row_mask = (jnp.arange(row_count, dtype=jnp.int32) < lengths[0])[:, None]
    named = jnp.any(
        routes[None, :, :] == jnp.arange(expert_count, dtype=jnp.int32)[:, None, None], axis=-1
    )
    upto = (jnp.arange(row_count)[:, None] <= jnp.arange(row_count)[None, :]).astype(LOW)
    ranks = jnp.where(named, dot_nn(named.astype(LOW), upto), 0.0).astype(LOW)
    lines = jnp.concatenate(
        [ranks, jnp.broadcast_to(lengths[0].astype(LOW), (expert_count, width - row_count))], axis=1
    )
    plain_in, scale_in = rms_parts(inputs)
    packet = jnp.concatenate([(plain_in * gain_attn).astype(LOW), lines], axis=0)
    cot_low = jnp.where(row_mask, out_grad, 0.0)
    cot_packet = jnp.concatenate([cot_low, lines], axis=0)
    heads = (w_query, w_key, w_value, w_out, gain_q, gain_k, cos_tab, sin_tab)
    share = replicas == 4 and groups == 8
    if share:
        packets, *kept = front(
            replicas, groups, packet, cot_packet, tokens, *heads, gain_moe.reshape(1, -1)
        )
        kept, (hidden, rows_all, cots), far_cots = (kept[:4], kept[4:7], kept[7:])
        plain_mid, scale_mid = rms_parts(hidden)
        pairs = rows_all.reshape((groups // 2, 2) + rows_all.shape[1:])
        core = lax.axis_index("shard") % 2
        near = [
            lax.dynamic_index_in_dim(part, core, 1, keepdims=False) for part in (pairs[:2], pairs[2:])
        ]
        rows_all, near = after((rows_all, near))
    else:
        packets = lax.all_gather(packet, "shard", axis=0)
        cot_packet, packets = after((cot_packet, packets))
        cots = lax.all_gather(cot_packet, "shard", axis=0)
        part, *kept = attend_forward(packets, *heads)
        hidden = inputs + scatter_sum(part)
        plain_mid, scale_mid = rms_parts(hidden)
        rows_all = lax.all_gather((plain_mid * gain_moe).astype(LOW), "shard", axis=0)

    acts = [expert_acts(ids, [rows_all], [cots], w_gate, w_up, w_down, w_router)]
    if share:
        over = [flip_replica(near[0], bits) for bits in (1, 2)]
        acts, over = after((acts, over))
        over_x, over_y = ([over[0]], [over[1]])
    _, _, gated, grad_gate_act, grad_up_act, dgates = acts[0]
    router_shape = (jax.ShapeDtypeStruct(w_router.shape, WIDE),)
    pull_part, grad_router = spread_call(
        pull_kernel, "expert_pull", ids, (rows_all,), cots,
        (grad_gate_act, grad_up_act, dgates), (w_gate, w_up, w_router), router_shape,
    )
    if share:
        over = [flip_replica(near[1], bits) for bits in (1, 2)]
        pull_part, over = after((pull_part, over))
        over_x, over_y = (over_x + [over[0]], over_y + [over[1]])
    grad_moe_in = scatter_sum(pull_part)
    gated, pull_part = after((gated, pull_part))
    if share:
        diagonal = [flip_replica(over_x[0], 2), flip_replica(over_y[1], 1)]
        flipped = [flip_shard(values, 1) for values in over_x + over_y]
        near, pull_part = after((over_x + over_y, pull_part))
        acts.append(expert_acts(ids, near, far_cots[0:2], w_gate, w_up, w_down, w_router))
        acts, diagonal, flipped = after((acts, diagonal, flipped))
        gated, acts = after((gated, acts))
        diagonal_flipped = [flip_shard(values, 1) for values in diagonal]
    (mix_part,) = spread_call(mix_kernel, "expert_mix", ids, (), cots, (gated,), (w_down,), ())
    if share:
        mix_part, diagonal_flipped = after((mix_part, diagonal_flipped))
        grad_moe_in, mix_part = after((grad_moe_in, mix_part))

    grad_out = cot_low.astype(WIDE)
    grad_hidden = grad_out + rms_back(plain_mid, scale_mid, gain_moe, grad_moe_in)
    gain_moe_sum = jnp.sum(grad_moe_in * plain_mid, axis=0)
    branch_low = grad_hidden.astype(LOW)
    upper = lax.all_gather(branch_low, "shard", axis=0)
    if share:
        rest, branch_low = after((diagonal + flipped + diagonal_flipped, branch_low))
        rest_cots = [far_cots[2], far_cots[3], far_cots[4], far_cots[5]]
        acts.append(expert_acts(ids, rest, rest_cots, w_gate, w_up, w_down, w_router))
        upper, acts = after((upper, acts))
    mix_part, upper = after((mix_part, upper))
    mixture = scatter_sum(mix_part)
    part, gw_in, gw_out, sum_q, sum_k, sum_n = attend_backward(upper, packets, kept, *heads)

    def sets(place):
        return [act[place] for act in acts]

    def exchange(values, axis, count):
        flip = flip_replica if axis == "rep" else flip_shard
        return [values] + [flip(values, bits) for bits in range(1, count)]

    def in_order(found, axis):
        order = lax.axis_index(axis) ^ jnp.arange(len(found), dtype=jnp.int32)
        return jnp.take(jnp.stack(found), order, axis=0)

    small = jnp.concatenate(
        [sum_n[0] / gain_attn, sum_q[0], sum_k[0], gain_moe_sum, grad_router.reshape(-1)]
    )
    if share:
        me = lax.axis_index("rep")

        def quarters(values):
            return values.astype(LOW).reshape((replicas, -1) + values.shape[1:])

        def traded(values):
            pieces = quarters(values)
            found = [
                lax.dynamic_index_in_dim(pieces, me ^ bits, axis=0, keepdims=False)
                for bits in range(replicas)
            ]
            return found[:1] + [flip_replica(found[bits], bits) for bits in range(1, replicas)]

        trades = [traded(gw_in), traded(gw_out), exchange(small, "rep", replicas)]
        acts, gw_in = after((acts, gw_in))
        grad_gate_w = weight_grad(sets(0), sets(3))
        grad_gate_w, trades, part, mixture = after((grad_gate_w, trades, part, mixture))
        grad_normed = scatter_sum(part)
        lows = [sum(piece.astype(WIDE) for piece in trade).astype(LOW) for trade in trades[:2]]
        small = jnp.sum(in_order(trades[2], "rep"), axis=0)
        acts, lows, small = after((acts, lows, small))
        shared = [exchange(low, "rep", replicas) for low in lows] + [exchange(small, "shard", groups)]
        grad_up_w = weight_grad(sets(0), sets(4))
        grad_up_w, shared, acts = after((grad_up_w, shared, acts))
        sum_in, sum_out = (
            in_order(pieces, "rep").reshape(values.shape).astype(WIDE)
            for pieces, values in zip(shared[:2], (gw_in, gw_out))
        )
        small = jnp.sum(in_order(shared[2], "shard"), axis=0)
        grad_down = weight_grad(sets(2), sets(1))
    else:
        grad_normed = scatter_sum(part)
        over_reps = lax.psum(
            (gw_in.astype(LOW), gw_out.astype(LOW))
            + tuple(
                weight_grad(sets(left), sets(right)).astype(LOW)
                for left, right in ((0, 3), (0, 4), (2, 1))
            ),
            "rep",
        )
        sum_in, sum_out, grad_gate_w, grad_up_w, grad_down = (
            values.astype(WIDE) for values in over_reps
        )
        small = lax.psum(small, ("rep", "shard"))
    output = (hidden + mixture).astype(LOW)
    grad_input = grad_hidden + rms_back(plain_in, scale_in, gain_attn, grad_normed)
    edges = [0, width, width + head_dim, width + 2 * head_dim, 2 * width + 2 * head_dim]
    grad_gain_attn, grad_gain_query, grad_gain_key, grad_gain_moe = (
        small[a:b] for a, b in zip(edges[:-1], edges[1:])
    )
    grad_router = small[edges[-1] :].reshape(w_router.shape)

    return (
        output, grad_input, grad_gain_attn, grad_gain_query, grad_gain_key,
        sum_in[:, :wide], sum_in[:, wide : 2 * wide], sum_in[:, 2 * wide :], sum_out,
        grad_gain_moe, grad_router, grad_gate_w, grad_up_w, grad_down,
    )


def solution(mesh):
    rows, flat, cols = (P(("rep", "shard"), None), P(), P(None, "shard"))
    lead, experts = (P("shard", None), P("shard", None, None))
    return jax.shard_map(
        local,
        mesh=mesh,
        in_specs=(
            rows, P(("rep", "shard")), rows, flat, flat, flat, cols, cols, cols, lead,
            flat, flat, experts, experts, experts, rows,
        ),
        out_specs=(
            rows, rows, flat, flat, flat, cols, cols, cols, lead,
            flat, flat, experts, experts, experts,
        ),
        check_vma=False,
    )
```

```python
import functools
import math

import jax
import jax.numpy as jnp
from jax import lax
from jax.experimental import pallas as pl
from jax.experimental.pallas import tpu as pltpu
from jax.sharding import PartitionSpec as P

CAP = 144
LINES = 16
EPS_NORM = 1e-06
ROPE_BASE = 50000.0
MASKED = -1e30
VMEM_BYTES = 60 * 1024 * 1024
LOW = jnp.bfloat16
WIDE = jnp.float32
COST = pl.CostEstimate(flops=1 << 20, bytes_accessed=1 << 16, transcendentals=0)


def dot_nn(a, b):
    return lax.dot_general(a, b, (((1,), (0,)), ((), ())), preferred_element_type=WIDE)


def dot_nt(a, b):
    return lax.dot_general(a, b, (((1,), (1,)), ((), ())), preferred_element_type=WIDE)


def dot_tn(a, b):
    return lax.dot_general(a, b, (((0,), (0,)), ((), ())), preferred_element_type=WIDE)


def rope_tables(seq_len, head_dim):
    half_dim = head_dim // 2
    places = jnp.arange(seq_len, dtype=WIDE)
    freqs = ROPE_BASE ** (-jnp.arange(half_dim, dtype=WIDE) * (2.0 / head_dim))
    angles = places[:, None] * freqs[None, :]
    cosine, sine = (jnp.cos(angles), jnp.sin(angles))
    return (
        jnp.concatenate([cosine, cosine], axis=-1),
        jnp.concatenate([-sine, sine], axis=-1),
    )


def head_forward(raw, gain, cos_tab, sin_tab):
    scale = lax.rsqrt(jnp.mean(raw * raw, axis=-1, keepdims=True) + EPS_NORM)
    plain = raw * scale
    scaled = plain * gain
    turned = pltpu.roll(scaled, raw.shape[-1] // 2, axis=1)
    return (scaled * cos_tab + turned * sin_tab, plain, scale)


def head_backward(grad, plain, scale, gain, cos_tab, sin_tab):
    back = grad * cos_tab + pltpu.roll(grad * sin_tab, grad.shape[-1] // 2, axis=1)
    gain_grad = jnp.sum(back * plain, axis=0, keepdims=True)
    back = back * gain
    raw_grad = scale * (back - plain * jnp.mean(back * plain, axis=-1, keepdims=True))
    return (raw_grad, gain_grad)


def soft_weights(query, key, length, score_scale):
    scores = dot_nt(query, key) * score_scale
    places = lax.broadcasted_iota(jnp.int32, scores.shape, 1).astype(WIDE)
    scores = jnp.where(places < length, scores, MASKED)
    expo = jnp.exp(scores - jnp.max(scores, axis=-1, keepdims=True))
    return expo / jnp.sum(expo, axis=-1, keepdims=True)


def attend_block(normed, length, wq, wk, wv, wo, gq, gk, cos_tab, sin_tab, keep):
    head_dim = gq.shape[-1]
    query_raw, key_raw = (dot_nn(normed, wq[...]), dot_nn(normed, wk[...]))
    value = dot_nn(normed, wv[...]).astype(LOW)
    heads = []
    for head in range(query_raw.shape[-1] // head_dim):
        span = slice(head * head_dim, (head + 1) * head_dim)
        query = head_forward(query_raw[:, span], gq, cos_tab, sin_tab)[0].astype(LOW)
        key = head_forward(key_raw[:, span], gk, cos_tab, sin_tab)[0].astype(LOW)
        weights = soft_weights(query, key, length, head_dim**-0.5).astype(LOW)
        heads.append(dot_nn(weights, value[:, span]).astype(LOW))
    joined = heads[0] if len(heads) == 1 else jnp.concatenate(heads, axis=-1)
    keep(query_raw, key_raw, value, joined)
    return dot_nn(joined, wo[...]).astype(LOW)


def attend_kernel(
    pk_ref, wq, wk, wv, wo, gq, gk, cos_ref, sin_ref, part_ref, qr_ref, kr_ref, v_ref, o_ref
):
    rows = pk_ref.shape[1] - LINES
    length = pk_ref[0, rows:, rows : rows + 128].astype(WIDE)[0:1, 0:1]

    def keep(query_raw, key_raw, value, joined):
        qr_ref[0], kr_ref[0], v_ref[0], o_ref[0] = (query_raw, key_raw, value, joined)

    part_ref[0] = attend_block(
        pk_ref[0, :rows], length, wq, wk, wv, wo, gq[...], gk[...], cos_ref[...], sin_ref[...], keep
    )


def whole_spec(array):
    return pl.BlockSpec(array.shape, lambda *_: (0,) * array.ndim, pipeline_mode=pl.Buffered(1))


def first_spec(array):
    return pl.BlockSpec((1,) + array.shape[1:], lambda i: (i,) + (0,) * (array.ndim - 1))


def attend_forward(packets, wq, wk, wv, wo, gq, gk, cos_tab, sin_tab):
    count, lines, width = packets.shape
    rows, wide = (lines - LINES, wq.shape[1])
    fixed = (wq, wk, wv, wo, gq, gk, cos_tab, sin_tab)
    out = (
        jax.ShapeDtypeStruct((count, rows, width), LOW),
        jax.ShapeDtypeStruct((count, rows, wide), WIDE),
        jax.ShapeDtypeStruct((count, rows, wide), WIDE),
        jax.ShapeDtypeStruct((count, rows, wide), LOW),
        jax.ShapeDtypeStruct((count, rows, wide), LOW),
    )
    return pl.pallas_call(
        attend_kernel,
        grid=(count,),
        in_specs=[first_spec(packets)] + [whole_spec(array) for array in fixed],
        out_specs=[first_spec(array) for array in out],
        out_shape=out,
        compiler_params=pltpu.CompilerParams(vmem_limit_bytes=VMEM_BYTES),
        cost_estimate=COST,
        name="attend_forward",
    )(packets, *fixed)


def attend_back_kernel(
    da_ref, pk_ref, qr_ref, kr_ref, v_ref, o_ref,
    wq, wk, wv, wo, gq, gk, cos_ref, sin_ref,
    part_ref, gw_ref, gain_q, gain_k, gain_n, gw_sum,
):
    rows = pk_ref.shape[1] - LINES
    head_dim = gq.shape[-1]
    length = pk_ref[0, rows:, rows : rows + 128].astype(WIDE)[0:1, 0:1]
    cos_tab, sin_tab = (cos_ref[...], sin_ref[...])
    score_scale = head_dim**-0.5

    @pl.when(pl.program_id(0) == 0)
    def _():
        for ref in (gw_sum, gain_q, gain_k, gain_n):
            ref[...] = jnp.zeros_like(ref)

    upper = da_ref[0]
    grad_joined = dot_nt(upper, wo[...]).astype(LOW)
    wide = qr_ref.shape[-1]
    gw_sum[:, 3 * wide :] += dot_tn(upper, o_ref[0])
    grads_q, grads_k, grads_v = ([], [], [])
    for head in range(qr_ref.shape[-1] // head_dim):
        span = slice(head * head_dim, (head + 1) * head_dim)
        query, plain_q, scale_q = head_forward(qr_ref[0, :, span], gq[...], cos_tab, sin_tab)
        key, plain_k, scale_k = head_forward(kr_ref[0, :, span], gk[...], cos_tab, sin_tab)
        query, key, value = (query.astype(LOW), key.astype(LOW), v_ref[0, :, span])
        probs = soft_weights(query, key, length, score_scale)
        grad_out = grad_joined[:, span]
        grads_v.append(dot_tn(probs.astype(LOW), grad_out).astype(LOW))
        grad_probs = dot_nt(grad_out, value)
        inner = jnp.sum(probs * grad_probs, axis=-1, keepdims=True)
        grad_scores = (probs * (grad_probs - inner)).astype(LOW)
        grad_q, head_gain_q = head_backward(
            dot_nn(grad_scores, key) * score_scale, plain_q, scale_q, gq[...], cos_tab, sin_tab
        )
        grad_k, head_gain_k = head_backward(
            dot_tn(grad_scores, query) * score_scale, plain_k, scale_k, gk[...], cos_tab, sin_tab
        )
        gain_q[...] += head_gain_q
        gain_k[...] += head_gain_k
        grads_q.append(grad_q.astype(LOW))
        grads_k.append(grad_k.astype(LOW))
    grads = jnp.concatenate(grads_q + grads_k + grads_v, axis=-1)
    part = (
        dot_nt(grads[:, :wide], wq[...])
        + dot_nt(grads[:, wide : 2 * wide], wk[...])
        + dot_nt(grads[:, 2 * wide :], wv[...])
    )
    normed = pk_ref[0, :rows]
    part_ref[0] = part.astype(LOW)
    gain_n[...] += jnp.sum(part * normed.astype(WIDE), axis=0, keepdims=True)
    gw_sum[:, : 3 * wide] += dot_tn(normed, grads)

    @pl.when(pl.program_id(0) == pl.num_programs(0) - 1)
    def _():
        gw_ref[...] = gw_sum[...].astype(LOW)


def attend_backward(upper, packets, kept, wq, wk, wv, wo, gq, gk, cos_tab, sin_tab):
    count, lines, width = packets.shape
    rows, wide = (lines - LINES, wq.shape[1])
    blocks = (upper, packets) + tuple(kept)
    fixed = (wq, wk, wv, wo, gq, gk, cos_tab, sin_tab)
    sums = tuple(
        jax.ShapeDtypeStruct(shape, kind)
        for shape, kind in (
            ((width, 4 * wide), LOW), (gq.shape, WIDE), (gk.shape, WIDE), ((1, width), WIDE)
        )
    )
    return pl.pallas_call(
        attend_back_kernel,
        grid=(count,),
        in_specs=[first_spec(array) for array in blocks] + [whole_spec(array) for array in fixed],
        out_specs=[first_spec(upper)] + [whole_spec(array) for array in sums],
        out_shape=(jax.ShapeDtypeStruct((count, rows, width), LOW),) + sums,
        scratch_shapes=[pltpu.VMEM((width, 4 * wide), WIDE)],
        compiler_params=pltpu.CompilerParams(vmem_limit_bytes=VMEM_BYTES),
        cost_estimate=COST,
        name="attend_backward",
    )(*blocks, *fixed)


def slot_spots(table, expert):
    row_count = table.shape[1]
    slots = lax.broadcasted_iota(jnp.int32, (CAP, row_count), 0).astype(WIDE) + 1.0
    mine = lax.broadcasted_iota(jnp.int32, table.shape, 0) == expert
    ranks = jnp.sum(jnp.where(mine, table, 0.0), axis=0, keepdims=True)
    return (slots == ranks).astype(LOW)


class Trades:
    def __init__(self, trades):
        self.trades = trades
        self.axes = sorted({(axis, size) for _, axis, size, _ in trades})
        self.arrays = [array for array, _, _, _ in trades]
        self.in_specs = [pl.BlockSpec(memory_space=pltpu.VMEM) for _ in trades]
        self.out_specs = [pl.BlockSpec(memory_space=pl.ANY) for _ in trades]
        self.out_shapes = [
            jax.ShapeDtypeStruct(array.shape if pieces else (size,) + array.shape, array.dtype)
            for array, _, size, pieces in trades
        ]
        self.scratch = [
            pltpu.SemaphoreType.DMA((size,)) for _, _, size, _ in trades for _ in range(2)
        ]

    def bind(self, sources, targets, sems):
        self.sources, self.targets, self.sems = (sources, targets, sems)

    def device(self, axis, size, bits):
        return {axis: lax.rem(lax.axis_index(axis) + bits, size)}

    def copies(self):
        for number, (_, axis, size, pieces) in enumerate(self.trades):
            me = lax.axis_index(axis)
            send, recv = (self.sems[2 * number], self.sems[2 * number + 1])
            target = self.targets[number].at[me]
            for bits in range(size):
                source = self.sources[number]
                source = source.at[lax.rem(me + bits, size)] if pieces else source
                if bits == 0:
                    yield pltpu.make_async_copy(source, target, send.at[0])
                else:
                    yield pltpu.make_async_remote_copy(
                        source, target, send.at[bits], recv.at[bits],
                        device_id=self.device(axis, size, bits),
                        device_id_type=pl.DeviceIdType.MESH,
                    )

    def start(self):
        barrier = pltpu.get_barrier_semaphore()
        for axis, size in self.axes:
            for bits in range(1, size):
                pl.semaphore_signal(
                    barrier, inc=1, device_id=self.device(axis, size, bits),
                    device_id_type=pl.DeviceIdType.MESH,
                )
        pl.semaphore_wait(barrier, sum(size - 1 for _, size in self.axes))
        for copy in self.copies():
            copy.start()

    def finish(self):
        for copy in self.copies():
            copy.wait()


UNIT = 2


def expert_kernel(row_counts, cot_counts, batch, trades, ex_ref, wg, wu, wd, wr, *refs):
    first, second = (len(row_counts), len(row_counts) + len(cot_counts))
    rows_in, cots_in = (refs[:first], refs[first:second])
    third, number = (second + len(trades.trades), len(trades.trades))
    x_ref, y_ref, m_ref, dg_ref, du_ref, dgate_ref = refs[third : third + 6]
    rows_buf, cots_buf, sems = refs[third + 6 + number : third + 9 + number]
    trades.bind(refs[second:third], refs[third + 6 : third + 6 + number], refs[third + 9 + number :])
    steps, units = (sum(row_counts) // batch, batch // UNIT)
    turn = pl.program_id(0) * steps + pl.program_id(1)
    slot = lax.rem(turn, 2)
    row_count = rows_buf.shape[2]

    def copy(kind, source, offset, place, part):
        buffer = (rows_buf, cots_buf)[kind]
        return pltpu.make_async_copy(
            source.at[pl.ds(offset, UNIT)],
            buffer.at[place, pl.ds(part * UNIT, UNIT)],
            sems.at[kind, place, part],
        )

    def fetch(step, place):
        for part in range(units):
            unit = step * units + part
            for kind, sources, counts in ((0, rows_in, row_counts), (1, cots_in, cot_counts)):
                begin = 0
                for source, count in zip(sources, counts):
                    size = count // UNIT

                    @pl.when((unit >= begin) & (unit < begin + size))
                    def _(source=source, begin=begin):
                        copy(kind, source, (unit - begin) * UNIT, place, part).start()

                    begin += size

    @pl.when(turn == 0)
    def _():
        fetch(turn, slot)
        if number:
            trades.start()

    @pl.when(turn + 1 < pl.num_programs(0) * steps)
    def _():
        fetch(lax.rem(turn + 1, steps), 1 - slot)

    for part in range(units):
        copy(0, rows_in[0], 0, slot, part).wait()
        copy(1, cots_in[0], 0, slot, part).wait()
    hidden = wg.shape[-1]
    expert = ex_ref[pl.program_id(0)]
    for seq in range(batch):
        table = cots_buf[slot, seq, row_count:, :row_count].astype(WIDE)
        spots = slot_spots(table, expert)
        span = pl.ds(seq * CAP, CAP)
        x_ref[0, span] = dot_nn(spots, rows_buf[slot, seq]).astype(LOW)
        y_ref[0, span] = dot_nn(spots, cots_buf[slot, seq, :row_count]).astype(LOW)
    x_all, y_all = (x_ref[0], y_ref[0])
    logits = dot_nn(x_all, wr[...])
    expo = jnp.exp(logits - jnp.max(logits, axis=-1, keepdims=True))
    chosen = lax.broadcasted_iota(jnp.int32, expo.shape, 1) == expert
    gates = jnp.sum(jnp.where(chosen, expo, 0.0), axis=-1, keepdims=True) / jnp.sum(
        expo, axis=-1, keepdims=True
    )
    step = min(256, hidden)
    dgate = jnp.zeros((x_all.shape[0], 1), WIDE)
    for start in range(0, hidden, step):
        span = slice(start, start + step)
        gate_act, up_act = (dot_nn(x_all, wg[0, :, span]), dot_nn(x_all, wu[0, :, span]))
        plain_grad = dot_nt(y_all, wd[0, span, :])
        sig = jax.nn.sigmoid(gate_act)
        silu = gate_act * sig
        joined = silu * up_act
        dgate += jnp.sum(joined * plain_grad, axis=-1, keepdims=True)
        grad = plain_grad * gates
        m_ref[0, :, span] = (joined * gates).astype(LOW)
        dg_ref[0, :, span] = (grad * up_act * (sig + silu * (1.0 - sig))).astype(LOW)
        du_ref[0, :, span] = (grad * silu).astype(LOW)
    dgate_ref[0] = jnp.broadcast_to(dgate, dgate_ref.shape[1:])
    if number:

        @pl.when(turn == pl.num_programs(0) * steps - 1)
        def _():
            trades.finish()


def expert_acts(ids, rows, cots, wg, wu, wd, wr, batch=4, trades=(), collective=None):
    trades = Trades(trades)
    row_count, width = rows[0].shape[1:]
    row_counts, cot_counts = ([array.shape[0] for array in arrays] for arrays in (rows, cots))
    count = sum(row_counts)
    own, _, hidden = wg.shape
    out_rows = batch * CAP

    def acts(cols, kind=LOW):
        return jax.ShapeDtypeStruct((own, count * CAP, cols), kind)

    def act_spec(cols):
        return pl.BlockSpec((1, out_rows, cols), lambda e, i: (e, i, 0))

    def weight_spec(array):
        return pl.BlockSpec(
            (1,) + array.shape[1:], lambda e, i: (e, 0, 0), pipeline_mode=pl.Buffered(1)
        )

    any_spec = pl.BlockSpec(memory_space=pl.ANY)
    columns = (width, width, hidden, hidden, hidden, 128)
    return pl.pallas_call(
        functools.partial(expert_kernel, row_counts, cot_counts, batch, trades),
        grid=(own, count // batch),
        in_specs=[
            pl.BlockSpec(memory_space=pltpu.SMEM),
            weight_spec(wg),
            weight_spec(wu),
            weight_spec(wd),
            pl.BlockSpec(wr.shape, lambda e, i: (0, 0)),
        ]
        + [any_spec] * (len(rows) + len(cots))
        + trades.in_specs,
        out_specs=[act_spec(cols) for cols in columns] + trades.out_specs,
        out_shape=[acts(cols) for cols in columns[:5]] + [acts(128, WIDE)] + trades.out_shapes,
        scratch_shapes=[
            pltpu.VMEM((2, batch) + rows[0].shape[1:], LOW),
            pltpu.VMEM((2, batch) + cots[0].shape[1:], LOW),
            pltpu.SemaphoreType.DMA((2, 2, batch // UNIT)),
        ]
        + trades.scratch,
        compiler_params=pltpu.CompilerParams(
            vmem_limit_bytes=VMEM_BYTES,
            collective_id=collective,
            has_side_effects=collective is not None,
        ),
        cost_estimate=COST,
        name="expert_acts",
    )(ids, wg, wu, wd, wr, *rows, *cots, *trades.arrays)


def pull_kernel(ex_ref, rows_ref, cot_ref, dg_ref, du_ref, dgate_ref, wg, wu, wr, part_ref, router):
    batch, row_count, _ = rows_ref.shape
    own = wg.shape[0]

    @pl.when(pl.program_id(0) == 0)
    def _():
        router[...] = jnp.zeros_like(router)

    backs = [
        (dot_nt(dg_ref[e], wg[e]) + dot_nt(du_ref[e], wu[e])).astype(LOW) for e in range(own)
    ]
    for seq in range(batch):
        table = cot_ref[seq, :, :row_count].astype(WIDE)
        logits = dot_nn(rows_ref[seq], wr[...])
        expo = jnp.exp(logits - jnp.max(logits, axis=-1, keepdims=True))
        probs = expo / jnp.sum(expo, axis=-1, keepdims=True)
        columns = lax.broadcasted_iota(jnp.int32, probs.shape, 1)
        grad_logits = jnp.zeros_like(probs)
        span = slice(seq * CAP, (seq + 1) * CAP)
        total = jnp.zeros(part_ref.shape[1:], WIDE)
        for e in range(own):
            spots = slot_spots(table, ex_ref[e])
            total += dot_tn(spots, backs[e][span])
            dgate = dgate_ref[e, span]
            high = dgate.astype(LOW)
            rest = (dgate - high.astype(WIDE)).astype(LOW)
            at_rows = (dot_tn(spots, high) + dot_tn(spots, rest))[:, : probs.shape[1]]
            chosen = (columns == ex_ref[e]).astype(WIDE)
            prob = jnp.sum(probs * chosen, axis=-1, keepdims=True)
            grad_logits += at_rows * prob * (chosen - probs)
        low_logits = grad_logits.astype(LOW)
        part_ref[seq] = (total + dot_nt(low_logits, wr[...])).astype(LOW)
        router[...] += dot_tn(low_logits, rows_ref[seq])


def mix_kernel(ex_ref, cot_ref, m_ref, wd, part_ref):
    batch, row_count, _ = part_ref.shape
    own = wd.shape[0]
    outs = [dot_nn(m_ref[e], wd[e]).astype(LOW) for e in range(own)]
    for seq in range(batch):
        table = cot_ref[seq, :, :row_count].astype(WIDE)
        span = slice(seq * CAP, (seq + 1) * CAP)
        total = sum(dot_tn(slot_spots(table, ex_ref[e]), outs[e][span]) for e in range(own))
        part_ref[seq] = total.astype(LOW)


def spread_call(kernel, name, ids, by_seq, cots, by_slot, fixed, router_shape, batch=2):
    count, lines, width = cots.shape
    row_count = lines - LINES
    part = jax.ShapeDtypeStruct((count, row_count, width), LOW)

    def seq_spec(array):
        return pl.BlockSpec((batch,) + array.shape[1:], lambda i: (i, 0, 0))

    def slot_spec(array):
        return pl.BlockSpec((array.shape[0], batch * CAP, array.shape[2]), lambda i: (0, i, 0))

    return pl.pallas_call(
        kernel,
        grid=(count // batch,),
        in_specs=[pl.BlockSpec(memory_space=pltpu.SMEM)]
        + [seq_spec(array) for array in by_seq]
        + [pl.BlockSpec((batch, LINES, width), lambda i: (i, row_count // LINES, 0))]
        + [slot_spec(array) for array in by_slot]
        + [whole_spec(array) for array in fixed],
        out_specs=[seq_spec(part)] + [whole_spec(shape) for shape in router_shape],
        out_shape=[part] + list(router_shape),
        compiler_params=pltpu.CompilerParams(vmem_limit_bytes=VMEM_BYTES),
        cost_estimate=COST,
        name=name,
    )(ids, *by_seq, cots, *by_slot, *fixed)


def weight_grad(lefts, rights, start=None):
    own, _, left_cols = lefts[0].shape
    right_cols = rights[0].shape[-1]
    sets = len(lefts)
    left_tile, right_tile = (min(512, left_cols), min(1024, right_cols))

    def kernel(*refs):
        total = sum(dot_tn(refs[i][0], refs[sets + i][0]) for i in range(sets))
        refs[-1][0] = total if start is None else total + refs[2 * sets][0]

    out_spec = pl.BlockSpec((1, left_tile, right_tile), lambda e, r, l: (e, l, r))
    return pl.pallas_call(
        kernel,
        grid=(own, right_cols // right_tile, left_cols // left_tile),
        in_specs=[
            pl.BlockSpec((1, array.shape[1], left_tile), lambda e, r, l: (e, 0, l))
            for array in lefts
        ]
        + [
            pl.BlockSpec((1, array.shape[1], right_tile), lambda e, r, l: (e, 0, r))
            for array in rights
        ]
        + [out_spec] * (start is not None),
        out_specs=out_spec,
        out_shape=jax.ShapeDtypeStruct((own, left_cols, right_cols), WIDE),
        input_output_aliases={} if start is None else {2 * sets: 0},
        compiler_params=pltpu.CompilerParams(vmem_limit_bytes=VMEM_BYTES),
        cost_estimate=COST,
        name="weight_grad",
    )(*lefts, *rights, *([] if start is None else [start]))


CHUNKS = 4
NEAR_LINES = 128


def front_kernel(
    replicas, groups,
    packet, cot, tokens, wq, wk, wv, wo, gq, gk, cos_ref, sin_ref, gain_ref,
    packets, qr_ref, kr_ref, v_ref, o_ref, hidden, rows_all, cots, fx, fy, fd, px, py, pd,
    nb, mine, pair_out, pair_in, line_r, line_l, low,
    n1_send, n1_recv, n1_pair, n2_send, n2_recv, n2_pair, cz_send, cz_recv, cz_pair,
    xy_send, xy_recv, dg_send, dg_recv, fl_send, fl_recv,
    po_send, po_recv, lr_send, lr_recv, ll_send, ll_recv, keep_sem, own_sem,
):
    rail = groups // 2
    rep, shard = (lax.axis_index("rep"), lax.axis_index("shard"))
    place, core = (shard // 2, shard % 2)
    rows = tokens.shape[0]
    step_rows = rows // CHUNKS
    last = rail - 1
    right, left, partner = ((rep, shard + 2), (rep, shard - 2), (rep, shard + 1 - 2 * core))
    over_x = (rep + 1 - 2 * (rep % 2), shard)
    over_y = ((rep + 2) % replicas, shard)

    def remote(source, target, send, recv, device):
        return pltpu.make_async_remote_copy(
            source, target, send, recv, device_id=device, device_id_type=pl.DeviceIdType.MESH
        )

    def each(size, body):
        def step(i, carry):
            body(i)
            return carry

        lax.fori_loop(0, size, step, 0)

    class Flood:
        def __init__(self, view, send, recv, pair, own):
            self.view, self.send, self.recv, self.pair, self.own = (view, send, recv, pair, own)

        def copy(self, way, q, own=False):
            slot = 2 * q + core
            source = self.own if own else self.view.at[slot]
            recv = self.pair.at[q] if way == 2 else self.recv.at[q]
            device = (right, left, partner)[way]
            return remote(source, self.view.at[slot], self.send.at[way, q], recv, device)

        def start_line(self):
            @pl.when(place < last)
            def _():
                self.copy(0, place, True).start()

            @pl.when(place > 0)
            def _():
                self.copy(1, place, True).start()

        def start_pair(self):
            self.copy(2, place, True).start()

        def onward(self, d, more=None):
            @pl.when((d > 0) & (place - d >= 0))
            def _():
                q = place - d
                self.copy(0, q).wait_recv()

                @pl.when(place < last)
                def _():
                    self.copy(0, q).start()

                self.copy(2, q).start()
                if more is not None:
                    more(q)

            @pl.when((d > 0) & (place + d <= last))
            def _():
                q = place + d
                self.copy(1, q).wait_recv()

                @pl.when(place > 0)
                def _():
                    self.copy(1, q).start()

                self.copy(2, q).start()
                if more is not None:
                    more(q)

        def wait_pair(self, q):
            slot = 2 * q + 1 - core
            remote(
                self.view.at[slot], self.view.at[slot], self.send.at[2, q], self.pair.at[q], partner
            ).wait_recv()

        def finish(self, pairs):
            def body(q):
                @pl.when((place < last) & (q <= place))
                def _():
                    self.copy(0, q).wait_send()

                @pl.when((place > 0) & (q >= place))
                def _():
                    self.copy(1, q).wait_send()

                self.copy(2, q).wait_send()
                if pairs:
                    self.wait_pair(q)

            each(rail, body)

    flood_n1 = Flood(nb, n1_send, n1_recv, n1_pair, packet)
    flood_n2 = Flood(rows_all, n2_send, n2_recv, n2_pair, low)
    flood_cot = Flood(cots, cz_send, cz_recv, cz_pair, cot)

    def cross(way, q, own=False):
        source = cot if own else cots.at[2 * q + core]
        target, device = ((fx, over_x), (fy, over_y))[way]
        return remote(source, target.at[q], xy_send.at[way, q], xy_recv.at[way, q], device)

    def cross_both(q):
        cross(0, q).start()
        cross(1, q).start()

    def diagonal(way, q):
        source, device = ((fx, over_y), (fy, over_x))[way]
        span = (pl.ds(0, NEAR_LINES), pl.ds(NEAR_LINES, cot.shape[0] - NEAR_LINES))[way]
        return remote(
            source.at[q, span], fd.at[q, span], dg_send.at[way, q], dg_recv.at[way, q], device
        )

    def flip(which, q):
        source, target = ((fx, px), (fy, py), (fd, pd))[which]
        return remote(
            source.at[q], target.at[q], fl_send.at[which, q], fl_recv.at[which, q], partner
        )

    def at_distance(d, body):
        if d < 0 or d > last:
            return
        if d == 0:
            body(place)
            return

        @pl.when(place - d >= 0)
        def _():
            body(place - d)

        @pl.when(place + d <= last)
        def _():
            body(place + d)

    def take_cross(q):
        for way in (0, 1):
            cross(way, q).wait_recv()
            diagonal(way, q).start()
            flip(way, q).start()

    def take_diagonal(q):
        for way in (0, 1):
            diagonal(way, q).wait_recv()
        flip(2, q).start()

    def event(d):
        if 1 <= d <= last:
            flood_cot.onward(d, cross_both)
        at_distance(d - 1, take_cross)
        at_distance(d - 2, take_diagonal)

    barrier = pltpu.get_barrier_semaphore()

    def greet(device):
        pl.semaphore_signal(
            barrier, inc=1, device_id=device, device_id_type=pl.DeviceIdType.MESH
        )

    for device in (partner, over_x, over_y):
        greet(device)

    @pl.when(place < last)
    def _():
        greet(right)

    @pl.when(place > 0)
    def _():
        greet(left)

    inner = (place > 0) & (place < last)

    @pl.when(inner)
    def _():
        pl.semaphore_wait(barrier, 5)

    @pl.when(jnp.logical_not(inner))
    def _():
        pl.semaphore_wait(barrier, 4)

    flood_n1.start_line()
    flood_n1.start_pair()
    own_block = pltpu.make_async_copy(packet, nb.at[shard], own_sem.at[0])
    own_block.start()
    own_cot = pltpu.make_async_copy(cot, cots.at[shard], own_sem.at[1])
    own_cot.start()
    cross(0, place, True).start()
    cross(1, place, True).start()
    flood_cot.start_pair()
    own_block.wait()

    def partial_out(q):
        return remote(
            pair_out.at[q], pair_in.at[q], po_send.at[q], po_recv.at[q], partner
        )

    def line(q, chunk, to_right):
        span = pl.ds(pl.multiple_of(chunk * step_rows, step_rows), step_rows)
        target, send, recv, device = (
            (line_r, lr_send, lr_recv, right) if to_right else (line_l, ll_send, ll_recv, left)
        )
        return remote(
            mine.at[q, span], target.at[q, span], send.at[q, chunk], recv.at[q, chunk], device
        )

    def add_up(q, chunk, extras):
        span = pl.ds(pl.multiple_of(chunk * step_rows, step_rows), step_rows)
        total = mine[q, span].astype(WIDE) + pair_in[q, span].astype(WIDE)
        for extra in extras:
            total = total + extra[q, span].astype(WIDE)
        return total

    def forward_line(q, to_right, first):
        partial_out(q).wait_recv()

        def body(chunk):
            extras = []
            if not first:
                line(q, chunk, to_right).wait_recv()
                extras = [line_r if to_right else line_l]
            span = pl.ds(pl.multiple_of(chunk * step_rows, step_rows), step_rows)
            mine[q, span] = add_up(q, chunk, extras).astype(LOW)
            line(q, chunk, to_right).start()

        each(CHUNKS, body)

    def keep_copy(slot):
        return pltpu.make_async_copy(nb.at[slot], packets.at[slot], keep_sem.at[slot])

    def one_distance(d):
        flood_n1.onward(d)

        def one_block(k):
            side, other = (k % 2, k // 2)
            q = place + (2 * side - 1) * d

            @pl.when((q >= 0) & (q <= last) & ((d > 0) | (side == 0)))
            def _():
                @pl.when(other == 1)
                def _():
                    flood_n1.wait_pair(q)

                slot = 2 * q + core + other * (1 - 2 * core)
                keep_copy(slot).start()
                length = nb[slot, rows:, rows : rows + 128].astype(WIDE)[0:1, 0:1]

                def keep(query_raw, key_raw, value, joined):
                    qr_ref[slot], kr_ref[slot] = (query_raw, key_raw)
                    v_ref[slot], o_ref[slot] = (value, joined)

                part = attend_block(
                    nb[slot, :rows], length, wq, wk, wv, wo, gq[...], gk[...],
                    cos_ref[...], sin_ref[...], keep,
                )

                @pl.when(other == 0)
                def _():
                    mine[q] = part

                @pl.when(other == 1)
                def _():
                    pair_out[q] = part
                    partial_out(q).start()

        each(4, one_block)

        @pl.when((place == 0) & (d > 0))
        def _():
            forward_line(d, True, True)

        @pl.when((place == last) & (d > 0))
        def _():
            forward_line(last - d, False, True)

    each(rail, one_distance)
    flood_cot.start_line()

    def rest_right():
        def body(j):
            @pl.when((place > 0) & (place + j <= last))
            def _():
                forward_line(place + j, True, False)

        each(last, lambda i: body(i + 1))

    def rest_left():
        def body(j):
            @pl.when((place < last) & (place - j >= 0))
            def _():
                forward_line(place - j, False, False)

        each(last, lambda i: body(i + 1))

    near_end = place < rail // 2
    pl.when(near_end)(rest_right)
    pl.when(jnp.logical_not(near_end))(rest_left)
    event(1)
    pl.when(near_end)(rest_left)
    pl.when(jnp.logical_not(near_end))(rest_right)

    partial_out(place).wait_recv()

    def finish_rows(chunk):
        @pl.when(place > 0)
        def _():
            line(place, chunk, True).wait_recv()

        @pl.when(place < last)
        def _():
            line(place, chunk, False).wait_recv()

        span = pl.ds(pl.multiple_of(chunk * step_rows, step_rows), step_rows)
        total = tokens[span].astype(WIDE) + add_up(place, chunk, [])
        from_left = jnp.where(place > 0, line_r[place, span].astype(WIDE), 0.0)
        from_right = jnp.where(place < last, line_l[place, span].astype(WIDE), 0.0)
        total = total + from_left + from_right
        hidden[span] = total
        scale = lax.rsqrt(jnp.mean(total * total, axis=-1, keepdims=True) + EPS_NORM)
        low[span] = (total * scale * gain_ref[...]).astype(LOW)

    each(CHUNKS, finish_rows)
    flood_n2.start_line()
    flood_n2.start_pair()
    own_low = pltpu.make_async_copy(low, rows_all.at[shard], own_sem.at[2])
    own_low.start()

    event(2)
    for d in range(1, rail):
        flood_n2.onward(d)
        event(d + 2)

    flood_n1.finish(False)
    flood_n2.finish(True)
    flood_cot.finish(True)
    own_cot.wait()
    own_low.wait()

    def settle(q):
        keep_copy(2 * q).wait()
        keep_copy(2 * q + 1).wait()
        partial_out(q).wait_send()
        for way in (0, 1):
            cross(way, q).wait_send()
            diagonal(way, q).wait_send()
        for which in (0, 1, 2):
            flip(which, q).wait_send()
            flip(which, q).wait_recv()

        def chunk_sends(chunk):
            @pl.when((place < last) & (q > place))
            def _():
                line(q, chunk, True).wait_send()

            @pl.when((place > 0) & (q < place))
            def _():
                line(q, chunk, False).wait_send()

        each(CHUNKS, chunk_sends)

    each(rail, settle)


def front(replicas, groups, packet, cot, tokens, wq, wk, wv, wo, gq, gk, cos_tab, sin_tab, gain):
    lines, width = packet.shape
    rows, wide, rail = (tokens.shape[0], wq.shape[1], groups // 2)
    any_spec, fast = (pl.BlockSpec(memory_space=pl.ANY), pl.BlockSpec(memory_space=pltpu.VMEM))

    def shape(*dims, kind=LOW):
        return jax.ShapeDtypeStruct(dims, kind)

    far = [shape(rail, lines, width)] * 6
    block = pltpu.VMEM((rail, rows, width), LOW)
    dma = pltpu.SemaphoreType.DMA
    return pl.pallas_call(
        functools.partial(front_kernel, replicas, groups),
        in_specs=[any_spec] * 2 + [fast] * 10,
        out_specs=[any_spec] + [fast] * 5 + [any_spec] * 8,
        out_shape=[
            shape(groups, lines, width),
            shape(groups, rows, wide, kind=WIDE),
            shape(groups, rows, wide, kind=WIDE),
            shape(groups, rows, wide),
            shape(groups, rows, wide),
            shape(rows, width, kind=WIDE),
            shape(groups, rows, width),
            shape(groups, lines, width),
        ]
        + far,
        scratch_shapes=[
            pltpu.VMEM((groups, lines, width), LOW),
            block, block, block, block, block,
            pltpu.VMEM((rows, width), LOW),
        ]
        + [dma((3, rail)), dma((rail,)), dma((rail,))] * 3
        + [dma((2, rail))] * 4
        + [dma((3, rail))] * 2
        + [dma((rail,))] * 2
        + [dma((rail, CHUNKS))] * 4
        + [dma((groups,)), dma((3,))],
        compiler_params=pltpu.CompilerParams(
            vmem_limit_bytes=VMEM_BYTES, collective_id=0, has_side_effects=True
        ),
        cost_estimate=COST,
        name="front",
    )(packet, cot, tokens, wq, wk, wv, wo, gq, gk, cos_tab, sin_tab, gain)


def rms_parts(values):
    scale = lax.rsqrt(jnp.mean(values * values, axis=-1, keepdims=True) + EPS_NORM)
    return (values * scale, scale)


def rms_back(plain, scale, gain, grad):
    back = grad * gain
    return scale * (back - plain * jnp.mean(back * plain, axis=-1, keepdims=True))


def local(
    tokens, lengths, routes, gain_attn, gain_query, gain_key,
    w_query, w_key, w_value, w_out, gain_moe, w_router,
    w_gate, w_up, w_down, out_grad,
):
    row_count, width = tokens.shape
    head_dim = gain_query.shape[0]
    groups, replicas = (lax.axis_size("shard"), lax.axis_size("rep"))
    expert_count, own = (w_router.shape[1], w_gate.shape[0])
    wide = w_query.shape[1]
    after = lax.optimization_barrier
    gain_q, gain_k = (gain_query.reshape(1, -1), gain_key.reshape(1, -1))
    cos_tab, sin_tab = rope_tables(row_count, head_dim)
    ids = lax.axis_index("shard") * own + jnp.arange(own, dtype=jnp.int32)

    def flip_replica(values, bits):
        return lax.ppermute(values, "rep", [(i, i ^ bits) for i in range(replicas)])

    def flip_shard(values, bits):
        return lax.ppermute(values, "shard", [(i, i ^ bits) for i in range(groups)])

    def scatter_sum(parts):
        return lax.psum_scatter(
            parts.reshape(-1, width), "shard", scatter_dimension=0, tiled=True
        ).astype(WIDE)

    inputs = tokens.astype(WIDE)
    row_mask = (jnp.arange(row_count, dtype=jnp.int32) < lengths[0])[:, None]
    named = jnp.any(
        routes[None, :, :] == jnp.arange(expert_count, dtype=jnp.int32)[:, None, None], axis=-1
    )
    upto = (jnp.arange(row_count)[:, None] <= jnp.arange(row_count)[None, :]).astype(LOW)
    ranks = jnp.where(named, dot_nn(named.astype(LOW), upto), 0.0).astype(LOW)
    lines = jnp.concatenate(
        [ranks, jnp.broadcast_to(lengths[0].astype(LOW), (expert_count, width - row_count))], axis=1
    )
    plain_in, scale_in = rms_parts(inputs)
    packet = jnp.concatenate([(plain_in * gain_attn).astype(LOW), lines], axis=0)
    cot_low = jnp.where(row_mask, out_grad, 0.0)
    cot_packet = jnp.concatenate([cot_low, lines], axis=0)
    heads = (w_query, w_key, w_value, w_out, gain_q, gain_k, cos_tab, sin_tab)
    share = replicas == 4 and groups == 8
    if share:
        packets, *kept = front(
            replicas, groups, packet, cot_packet, tokens, *heads, gain_moe.reshape(1, -1)
        )
        kept, (hidden, rows_all, cots), far_cots = (kept[:4], kept[4:7], kept[7:])
        pairs = rows_all.reshape((groups // 2, 2) + rows_all.shape[1:])
        core = lax.axis_index("shard") % 2
        near = [
            lax.dynamic_index_in_dim(part, core, 1, keepdims=False) for part in (pairs[:2], pairs[2:])
        ]
        rows_all, near = after((rows_all, near))
    else:
        packets = lax.all_gather(packet, "shard", axis=0)
        cot_packet, packets = after((cot_packet, packets))
        cots = lax.all_gather(cot_packet, "shard", axis=0)
        part, *kept = attend_forward(packets, *heads)
        hidden = inputs + scatter_sum(part)
        plain_mid, scale_mid = rms_parts(hidden)
        rows_all = lax.all_gather((plain_mid * gain_moe).astype(LOW), "shard", axis=0)

    acts = [expert_acts(ids, [rows_all], [cots], w_gate, w_up, w_down, w_router)]
    if share:
        early, late = ([flip_replica(part, bits) for bits in (1, 2)] for part in near)
        acts, early = after((acts, early))
    _, _, gated, grad_gate_act, grad_up_act, dgates = acts[0]
    router_shape = (jax.ShapeDtypeStruct(w_router.shape[::-1], WIDE),)
    pull_part, grad_router = spread_call(
        pull_kernel, "expert_pull", ids, (rows_all,), cots,
        (grad_gate_act, grad_up_act, dgates), (w_gate, w_up, w_router), router_shape,
    )
    if share:
        early_flipped = [flip_shard(values, 1) for values in early]
        pull_part, late, early_flipped = after((pull_part, late, early_flipped))
    grad_moe_in = scatter_sum(pull_part)
    gated, pull_part = after((gated, pull_part))
    if share:
        diagonal = [flip_replica(early[0], 2), flip_replica(late[1], 1)]
        late_flipped = [flip_shard(values, 1) for values in late]
        near, pull_part = after(([early[0], late[0], early[1], late[1]], pull_part))
        acts.append(expert_acts(ids, near, far_cots[0:2], w_gate, w_up, w_down, w_router))
        acts, diagonal, late_flipped = after((acts, diagonal, late_flipped))
        gated, acts = after((gated, acts))
        flipped = [early_flipped[0], late_flipped[0], early_flipped[1], late_flipped[1]]
        diagonal_flipped = [flip_shard(values, 1) for values in diagonal]
    (mix_part,) = spread_call(mix_kernel, "expert_mix", ids, (), cots, (gated,), (w_down,), ())
    if share:
        mix_part, diagonal_flipped = after((mix_part, diagonal_flipped))
        grad_moe_in, mix_part = after((grad_moe_in, mix_part))

    grad_out = cot_low.astype(WIDE)
    if share:
        hidden, grad_moe_in = after((hidden, grad_moe_in))
        plain_mid, scale_mid = rms_parts(hidden)
    grad_hidden = grad_out + rms_back(plain_mid, scale_mid, gain_moe, grad_moe_in)
    gain_moe_sum = jnp.sum(grad_moe_in * plain_mid, axis=0)
    branch_low = grad_hidden.astype(LOW)
    upper = lax.all_gather(branch_low, "shard", axis=0)
    if share:
        acts, branch_low = after((acts, branch_low))
        started = [
            weight_grad([act[left] for act in acts], [act[right] for act in acts])
            for left, right in ((0, 3), (0, 4), (2, 1))
        ]
        upper, started = after((upper, started))
    mix_part, upper = after((mix_part, upper))
    mixture = scatter_sum(mix_part)
    part, gw_low, sum_q, sum_k, sum_n = attend_backward(upper, packets, kept, *heads)

    def sets(place):
        return [act[place] for act in acts]

    small = jnp.concatenate(
        [
            grad_router,
            gain_moe_sum[None],
            sum_n / gain_attn,
            jnp.pad(
                jnp.concatenate([sum_q, sum_k], axis=1), ((0, 0), (0, width - 2 * head_dim))
            ),
            jnp.zeros((5, width), WIDE),
        ]
    )
    if share:
        experts = (w_gate, w_up, w_down, w_router)
        pieces = gw_low.reshape((replicas, -1) + gw_low.shape[1:])
        *act, traded, smalls = expert_acts(
            ids, flipped, far_cots[3:5], *experts,
            trades=((pieces, "rep", replicas, True), (small, "rep", replicas, False)), collective=1,
        )
        act, traded, smalls, part, mixture = after((act, traded, smalls, part, mixture))
        acts = [act]
        grad_normed = scatter_sum(part)
        low = jnp.sum(traded.astype(WIDE), axis=0).astype(LOW)
        small = jnp.sum(smalls, axis=0)
        *act, found, smalls = expert_acts(
            ids, diagonal + diagonal_flipped, [far_cots[2], far_cots[5]], *experts,
            trades=((low, "rep", replicas, False), (small, "shard", groups, False)), collective=2,
        )
        acts.append(act)
        gw_sum = found.reshape(gw_low.shape)
        small = jnp.sum(smalls, axis=0)
        grad_gate_w, grad_up_w, grad_down = (
            weight_grad(sets(left), sets(right), begun)
            for (left, right), begun in zip(((0, 3), (0, 4), (2, 1)), started)
        )
    else:
        grad_normed = scatter_sum(part)
        over_reps = lax.psum(
            (gw_low,)
            + tuple(
                weight_grad(sets(left), sets(right)).astype(LOW)
                for left, right in ((0, 3), (0, 4), (2, 1))
            ),
            "rep",
        )
        gw_sum = over_reps[0]
        grad_gate_w, grad_up_w, grad_down = (values.astype(WIDE) for values in over_reps[1:])
        small = lax.psum(small, ("rep", "shard"))
    grads_q, grads_k, grads_v, grads_o = (
        gw_sum[:, i * wide : (i + 1) * wide].astype(WIDE) for i in range(4)
    )
    grad_router = small[:expert_count].T
    grad_gain_moe, grad_gain_attn = (small[expert_count], small[expert_count + 1])
    grad_gain_query, grad_gain_key = (
        small[expert_count + 2, i * head_dim : (i + 1) * head_dim] for i in range(2)
    )
    output = (hidden + mixture).astype(LOW)
    grad_input = grad_hidden + rms_back(plain_in, scale_in, gain_attn, grad_normed)
    return (
        output, grad_input, grad_gain_attn, grad_gain_query, grad_gain_key,
        grads_q, grads_k, grads_v, grads_o.T,
        grad_gain_moe, grad_router, grad_gate_w, grad_up_w, grad_down,
    )


def solution(mesh):
    rows, flat, cols = (P(("rep", "shard"), None), P(), P(None, "shard"))
    lead, experts = (P("shard", None), P("shard", None, None))
    return jax.shard_map(
        local,
        mesh=mesh,
        in_specs=(
            rows, P(("rep", "shard")), rows, flat, flat, flat, cols, cols, cols, lead,
            flat, flat, experts, experts, experts, rows,
        ),
        out_specs=(
            rows, rows, flat, flat, flat, cols, cols, cols, lead,
            flat, flat, experts, experts, experts,
        ),
        check_vma=False,
    )
```

```python
import functools
import math

import jax
import jax.numpy as jnp
from jax import lax
from jax.experimental import pallas as pl
from jax.experimental.pallas import tpu as pltpu
from jax.sharding import PartitionSpec as P

CAP = 144
LINES = 16
EPS_NORM = 1e-06
ROPE_BASE = 50000.0
MASKED = -1e30
VMEM_BYTES = 60 * 1024 * 1024
LOW = jnp.bfloat16
WIDE = jnp.float32
COST = pl.CostEstimate(flops=1 << 20, bytes_accessed=1 << 16, transcendentals=0)


def dot_nn(a, b):
    return lax.dot_general(a, b, (((1,), (0,)), ((), ())), preferred_element_type=WIDE)


def dot_nt(a, b):
    return lax.dot_general(a, b, (((1,), (1,)), ((), ())), preferred_element_type=WIDE)


def dot_tn(a, b):
    return lax.dot_general(a, b, (((0,), (0,)), ((), ())), preferred_element_type=WIDE)


def rope_tables(seq_len, head_dim):
    half_dim = head_dim // 2
    places = jnp.arange(seq_len, dtype=WIDE)
    freqs = ROPE_BASE ** (-jnp.arange(half_dim, dtype=WIDE) * (2.0 / head_dim))
    angles = places[:, None] * freqs[None, :]
    cosine, sine = (jnp.cos(angles), jnp.sin(angles))
    return (
        jnp.concatenate([cosine, cosine], axis=-1),
        jnp.concatenate([-sine, sine], axis=-1),
    )


def head_forward(raw, gain, cos_tab, sin_tab):
    scale = lax.rsqrt(jnp.mean(raw * raw, axis=-1, keepdims=True) + EPS_NORM)
    plain = raw * scale
    scaled = plain * gain
    turned = pltpu.roll(scaled, raw.shape[-1] // 2, axis=1)
    return (scaled * cos_tab + turned * sin_tab, plain, scale)


def head_backward(grad, plain, scale, gain, cos_tab, sin_tab):
    back = grad * cos_tab + pltpu.roll(grad * sin_tab, grad.shape[-1] // 2, axis=1)
    gain_grad = jnp.sum(back * plain, axis=0, keepdims=True)
    back = back * gain
    raw_grad = scale * (back - plain * jnp.mean(back * plain, axis=-1, keepdims=True))
    return (raw_grad, gain_grad)


def soft_weights(query, key, length, score_scale):
    scores = dot_nt(query, key) * score_scale
    places = lax.broadcasted_iota(jnp.int32, scores.shape, 1).astype(WIDE)
    scores = jnp.where(places < length, scores, MASKED)
    expo = jnp.exp(scores - jnp.max(scores, axis=-1, keepdims=True))
    return expo / jnp.sum(expo, axis=-1, keepdims=True)


def attend_block(normed, length, wq, wk, wv, wo, gq, gk, cos_tab, sin_tab, keep):
    head_dim = gq.shape[-1]
    query_raw, key_raw = (dot_nn(normed, wq[...]), dot_nn(normed, wk[...]))
    value = dot_nn(normed, wv[...]).astype(LOW)
    heads = []
    for head in range(query_raw.shape[-1] // head_dim):
        span = slice(head * head_dim, (head + 1) * head_dim)
        query = head_forward(query_raw[:, span], gq, cos_tab, sin_tab)[0].astype(LOW)
        key = head_forward(key_raw[:, span], gk, cos_tab, sin_tab)[0].astype(LOW)
        weights = soft_weights(query, key, length, head_dim**-0.5).astype(LOW)
        heads.append(dot_nn(weights, value[:, span]).astype(LOW))
    joined = heads[0] if len(heads) == 1 else jnp.concatenate(heads, axis=-1)
    keep(query_raw, key_raw, value, joined)
    return dot_nn(joined, wo[...]).astype(LOW)


def attend_kernel(
    pk_ref, wq, wk, wv, wo, gq, gk, cos_ref, sin_ref, part_ref, qr_ref, kr_ref, v_ref, o_ref
):
    rows = pk_ref.shape[1] - LINES
    length = pk_ref[0, rows:, rows : rows + 128].astype(WIDE)[0:1, 0:1]

    def keep(query_raw, key_raw, value, joined):
        qr_ref[0], kr_ref[0], v_ref[0], o_ref[0] = (query_raw, key_raw, value, joined)

    part_ref[0] = attend_block(
        pk_ref[0, :rows], length, wq, wk, wv, wo, gq[...], gk[...], cos_ref[...], sin_ref[...], keep
    )


def whole_spec(array):
    return pl.BlockSpec(array.shape, lambda *_: (0,) * array.ndim, pipeline_mode=pl.Buffered(1))


def first_spec(array):
    return pl.BlockSpec((1,) + array.shape[1:], lambda i: (i,) + (0,) * (array.ndim - 1))


def attend_forward(packets, wq, wk, wv, wo, gq, gk, cos_tab, sin_tab):
    count, lines, width = packets.shape
    rows, wide = (lines - LINES, wq.shape[1])
    fixed = (wq, wk, wv, wo, gq, gk, cos_tab, sin_tab)
    out = (
        jax.ShapeDtypeStruct((count, rows, width), LOW),
        jax.ShapeDtypeStruct((count, rows, wide), WIDE),
        jax.ShapeDtypeStruct((count, rows, wide), WIDE),
        jax.ShapeDtypeStruct((count, rows, wide), LOW),
        jax.ShapeDtypeStruct((count, rows, wide), LOW),
    )
    return pl.pallas_call(
        attend_kernel,
        grid=(count,),
        in_specs=[first_spec(packets)] + [whole_spec(array) for array in fixed],
        out_specs=[first_spec(array) for array in out],
        out_shape=out,
        compiler_params=pltpu.CompilerParams(vmem_limit_bytes=VMEM_BYTES),
        cost_estimate=COST,
        name="attend_forward",
    )(packets, *fixed)


def attend_back_kernel(
    da_ref, pk_ref, qr_ref, kr_ref, v_ref, o_ref,
    wq, wk, wv, wo, gq, gk, cos_ref, sin_ref,
    part_ref, gw_ref, gain_q, gain_k, gain_n, gw_sum,
):
    rows = pk_ref.shape[1] - LINES
    head_dim = gq.shape[-1]
    length = pk_ref[0, rows:, rows : rows + 128].astype(WIDE)[0:1, 0:1]
    cos_tab, sin_tab = (cos_ref[...], sin_ref[...])
    score_scale = head_dim**-0.5

    @pl.when(pl.program_id(0) == 0)
    def _():
        for ref in (gw_sum, gain_q, gain_k, gain_n):
            ref[...] = jnp.zeros_like(ref)

    upper = da_ref[0]
    grad_joined = dot_nt(upper, wo[...]).astype(LOW)
    wide = qr_ref.shape[-1]
    gw_sum[:, 3 * wide :] += dot_tn(upper, o_ref[0])
    grads_q, grads_k, grads_v = ([], [], [])
    for head in range(qr_ref.shape[-1] // head_dim):
        span = slice(head * head_dim, (head + 1) * head_dim)
        query, plain_q, scale_q = head_forward(qr_ref[0, :, span], gq[...], cos_tab, sin_tab)
        key, plain_k, scale_k = head_forward(kr_ref[0, :, span], gk[...], cos_tab, sin_tab)
        query, key, value = (query.astype(LOW), key.astype(LOW), v_ref[0, :, span])
        probs = soft_weights(query, key, length, score_scale)
        grad_out = grad_joined[:, span]
        grads_v.append(dot_tn(probs.astype(LOW), grad_out).astype(LOW))
        grad_probs = dot_nt(grad_out, value)
        inner = jnp.sum(probs * grad_probs, axis=-1, keepdims=True)
        grad_scores = (probs * (grad_probs - inner)).astype(LOW)
        grad_q, head_gain_q = head_backward(
            dot_nn(grad_scores, key) * score_scale, plain_q, scale_q, gq[...], cos_tab, sin_tab
        )
        grad_k, head_gain_k = head_backward(
            dot_tn(grad_scores, query) * score_scale, plain_k, scale_k, gk[...], cos_tab, sin_tab
        )
        gain_q[...] += head_gain_q
        gain_k[...] += head_gain_k
        grads_q.append(grad_q.astype(LOW))
        grads_k.append(grad_k.astype(LOW))
    grads = jnp.concatenate(grads_q + grads_k + grads_v, axis=-1)
    part = (
        dot_nt(grads[:, :wide], wq[...])
        + dot_nt(grads[:, wide : 2 * wide], wk[...])
        + dot_nt(grads[:, 2 * wide :], wv[...])
    )
    normed = pk_ref[0, :rows]
    part_ref[0] = part.astype(LOW)
    gain_n[...] += jnp.sum(part * normed.astype(WIDE), axis=0, keepdims=True)
    gw_sum[:, : 3 * wide] += dot_tn(normed, grads)

    @pl.when(pl.program_id(0) == pl.num_programs(0) - 1)
    def _():
        gw_ref[...] = gw_sum[...].astype(LOW)


def attend_backward(upper, packets, kept, wq, wk, wv, wo, gq, gk, cos_tab, sin_tab):
    count, lines, width = packets.shape
    rows, wide = (lines - LINES, wq.shape[1])
    blocks = (upper, packets) + tuple(kept)
    fixed = (wq, wk, wv, wo, gq, gk, cos_tab, sin_tab)
    sums = tuple(
        jax.ShapeDtypeStruct(shape, kind)
        for shape, kind in (
            ((width, 4 * wide), LOW), (gq.shape, WIDE), (gk.shape, WIDE), ((1, width), WIDE)
        )
    )
    return pl.pallas_call(
        attend_back_kernel,
        grid=(count,),
        in_specs=[first_spec(array) for array in blocks] + [whole_spec(array) for array in fixed],
        out_specs=[first_spec(upper)] + [whole_spec(array) for array in sums],
        out_shape=(jax.ShapeDtypeStruct((count, rows, width), LOW),) + sums,
        scratch_shapes=[pltpu.VMEM((width, 4 * wide), WIDE)],
        compiler_params=pltpu.CompilerParams(vmem_limit_bytes=VMEM_BYTES),
        cost_estimate=COST,
        name="attend_backward",
    )(*blocks, *fixed)


def slot_spots(table, expert):
    row_count = table.shape[1]
    slots = lax.broadcasted_iota(jnp.int32, (CAP, row_count), 0).astype(WIDE) + 1.0
    mine = lax.broadcasted_iota(jnp.int32, table.shape, 0) == expert
    ranks = jnp.sum(jnp.where(mine, table, 0.0), axis=0, keepdims=True)
    return (slots == ranks).astype(LOW)


class Trades:
    def __init__(self, trades):
        self.trades = trades
        self.axes = sorted({(axis, size) for _, axis, size, _ in trades})
        self.arrays = [array for array, _, _, _ in trades]
        self.in_specs = [pl.BlockSpec(memory_space=pltpu.VMEM) for _ in trades]
        self.out_specs = [pl.BlockSpec(memory_space=pl.ANY) for _ in trades]
        self.out_shapes = [
            jax.ShapeDtypeStruct(array.shape if pieces else (size,) + array.shape, array.dtype)
            for array, _, size, pieces in trades
        ]
        self.scratch = [
            pltpu.SemaphoreType.DMA((size,)) for _, _, size, _ in trades for _ in range(2)
        ]

    def bind(self, sources, targets, sems):
        self.sources, self.targets, self.sems = (sources, targets, sems)

    def device(self, axis, size, bits):
        return {axis: lax.rem(lax.axis_index(axis) + bits, size)}

    def copies(self):
        for number, (_, axis, size, pieces) in enumerate(self.trades):
            me = lax.axis_index(axis)
            send, recv = (self.sems[2 * number], self.sems[2 * number + 1])
            target = self.targets[number].at[me]
            for bits in range(size):
                source = self.sources[number]
                source = source.at[lax.rem(me + bits, size)] if pieces else source
                if bits == 0:
                    yield pltpu.make_async_copy(source, target, send.at[0])
                else:
                    yield pltpu.make_async_remote_copy(
                        source, target, send.at[bits], recv.at[bits],
                        device_id=self.device(axis, size, bits),
                        device_id_type=pl.DeviceIdType.MESH,
                    )

    def start(self):
        barrier = pltpu.get_barrier_semaphore()
        for axis, size in self.axes:
            for bits in range(1, size):
                pl.semaphore_signal(
                    barrier, inc=1, device_id=self.device(axis, size, bits),
                    device_id_type=pl.DeviceIdType.MESH,
                )
        pl.semaphore_wait(barrier, sum(size - 1 for _, size in self.axes))
        for copy in self.copies():
            copy.start()

    def finish(self):
        for copy in self.copies():
            copy.wait()


UNIT = 2


def expert_block(expert, rows_in, cots_in, wg, wu, wd, wr, x_ref, y_ref, m_ref, dg_ref, du_ref):
    row_count, hidden = (rows_in[0].shape[0], wg.shape[-1])
    for seq, (rows, cots) in enumerate(zip(rows_in, cots_in)):
        spots = slot_spots(cots[row_count:, :row_count].astype(WIDE), expert)
        span = pl.ds(seq * CAP, CAP)
        x_ref[span] = dot_nn(spots, rows[...]).astype(LOW)
        y_ref[span] = dot_nn(spots, cots[:row_count]).astype(LOW)
    x_all, y_all = (x_ref[...], y_ref[...])
    logits = dot_nn(x_all, wr[...])
    expo = jnp.exp(logits - jnp.max(logits, axis=-1, keepdims=True))
    chosen = lax.broadcasted_iota(jnp.int32, expo.shape, 1) == expert
    gates = jnp.sum(jnp.where(chosen, expo, 0.0), axis=-1, keepdims=True) / jnp.sum(
        expo, axis=-1, keepdims=True
    )
    step = min(256, hidden)
    dgate = jnp.zeros((x_all.shape[0], 1), WIDE)
    for start in range(0, hidden, step):
        span = slice(start, start + step)
        gate_act, up_act = (dot_nn(x_all, wg[:, span]), dot_nn(x_all, wu[:, span]))
        plain_grad = dot_nt(y_all, wd[span, :])
        sig = jax.nn.sigmoid(gate_act)
        silu = gate_act * sig
        joined = silu * up_act
        dgate += jnp.sum(joined * plain_grad, axis=-1, keepdims=True)
        grad = plain_grad * gates
        m_ref[:, span] = (joined * gates).astype(LOW)
        dg_ref[:, span] = (grad * up_act * (sig + silu * (1.0 - sig))).astype(LOW)
        du_ref[:, span] = (grad * silu).astype(LOW)
    return dgate


def expert_kernel(row_spans, cot_spans, batch, trades, ex_ref, wg, wu, wd, wr, *refs):
    first, second = (len(row_spans), len(row_spans) + len(cot_spans))
    rows_in, cots_in = (refs[:first], refs[first:second])
    third, number = (second + len(trades.trades), len(trades.trades))
    x_ref, y_ref, m_ref, dg_ref, du_ref, dgate_ref = refs[third : third + 6]
    rows_buf, cots_buf, sems = refs[third + 6 + number : third + 9 + number]
    trades.bind(refs[second:third], refs[third + 6 : third + 6 + number], refs[third + 9 + number :])
    steps, units = (sum(count for _, count in row_spans) // batch, batch // UNIT)
    turn = pl.program_id(0) * steps + pl.program_id(1)
    slot = lax.rem(turn, 2)
    row_count = rows_buf.shape[2]

    def copy(kind, source, offset, place, part):
        buffer = (rows_buf, cots_buf)[kind]
        return pltpu.make_async_copy(
            source.at[pl.ds(offset, UNIT)],
            buffer.at[place, pl.ds(part * UNIT, UNIT)],
            sems.at[kind, place, part],
        )

    def fetch(step, place):
        for part in range(units):
            unit = step * units + part
            for kind, sources, spans in ((0, rows_in, row_spans), (1, cots_in, cot_spans)):
                begin = 0
                for source, (offset, count) in zip(sources, spans):
                    size = count // UNIT

                    @pl.when((unit >= begin) & (unit < begin + size))
                    def _(source=source, begin=begin, offset=offset):
                        copy(kind, source, offset + (unit - begin) * UNIT, place, part).start()

                    begin += size

    @pl.when(turn == 0)
    def _():
        fetch(turn, slot)
        if number:
            trades.start()

    @pl.when(turn + 1 < pl.num_programs(0) * steps)
    def _():
        fetch(lax.rem(turn + 1, steps), 1 - slot)

    for part in range(units):
        copy(0, rows_in[0], 0, slot, part).wait()
        copy(1, cots_in[0], 0, slot, part).wait()
    dgate = expert_block(
        ex_ref[pl.program_id(0)],
        [rows_buf.at[slot, seq] for seq in range(batch)],
        [cots_buf.at[slot, seq] for seq in range(batch)],
        wg.at[0], wu.at[0], wd.at[0], wr,
        x_ref.at[0], y_ref.at[0], m_ref.at[0], dg_ref.at[0], du_ref.at[0],
    )
    dgate_ref[0] = jnp.broadcast_to(dgate, dgate_ref.shape[1:])
    if number:

        @pl.when(turn == pl.num_programs(0) * steps - 1)
        def _():
            trades.finish()


def expert_acts(ids, rows, cots, wg, wu, wd, wr, batch=4, trades=(), collective=None):
    trades = Trades(trades)
    row_spans, cot_spans = ([span for _, span in items] for items in (rows, cots))
    rows, cots = ([array for array, _ in items] for items in (rows, cots))
    count = sum(size for _, size in row_spans)
    width = rows[0].shape[2]
    own, _, hidden = wg.shape
    out_rows = batch * CAP

    def acts(cols, kind=LOW):
        return jax.ShapeDtypeStruct((own, count * CAP, cols), kind)

    def act_spec(cols):
        return pl.BlockSpec((1, out_rows, cols), lambda e, i: (e, i, 0))

    def weight_spec(array):
        return pl.BlockSpec(
            (1,) + array.shape[1:], lambda e, i: (e, 0, 0), pipeline_mode=pl.Buffered(1)
        )

    any_spec = pl.BlockSpec(memory_space=pl.ANY)
    columns = (width, width, hidden, hidden, hidden, 128)
    return pl.pallas_call(
        functools.partial(expert_kernel, row_spans, cot_spans, batch, trades),
        grid=(own, count // batch),
        in_specs=[
            pl.BlockSpec(memory_space=pltpu.SMEM),
            weight_spec(wg),
            weight_spec(wu),
            weight_spec(wd),
            pl.BlockSpec(wr.shape, lambda e, i: (0, 0)),
        ]
        + [any_spec] * (len(rows) + len(cots))
        + trades.in_specs,
        out_specs=[act_spec(cols) for cols in columns] + trades.out_specs,
        out_shape=[acts(cols) for cols in columns[:5]] + [acts(128, WIDE)] + trades.out_shapes,
        scratch_shapes=[
            pltpu.VMEM((2, batch) + rows[0].shape[1:], LOW),
            pltpu.VMEM((2, batch) + cots[0].shape[1:], LOW),
            pltpu.SemaphoreType.DMA((2, 2, batch // UNIT)),
        ]
        + trades.scratch,
        compiler_params=pltpu.CompilerParams(
            vmem_limit_bytes=VMEM_BYTES,
            collective_id=collective,
            has_side_effects=collective is not None,
        ),
        cost_estimate=COST,
        name="expert_acts",
    )(ids, wg, wu, wd, wr, *rows, *cots, *trades.arrays)


def pull_block(experts, rows, table, backs, dgates, wr):
    logits = dot_nn(rows, wr[...])
    expo = jnp.exp(logits - jnp.max(logits, axis=-1, keepdims=True))
    probs = expo / jnp.sum(expo, axis=-1, keepdims=True)
    columns = lax.broadcasted_iota(jnp.int32, probs.shape, 1)
    grad_logits = jnp.zeros_like(probs)
    total = jnp.zeros(rows.shape, WIDE)
    for expert, back, dgate in zip(experts, backs, dgates):
        spots = slot_spots(table, expert)
        total += dot_tn(spots, back)
        high = dgate.astype(LOW)
        rest = (dgate - high.astype(WIDE)).astype(LOW)
        at_rows = (dot_tn(spots, high) + dot_tn(spots, rest))[:, : probs.shape[1]]
        chosen = (columns == expert).astype(WIDE)
        prob = jnp.sum(probs * chosen, axis=-1, keepdims=True)
        grad_logits += at_rows * prob * (chosen - probs)
    low_logits = grad_logits.astype(LOW)
    return (total + dot_nt(low_logits, wr[...])).astype(LOW), dot_tn(low_logits, rows)


def pull_kernel(ex_ref, rows_ref, cot_ref, dg_ref, du_ref, dgate_ref, wg, wu, wr, part_ref, router):
    batch, row_count, _ = rows_ref.shape
    own = wg.shape[0]

    @pl.when(pl.program_id(0) == 0)
    def _():
        router[...] = jnp.zeros_like(router)

    backs = [
        (dot_nt(dg_ref[e], wg[e]) + dot_nt(du_ref[e], wu[e])).astype(LOW) for e in range(own)
    ]
    for seq in range(batch):
        span = slice(seq * CAP, (seq + 1) * CAP)
        part_ref[seq], router_part = pull_block(
            [ex_ref[e] for e in range(own)],
            rows_ref[seq],
            cot_ref[seq, :, :row_count].astype(WIDE),
            [back[span] for back in backs],
            [dgate_ref[e, span] for e in range(own)],
            wr,
        )
        router[...] += router_part


def mix_kernel(ex_ref, cot_ref, m_ref, wd, part_ref):
    batch, row_count, _ = part_ref.shape
    own = wd.shape[0]
    outs = [dot_nn(m_ref[e], wd[e]).astype(LOW) for e in range(own)]
    for seq in range(batch):
        table = cot_ref[seq, :, :row_count].astype(WIDE)
        span = slice(seq * CAP, (seq + 1) * CAP)
        total = sum(dot_tn(slot_spots(table, ex_ref[e]), outs[e][span]) for e in range(own))
        part_ref[seq] = total.astype(LOW)


def spread_call(kernel, name, ids, by_seq, cots, by_slot, fixed, router_shape, batch=2):
    count, lines, width = cots.shape
    row_count = lines - LINES
    part = jax.ShapeDtypeStruct((count, row_count, width), LOW)

    def seq_spec(array):
        return pl.BlockSpec((batch,) + array.shape[1:], lambda i: (i, 0, 0))

    def slot_spec(array):
        return pl.BlockSpec((array.shape[0], batch * CAP, array.shape[2]), lambda i: (0, i, 0))

    return pl.pallas_call(
        kernel,
        grid=(count // batch,),
        in_specs=[pl.BlockSpec(memory_space=pltpu.SMEM)]
        + [seq_spec(array) for array in by_seq]
        + [pl.BlockSpec((batch, LINES, width), lambda i: (i, row_count // LINES, 0))]
        + [slot_spec(array) for array in by_slot]
        + [whole_spec(array) for array in fixed],
        out_specs=[seq_spec(part)] + [whole_spec(shape) for shape in router_shape],
        out_shape=[part] + list(router_shape),
        compiler_params=pltpu.CompilerParams(vmem_limit_bytes=VMEM_BYTES),
        cost_estimate=COST,
        name=name,
    )(ids, *by_seq, cots, *by_slot, *fixed)


def weight_grad(lefts, rights, start=None):
    own, _, left_cols = lefts[0].shape
    right_cols = rights[0].shape[-1]
    sets = len(lefts)
    left_tile, right_tile = (min(512, left_cols), min(1024, right_cols))

    def kernel(*refs):
        total = sum(dot_tn(refs[i][0], refs[sets + i][0]) for i in range(sets))
        refs[-1][0] = total if start is None else total + refs[2 * sets][0]

    out_spec = pl.BlockSpec((1, left_tile, right_tile), lambda e, r, l: (e, l, r))
    return pl.pallas_call(
        kernel,
        grid=(own, right_cols // right_tile, left_cols // left_tile),
        in_specs=[
            pl.BlockSpec((1, array.shape[1], left_tile), lambda e, r, l: (e, 0, l))
            for array in lefts
        ]
        + [
            pl.BlockSpec((1, array.shape[1], right_tile), lambda e, r, l: (e, 0, r))
            for array in rights
        ]
        + [out_spec] * (start is not None),
        out_specs=out_spec,
        out_shape=jax.ShapeDtypeStruct((own, left_cols, right_cols), WIDE),
        input_output_aliases={} if start is None else {2 * sets: 0},
        compiler_params=pltpu.CompilerParams(vmem_limit_bytes=VMEM_BYTES),
        cost_estimate=COST,
        name="weight_grad",
    )(*lefts, *rights, *([] if start is None else [start]))


CHUNKS = 4
NEAR_LINES = 128


def each(size, body):
    def step(i, carry):
        body(i)
        return carry

    lax.fori_loop(0, size, step, 0)


def remote(source, target, send, recv, device):
    return pltpu.make_async_remote_copy(
        source, target, send, recv, device_id=device, device_id_type=pl.DeviceIdType.MESH
    )


class Links:
    def __init__(self, replicas, groups):
        rep, shard = (lax.axis_index("rep"), lax.axis_index("shard"))
        self.rail = groups // 2
        self.last = self.rail - 1
        self.shard, self.place, self.core = (shard, shard // 2, shard % 2)
        self.right, self.left = ((rep, shard + 2), (rep, shard - 2))
        self.partner = (rep, shard + 1 - 2 * self.core)
        self.over_x = (rep + 1 - 2 * (rep % 2), shard)
        self.over_y = ((rep + 2) % replicas, shard)

    def greet(self, others):
        barrier = pltpu.get_barrier_semaphore()

        def signal(device):
            pl.semaphore_signal(
                barrier, inc=1, device_id=device, device_id_type=pl.DeviceIdType.MESH
            )

        for device in others:
            signal(device)
        pl.when(self.place < self.last)(lambda: signal(self.right))
        pl.when(self.place > 0)(lambda: signal(self.left))
        inner = (self.place > 0) & (self.place < self.last)
        pl.when(inner)(lambda: pl.semaphore_wait(barrier, len(others) + 2))
        pl.when(jnp.logical_not(inner))(lambda: pl.semaphore_wait(barrier, len(others) + 1))


class Flood:
    def __init__(self, links, view, send, recv, pair, own):
        self.links, self.view, self.own = (links, view, own)
        self.send, self.recv, self.pair = (send, recv, pair)

    def copy(self, way, q, own=False):
        links = self.links
        slot = 2 * q + links.core
        source = self.own if own else self.view.at[slot]
        recv = self.pair.at[q] if way == 2 else self.recv.at[q]
        device = (links.right, links.left, links.partner)[way]
        return remote(source, self.view.at[slot], self.send.at[way, q], recv, device)

    def start(self):
        place = self.links.place

        @pl.when(place < self.links.last)
        def _():
            self.copy(0, place, True).start()

        @pl.when(place > 0)
        def _():
            self.copy(1, place, True).start()

        self.copy(2, place, True).start()

    def onward(self, d, more=None):
        place, last = (self.links.place, self.links.last)

        @pl.when((d > 0) & (place - d >= 0))
        def _():
            q = place - d
            self.copy(0, q).wait_recv()

            @pl.when(place < last)
            def _():
                self.copy(0, q).start()

            self.copy(2, q).start()
            if more is not None:
                more(q)

        @pl.when((d > 0) & (place + d <= last))
        def _():
            q = place + d
            self.copy(1, q).wait_recv()

            @pl.when(place > 0)
            def _():
                self.copy(1, q).start()

            self.copy(2, q).start()
            if more is not None:
                more(q)

    def wait_pair(self, q):
        slot = self.view.at[2 * q + 1 - self.links.core]
        remote(slot, slot, self.send.at[2, q], self.pair.at[q], self.links.partner).wait_recv()

    def finish(self, q):
        place = self.links.place

        @pl.when((place < self.links.last) & (q <= place))
        def _():
            self.copy(0, q).wait_send()

        @pl.when((place > 0) & (q >= place))
        def _():
            self.copy(1, q).wait_send()

        self.copy(2, q).wait_send()


def front_kernel(
    replicas, groups,
    packet, tokens, wq, wk, wv, wo, gq, gk, cos_ref, sin_ref, gain_ref,
    packets, qr_ref, kr_ref, v_ref, o_ref, hidden, low,
    nb, mine, pair_out, pair_in, line_r, line_l,
    n1_send, n1_recv, n1_pair, po_send, po_recv, lr_send, lr_recv, ll_send, ll_recv, keep_sem, own_sem,
):
    links = Links(replicas, groups)
    rail, last, place, core = (links.rail, links.last, links.place, links.core)
    rows = tokens.shape[0]
    step_rows = rows // CHUNKS
    flood = Flood(links, nb, n1_send, n1_recv, n1_pair, packet)
    links.greet([links.partner])
    flood.start()
    own_block = pltpu.make_async_copy(packet, nb.at[links.shard], own_sem.at[0])
    own_block.start()
    own_block.wait()

    def partial_out(q):
        return remote(pair_out.at[q], pair_in.at[q], po_send.at[q], po_recv.at[q], links.partner)

    def chunk_span(chunk):
        return pl.ds(pl.multiple_of(chunk * step_rows, step_rows), step_rows)

    def line(q, chunk, to_right):
        span = chunk_span(chunk)
        target, send, recv, device = (
            (line_r, lr_send, lr_recv, links.right)
            if to_right
            else (line_l, ll_send, ll_recv, links.left)
        )
        return remote(
            mine.at[q, span], target.at[q, span], send.at[q, chunk], recv.at[q, chunk], device
        )

    def add_up(q, chunk, extras):
        span = chunk_span(chunk)
        total = mine[q, span].astype(WIDE) + pair_in[q, span].astype(WIDE)
        for extra in extras:
            total = total + extra[q, span].astype(WIDE)
        return total

    def forward_line(q, to_right, first):
        partial_out(q).wait_recv()

        def body(chunk):
            extras = []
            if not first:
                line(q, chunk, to_right).wait_recv()
                extras = [line_r if to_right else line_l]
            mine[q, chunk_span(chunk)] = add_up(q, chunk, extras).astype(LOW)
            line(q, chunk, to_right).start()

        each(CHUNKS, body)

    def keep_copy(slot):
        return pltpu.make_async_copy(nb.at[slot], packets.at[slot], keep_sem.at[slot])

    def one_distance(d):
        flood.onward(d)

        def one_block(k):
            side, other = (k % 2, k // 2)
            q = place + (2 * side - 1) * d

            @pl.when((q >= 0) & (q <= last) & ((d > 0) | (side == 0)))
            def _():
                @pl.when(other == 1)
                def _():
                    flood.wait_pair(q)

                slot = 2 * q + core + other * (1 - 2 * core)
                keep_copy(slot).start()
                length = nb[slot, rows:, rows : rows + 128].astype(WIDE)[0:1, 0:1]

                def keep(query_raw, key_raw, value, joined):
                    qr_ref[slot], kr_ref[slot] = (query_raw, key_raw)
                    v_ref[slot], o_ref[slot] = (value, joined)

                part = attend_block(
                    nb[slot, :rows], length, wq, wk, wv, wo, gq[...], gk[...],
                    cos_ref[...], sin_ref[...], keep,
                )

                @pl.when(other == 0)
                def _():
                    mine[q] = part

                @pl.when(other == 1)
                def _():
                    pair_out[q] = part
                    partial_out(q).start()

        each(4, one_block)

        @pl.when((place == 0) & (d > 0))
        def _():
            forward_line(d, True, True)

        @pl.when((place == last) & (d > 0))
        def _():
            forward_line(last - d, False, True)

    each(rail, one_distance)

    def rest_right():
        def body(j):
            @pl.when((place > 0) & (place + j <= last))
            def _():
                forward_line(place + j, True, False)

        each(last, lambda i: body(i + 1))

    def rest_left():
        def body(j):
            @pl.when((place < last) & (place - j >= 0))
            def _():
                forward_line(place - j, False, False)

        each(last, lambda i: body(i + 1))

    near_end = place < rail // 2
    pl.when(near_end)(rest_right)
    pl.when(jnp.logical_not(near_end))(rest_left)
    pl.when(near_end)(rest_left)
    pl.when(jnp.logical_not(near_end))(rest_right)
    partial_out(place).wait_recv()

    def finish_rows(chunk):
        @pl.when(place > 0)
        def _():
            line(place, chunk, True).wait_recv()

        @pl.when(place < last)
        def _():
            line(place, chunk, False).wait_recv()

        span = chunk_span(chunk)
        total = tokens[span].astype(WIDE) + add_up(place, chunk, [])
        from_left = jnp.where(place > 0, line_r[place, span].astype(WIDE), 0.0)
        from_right = jnp.where(place < last, line_l[place, span].astype(WIDE), 0.0)
        total = total + from_left + from_right
        hidden[span] = total
        scale = lax.rsqrt(jnp.mean(total * total, axis=-1, keepdims=True) + EPS_NORM)
        low[span] = (total * scale * gain_ref[...]).astype(LOW)

    each(CHUNKS, finish_rows)

    def settle(q):
        flood.finish(q)
        keep_copy(2 * q).wait()
        keep_copy(2 * q + 1).wait()
        partial_out(q).wait_send()

        def chunk_sends(chunk):
            @pl.when((place < last) & (q > place))
            def _():
                line(q, chunk, True).wait_send()

            @pl.when((place > 0) & (q < place))
            def _():
                line(q, chunk, False).wait_send()

        each(CHUNKS, chunk_sends)

    each(rail, settle)


ANY_SPEC = pl.BlockSpec(memory_space=pl.ANY)
FAST_SPEC = pl.BlockSpec(memory_space=pltpu.VMEM)


def shape(*dims, kind=LOW):
    return jax.ShapeDtypeStruct(dims, kind)


def front(replicas, groups, packet, tokens, wq, wk, wv, wo, gq, gk, cos_tab, sin_tab, gain):
    lines, width = packet.shape
    rows, wide, rail = (tokens.shape[0], wq.shape[1], groups // 2)
    block = pltpu.VMEM((rail, rows, width), LOW)
    dma = pltpu.SemaphoreType.DMA
    return pl.pallas_call(
        functools.partial(front_kernel, replicas, groups),
        in_specs=[ANY_SPEC] + [FAST_SPEC] * 10,
        out_specs=[ANY_SPEC] + [FAST_SPEC] * 6,
        out_shape=[
            shape(groups, lines, width),
            shape(groups, rows, wide, kind=WIDE),
            shape(groups, rows, wide, kind=WIDE),
            shape(groups, rows, wide),
            shape(groups, rows, wide),
            shape(rows, width, kind=WIDE),
            shape(rows, width),
        ],
        scratch_shapes=[pltpu.VMEM((groups, lines, width), LOW), block, block, block, block, block]
        + [dma((3, rail)), dma((rail,)), dma((rail,))]
        + [dma((rail,))] * 2
        + [dma((rail, CHUNKS))] * 4
        + [dma((groups,)), dma((1,))],
        compiler_params=pltpu.CompilerParams(
            vmem_limit_bytes=VMEM_BYTES, collective_id=0, has_side_effects=True
        ),
        cost_estimate=COST,
        name="front",
    )(packet, tokens, wq, wk, wv, wo, gq, gk, cos_tab, sin_tab, gain)


def moe_kernel(
    replicas, groups,
    ex_ref, low, cot, wg_in, wu_in, wd_in, wr,
    rows_all, cots, fx, fy, fd, px, py, pd, x_out, y_out, m_out, dg_out, du_out, part_out, router,
    wg, wu, wd, rows_buf, cots_buf, x_s, y_s, m_s, dg_s, du_s, part_s,
    n2_send, n2_recv, n2_pair, cz_send, cz_recv, cz_pair,
    xy_send, xy_recv, dg_send, dg_recv, fl_send, fl_recv, own_sem, load_sem, out_sem, part_sem,
):
    links = Links(replicas, groups)
    rail, last, place, core = (links.rail, links.last, links.place, links.core)
    own, row_count = (wg.shape[0], low.shape[0])
    flood_n2 = Flood(links, rows_all, n2_send, n2_recv, n2_pair, low)
    flood_cot = Flood(links, cots, cz_send, cz_recv, cz_pair, cot)

    def cross(way, q, own_block=False):
        source = cot if own_block else cots.at[2 * q + core]
        target, device = ((fx, links.over_x), (fy, links.over_y))[way]
        return remote(source, target.at[q], xy_send.at[way, q], xy_recv.at[way, q], device)

    def cross_both(q):
        cross(0, q).start()
        cross(1, q).start()

    def diagonal(way, q):
        source, device = ((fx, links.over_y), (fy, links.over_x))[way]
        span = (pl.ds(0, NEAR_LINES), pl.ds(NEAR_LINES, cot.shape[0] - NEAR_LINES))[way]
        return remote(
            source.at[q, span], fd.at[q, span], dg_send.at[way, q], dg_recv.at[way, q], device
        )

    def flip(which, q):
        source, target = ((fx, px), (fy, py), (fd, pd))[which]
        return remote(
            source.at[q], target.at[q], fl_send.at[which, q], fl_recv.at[which, q], links.partner
        )

    def at_distance(d, body):
        @pl.when((d >= 0) & (place - d >= 0))
        def _():
            body(place - d)

        @pl.when((d > 0) & (place + d <= last))
        def _():
            body(place + d)

    def take_cross(q):
        for way in (0, 1):
            cross(way, q).wait_recv()
            diagonal(way, q).start()
            flip(way, q).start()

    def take_diagonal(q):
        for way in (0, 1):
            diagonal(way, q).wait_recv()
        flip(2, q).start()

    links.greet([links.partner, links.over_x, links.over_y])
    flood_cot.start()
    flood_n2.start()
    cross(0, place, True).start()
    cross(1, place, True).start()
    own_copies = (
        pltpu.make_async_copy(low, rows_all.at[links.shard], own_sem.at[0]),
        pltpu.make_async_copy(cot, cots.at[links.shard], own_sem.at[1]),
        pltpu.make_async_copy(wg_in, wg, own_sem.at[2]),
        pltpu.make_async_copy(wu_in, wu, own_sem.at[3]),
        pltpu.make_async_copy(wd_in, wd, own_sem.at[4]),
    )
    for copy in own_copies:
        copy.start()
    router[...] = jnp.zeros_like(router)
    for copy in own_copies:
        copy.wait()

    def out_copies(q):
        span = pl.ds(2 * q * CAP, 2 * CAP)
        pairs = ((x_s, x_out), (y_s, y_out), (m_s, m_out), (dg_s, dg_out), (du_s, du_out))
        return [
            pltpu.make_async_copy(source.at[e], target.at[e, span], out_sem.at[e, i])
            for e in range(own)
            for i, (source, target) in enumerate(pairs)
        ]

    def part_copy(q):
        return pltpu.make_async_copy(part_s, part_out.at[pl.ds(2 * q, 2)], part_sem.at[0])

    near = jnp.where(place <= last - place, place, last - place)
    far_sign = jnp.where(place <= last - place, 1, -1)

    def one_step(k):
        flood_cot.onward(k, cross_both)
        flood_n2.onward(k)
        at_distance(k - 1, take_cross)
        at_distance(k - 2, take_diagonal)
        within = k <= 2 * near
        sign = jnp.where(within & (k % 2 == 1), -far_sign, far_sign)
        q = place + sign * jnp.where(within, (k + 1) // 2, k - near)
        flood_cot.wait_pair(q)
        flood_n2.wait_pair(q)
        loads = (
            pltpu.make_async_copy(rows_all.at[pl.ds(2 * q, 2)], rows_buf, load_sem.at[0]),
            pltpu.make_async_copy(cots.at[pl.ds(2 * q, 2)], cots_buf, load_sem.at[1]),
        )
        for copy in loads:
            copy.start()

        @pl.when(k > 0)
        def _():
            for copy in out_copies(0):
                copy.wait()
            part_copy(0).wait()

        for copy in loads:
            copy.wait()
        dgates, backs = ([], [])
        for e in range(own):
            dgate = expert_block(
                ex_ref[e],
                [rows_buf.at[seq] for seq in range(2)],
                [cots_buf.at[seq] for seq in range(2)],
                wg.at[e], wu.at[e], wd.at[e], wr,
                x_s.at[e], y_s.at[e], m_s.at[e], dg_s.at[e], du_s.at[e],
            )
            dgates.append(jnp.broadcast_to(dgate, (dgate.shape[0], 128)))
            backs.append((dot_nt(dg_s[e], wg[e]) + dot_nt(du_s[e], wu[e])).astype(LOW))
        for copy in out_copies(q):
            copy.start()
        for seq in range(2):
            span = slice(seq * CAP, (seq + 1) * CAP)
            part_s[seq], router_part = pull_block(
                [ex_ref[e] for e in range(own)],
                rows_buf[seq],
                cots_buf[seq, row_count:, :row_count].astype(WIDE),
                [back[span] for back in backs],
                [dgate[span] for dgate in dgates],
                wr,
            )
            router[...] += router_part
        part_copy(q).start()

    each(rail, one_step)
    at_distance(last, take_cross)
    at_distance(last - 1, take_diagonal)
    at_distance(last, take_diagonal)
    for copy in out_copies(0):
        copy.wait()
    part_copy(0).wait()

    def settle(q):
        flood_n2.finish(q)
        flood_cot.finish(q)
        for way in (0, 1):
            cross(way, q).wait_send()
            diagonal(way, q).wait_send()
        for which in (0, 1, 2):
            flip(which, q).wait_send()
            flip(which, q).wait_recv()

    each(rail, settle)


def moe(replicas, groups, ids, low, cot, wg, wu, wd, wr):
    lines, width = cot.shape
    rows, rail = (low.shape[0], groups // 2)
    own, _, hidden = wg.shape
    pair = 2 * CAP
    dma, vmem = (pltpu.SemaphoreType.DMA, pltpu.VMEM)
    acts = [shape(own, groups * CAP, cols) for cols in (width, width, hidden, hidden, hidden)]
    return pl.pallas_call(
        functools.partial(moe_kernel, replicas, groups),
        in_specs=[pl.BlockSpec(memory_space=pltpu.SMEM)]
        + [FAST_SPEC] * 2
        + [ANY_SPEC] * 3
        + [FAST_SPEC],
        out_specs=[ANY_SPEC] * 14 + [FAST_SPEC],
        out_shape=[shape(groups, rows, width), shape(groups, lines, width)]
        + [shape(rail, lines, width)] * 6
        + acts
        + [shape(groups, rows, width), shape(wr.shape[1], width, kind=WIDE)],
        scratch_shapes=[vmem(array.shape, LOW) for array in (wg, wu, wd)]
        + [vmem((2, rows, width), LOW), vmem((2, lines, width), LOW)]
        + [vmem((own, pair, cols), LOW) for cols in (width, width, hidden, hidden, hidden)]
        + [vmem((2, rows, width), LOW)]
        + [dma((3, rail)), dma((rail,)), dma((rail,))] * 2
        + [dma((2, rail))] * 4
        + [dma((3, rail))] * 2
        + [dma((5,)), dma((2,)), dma((own, 5)), dma((1,))],
        compiler_params=pltpu.CompilerParams(
            vmem_limit_bytes=VMEM_BYTES, collective_id=3, has_side_effects=True
        ),
        cost_estimate=COST,
        name="moe",
    )(ids, low, cot, wg, wu, wd, wr)


def rms_parts(values):
    scale = lax.rsqrt(jnp.mean(values * values, axis=-1, keepdims=True) + EPS_NORM)
    return (values * scale, scale)


def rms_back(plain, scale, gain, grad):
    back = grad * gain
    return scale * (back - plain * jnp.mean(back * plain, axis=-1, keepdims=True))


def local(
    tokens, lengths, routes, gain_attn, gain_query, gain_key,
    w_query, w_key, w_value, w_out, gain_moe, w_router,
    w_gate, w_up, w_down, out_grad,
):
    row_count, width = tokens.shape
    head_dim = gain_query.shape[0]
    groups, replicas = (lax.axis_size("shard"), lax.axis_size("rep"))
    expert_count, own = (w_router.shape[1], w_gate.shape[0])
    wide = w_query.shape[1]
    after = lax.optimization_barrier
    gain_q, gain_k = (gain_query.reshape(1, -1), gain_key.reshape(1, -1))
    cos_tab, sin_tab = rope_tables(row_count, head_dim)
    ids = lax.axis_index("shard") * own + jnp.arange(own, dtype=jnp.int32)

    def flip_replica(values, bits):
        return lax.ppermute(values, "rep", [(i, i ^ bits) for i in range(replicas)])

    def flip_shard(values, bits):
        return lax.ppermute(values, "shard", [(i, i ^ bits) for i in range(groups)])

    def scatter_sum(parts):
        return lax.psum_scatter(
            parts.reshape(-1, width), "shard", scatter_dimension=0, tiled=True
        ).astype(WIDE)

    experts = (w_gate, w_up, w_down, w_router)

    def whole(*arrays):
        return [(array, (0, array.shape[0])) for array in arrays]

    def add_grads(acts, grads=None):
        return [
            weight_grad(
                [act[left] for act in acts],
                [act[right] for act in acts],
                None if grads is None else grads[number],
            )
            for number, (left, right) in enumerate(((0, 3), (0, 4), (2, 1)))
        ]

    inputs = tokens.astype(WIDE)
    row_mask = (jnp.arange(row_count, dtype=jnp.int32) < lengths[0])[:, None]
    named = jnp.any(
        routes[None, :, :] == jnp.arange(expert_count, dtype=jnp.int32)[:, None, None], axis=-1
    )
    upto = (jnp.arange(row_count)[:, None] <= jnp.arange(row_count)[None, :]).astype(LOW)
    ranks = jnp.where(named, dot_nn(named.astype(LOW), upto), 0.0).astype(LOW)
    lines = jnp.concatenate(
        [ranks, jnp.broadcast_to(lengths[0].astype(LOW), (expert_count, width - row_count))], axis=1
    )
    plain_in, scale_in = rms_parts(inputs)
    packet = jnp.concatenate([(plain_in * gain_attn).astype(LOW), lines], axis=0)
    cot_low = jnp.where(row_mask, out_grad, 0.0)
    cot_packet = jnp.concatenate([cot_low, lines], axis=0)
    heads = (w_query, w_key, w_value, w_out, gain_q, gain_k, cos_tab, sin_tab)
    share = replicas == 4 and groups == 8
    if share:
        packets, *kept, hidden, low = front(
            replicas, groups, packet, tokens, *heads, gain_moe.reshape(1, -1)
        )
        rows_all, cots, *found = moe(
            replicas, groups, ids, low, cot_packet, w_gate, w_up, w_down, w_router
        )
        far_cots, acts, (pull_part, grad_router) = (found[:6], [found[6:11]], found[11:])
        gated = acts[0][2]
        pairs = rows_all.reshape((groups // 2, 2) + rows_all.shape[1:])
        core = lax.axis_index("shard") % 2
        near = [
            lax.dynamic_slice(pairs, (start, core, 0, 0), (2, 1) + pairs.shape[2:])[:, 0]
            for start in (0, 2)
        ]
        early, late = ([flip_replica(part, bits) for bits in (1, 2)] for part in near)
    else:
        packets = lax.all_gather(packet, "shard", axis=0)
        cot_packet, packets = after((cot_packet, packets))
        cots = lax.all_gather(cot_packet, "shard", axis=0)
        part, *kept = attend_forward(packets, *heads)
        hidden = inputs + scatter_sum(part)
        plain_mid, scale_mid = rms_parts(hidden)
        rows_all = lax.all_gather((plain_mid * gain_moe).astype(LOW), "shard", axis=0)

        acts = [expert_acts(ids, whole(rows_all), whole(cots), *experts)]
        _, _, gated, grad_gate_act, grad_up_act, dgates = acts[0]
        pull_part, grad_router = spread_call(
            pull_kernel, "expert_pull", ids, (rows_all,), cots,
            (grad_gate_act, grad_up_act, dgates), (w_gate, w_up, w_router),
            (jax.ShapeDtypeStruct(w_router.shape[::-1], WIDE),),
        )
    grad_moe_in = scatter_sum(pull_part)
    gated, pull_part = after((gated, pull_part))
    (mix_part,) = spread_call(mix_kernel, "expert_mix", ids, (), cots, (gated,), (w_down,), ())
    if share:
        acts, mix_part = after((acts, mix_part))
        grads = add_grads(acts)
        grads, early = after((grads, early))
        acts = [
            expert_acts(
                ids, whole(*early), [(array, (0, 2)) for array in far_cots[:2]], *experts
            )
        ]
        early_flipped = [flip_shard(values, 1) for values in early]
        acts, late, early_flipped, grads = after((acts, late, early_flipped, grads))
        grad_moe_in, acts, grads = after((grad_moe_in, acts, grads))

    grad_out = cot_low.astype(WIDE)
    if share:
        hidden, grad_moe_in = after((hidden, grad_moe_in))
        plain_mid, scale_mid = rms_parts(hidden)
    grad_hidden = grad_out + rms_back(plain_mid, scale_mid, gain_moe, grad_moe_in)
    gain_moe_sum = jnp.sum(grad_moe_in * plain_mid, axis=0)
    branch_low = grad_hidden.astype(LOW)
    upper = lax.all_gather(branch_low, "shard", axis=0)
    if share:
        late, acts, grads, branch_low = after((late, acts, grads, branch_low))
        diagonal = [flip_replica(early[0], 2), flip_replica(late[1], 1)]
        late_flipped = [flip_shard(values, 1) for values in late]
        acts.append(
            expert_acts(ids, whole(*late), [(array, (2, 2)) for array in far_cots[:2]], *experts)
        )
        grads = add_grads(acts, grads)
        upper, grads, diagonal, late_flipped = after((upper, grads, diagonal, late_flipped))
        diagonal_flipped = [flip_shard(values, 1) for values in diagonal]
        flipped = [early_flipped[0], late_flipped[0], early_flipped[1], late_flipped[1]]
    mix_part, upper = after((mix_part, upper))
    mixture = scatter_sum(mix_part)
    part, gw_low, sum_q, sum_k, sum_n = attend_backward(upper, packets, kept, *heads)

    small = jnp.concatenate(
        [
            grad_router,
            gain_moe_sum[None],
            sum_n / gain_attn,
            jnp.pad(
                jnp.concatenate([sum_q, sum_k], axis=1), ((0, 0), (0, width - 2 * head_dim))
            ),
            jnp.zeros((5, width), WIDE),
        ]
    )
    if share:
        part, gw_low, diagonal_flipped = after((part, gw_low, diagonal_flipped))
        pieces = gw_low.reshape((replicas, -1) + gw_low.shape[1:])
        *act, traded, smalls = expert_acts(
            ids, whole(*flipped), whole(*far_cots[3:5]), *experts,
            trades=((pieces, "rep", replicas, True), (small, "rep", replicas, False)), collective=1,
        )
        act, traded, smalls, part, mixture = after((act, traded, smalls, part, mixture))
        acts = [act]
        grad_normed = scatter_sum(part)
        low = jnp.sum(traded.astype(WIDE), axis=0).astype(LOW)
        small = jnp.sum(smalls, axis=0)
        *act, found, smalls = expert_acts(
            ids, whole(*diagonal, *diagonal_flipped), whole(far_cots[2], far_cots[5]), *experts,
            trades=((low, "rep", replicas, False), (small, "shard", groups, False)), collective=2,
        )
        acts.append(act)
        gw_sum = found.reshape(gw_low.shape)
        small = jnp.sum(smalls, axis=0)
        grad_gate_w, grad_up_w, grad_down = add_grads(acts, grads)
    else:
        grad_normed = scatter_sum(part)
        over_reps = lax.psum(
            (gw_low,) + tuple(values.astype(LOW) for values in add_grads(acts)),
            "rep",
        )
        gw_sum = over_reps[0]
        grad_gate_w, grad_up_w, grad_down = (values.astype(WIDE) for values in over_reps[1:])
        small = lax.psum(small, ("rep", "shard"))
    grads_q, grads_k, grads_v, grads_o = (
        gw_sum[:, i * wide : (i + 1) * wide].astype(WIDE) for i in range(4)
    )
    grad_router = small[:expert_count].T
    grad_gain_moe, grad_gain_attn = (small[expert_count], small[expert_count + 1])
    grad_gain_query, grad_gain_key = (
        small[expert_count + 2, i * head_dim : (i + 1) * head_dim] for i in range(2)
    )
    output = (hidden + mixture).astype(LOW)
    grad_input = grad_hidden + rms_back(plain_in, scale_in, gain_attn, grad_normed)
    return (
        output, grad_input, grad_gain_attn, grad_gain_query, grad_gain_key,
        grads_q, grads_k, grads_v, grads_o.T,
        grad_gain_moe, grad_router, grad_gate_w, grad_up_w, grad_down,
    )


def solution(mesh):
    rows, flat, cols = (P(("rep", "shard"), None), P(), P(None, "shard"))
    lead, experts = (P("shard", None), P("shard", None, None))
    return jax.shard_map(
        local,
        mesh=mesh,
        in_specs=(
            rows, P(("rep", "shard")), rows, flat, flat, flat, cols, cols, cols, lead,
            flat, flat, experts, experts, experts, rows,
        ),
        out_specs=(
            rows, rows, flat, flat, flat, cols, cols, cols, lead,
            flat, flat, experts, experts, experts,
        ),
        check_vma=False,
    )
```

```python
import functools
import math

import jax
import jax.numpy as jnp
from jax import lax
from jax.experimental import pallas as pl
from jax.experimental.pallas import tpu as pltpu
from jax.sharding import PartitionSpec as P

CAP = 144
LINES = 16
EPS_NORM = 1e-06
ROPE_BASE = 50000.0
MASKED = -1e30
VMEM_BYTES = 60 * 1024 * 1024
LOW = jnp.bfloat16
WIDE = jnp.float32
COST = pl.CostEstimate(flops=1 << 20, bytes_accessed=1 << 16, transcendentals=0)


def dot_nn(a, b):
    return lax.dot_general(a, b, (((1,), (0,)), ((), ())), preferred_element_type=WIDE)


def dot_nt(a, b):
    return lax.dot_general(a, b, (((1,), (1,)), ((), ())), preferred_element_type=WIDE)


def dot_tn(a, b):
    return lax.dot_general(a, b, (((0,), (0,)), ((), ())), preferred_element_type=WIDE)


def rope_tables(seq_len, head_dim):
    half_dim = head_dim // 2
    places = jnp.arange(seq_len, dtype=WIDE)
    freqs = ROPE_BASE ** (-jnp.arange(half_dim, dtype=WIDE) * (2.0 / head_dim))
    angles = places[:, None] * freqs[None, :]
    cosine, sine = (jnp.cos(angles), jnp.sin(angles))
    return (
        jnp.concatenate([cosine, cosine], axis=-1),
        jnp.concatenate([-sine, sine], axis=-1),
    )


def head_forward(raw, gain, cos_tab, sin_tab):
    scale = lax.rsqrt(jnp.mean(raw * raw, axis=-1, keepdims=True) + EPS_NORM)
    plain = raw * scale
    scaled = plain * gain
    turned = pltpu.roll(scaled, raw.shape[-1] // 2, axis=1)
    return (scaled * cos_tab + turned * sin_tab, plain, scale)


def head_backward(grad, plain, scale, gain, cos_tab, sin_tab):
    back = grad * cos_tab + pltpu.roll(grad * sin_tab, grad.shape[-1] // 2, axis=1)
    gain_grad = jnp.sum(back * plain, axis=0, keepdims=True)
    back = back * gain
    raw_grad = scale * (back - plain * jnp.mean(back * plain, axis=-1, keepdims=True))
    return (raw_grad, gain_grad)


def soft_weights(query, key, length, score_scale):
    scores = dot_nt(query, key) * score_scale
    places = lax.broadcasted_iota(jnp.int32, scores.shape, 1).astype(WIDE)
    scores = jnp.where(places < length, scores, MASKED)
    expo = jnp.exp(scores - jnp.max(scores, axis=-1, keepdims=True))
    return expo / jnp.sum(expo, axis=-1, keepdims=True)


def attend_block(normed, length, wq, wk, wv, wo, gq, gk, cos_tab, sin_tab, keep):
    head_dim = gq.shape[-1]
    query_raw, key_raw = (dot_nn(normed, wq[...]), dot_nn(normed, wk[...]))
    value = dot_nn(normed, wv[...]).astype(LOW)
    heads = []
    for head in range(query_raw.shape[-1] // head_dim):
        span = slice(head * head_dim, (head + 1) * head_dim)
        query = head_forward(query_raw[:, span], gq, cos_tab, sin_tab)[0].astype(LOW)
        key = head_forward(key_raw[:, span], gk, cos_tab, sin_tab)[0].astype(LOW)
        weights = soft_weights(query, key, length, head_dim**-0.5).astype(LOW)
        heads.append(dot_nn(weights, value[:, span]).astype(LOW))
    joined = heads[0] if len(heads) == 1 else jnp.concatenate(heads, axis=-1)
    keep(query_raw, key_raw, value, joined)
    return dot_nn(joined, wo[...]).astype(LOW)


def attend_kernel(
    pk_ref, wq, wk, wv, wo, gq, gk, cos_ref, sin_ref, part_ref, qr_ref, kr_ref, v_ref, o_ref
):
    rows = pk_ref.shape[1] - LINES
    length = pk_ref[0, rows:, rows : rows + 128].astype(WIDE)[0:1, 0:1]

    def keep(query_raw, key_raw, value, joined):
        qr_ref[0], kr_ref[0], v_ref[0], o_ref[0] = (query_raw, key_raw, value, joined)

    part_ref[0] = attend_block(
        pk_ref[0, :rows], length, wq, wk, wv, wo, gq[...], gk[...], cos_ref[...], sin_ref[...], keep
    )


def whole_spec(array):
    return pl.BlockSpec(array.shape, lambda *_: (0,) * array.ndim, pipeline_mode=pl.Buffered(1))


def first_spec(array):
    return pl.BlockSpec((1,) + array.shape[1:], lambda i: (i,) + (0,) * (array.ndim - 1))


def attend_forward(packets, wq, wk, wv, wo, gq, gk, cos_tab, sin_tab):
    count, lines, width = packets.shape
    rows, wide = (lines - LINES, wq.shape[1])
    fixed = (wq, wk, wv, wo, gq, gk, cos_tab, sin_tab)
    out = (
        jax.ShapeDtypeStruct((count, rows, width), LOW),
        jax.ShapeDtypeStruct((count, rows, wide), WIDE),
        jax.ShapeDtypeStruct((count, rows, wide), WIDE),
        jax.ShapeDtypeStruct((count, rows, wide), LOW),
        jax.ShapeDtypeStruct((count, rows, wide), LOW),
    )
    return pl.pallas_call(
        attend_kernel,
        grid=(count,),
        in_specs=[first_spec(packets)] + [whole_spec(array) for array in fixed],
        out_specs=[first_spec(array) for array in out],
        out_shape=out,
        compiler_params=pltpu.CompilerParams(vmem_limit_bytes=VMEM_BYTES),
        cost_estimate=COST,
        name="attend_forward",
    )(packets, *fixed)


def attend_back_kernel(
    da_ref, pk_ref, qr_ref, kr_ref, v_ref, o_ref,
    wq, wk, wv, wo, gq, gk, cos_ref, sin_ref,
    part_ref, gw_ref, gain_q, gain_k, gain_n, gw_sum,
):
    rows = pk_ref.shape[1] - LINES
    head_dim = gq.shape[-1]
    length = pk_ref[0, rows:, rows : rows + 128].astype(WIDE)[0:1, 0:1]
    cos_tab, sin_tab = (cos_ref[...], sin_ref[...])
    score_scale = head_dim**-0.5

    @pl.when(pl.program_id(0) == 0)
    def _():
        for ref in (gw_sum, gain_q, gain_k, gain_n):
            ref[...] = jnp.zeros_like(ref)

    upper = da_ref[0]
    grad_joined = dot_nt(upper, wo[...]).astype(LOW)
    wide = qr_ref.shape[-1]
    gw_sum[:, 3 * wide :] += dot_tn(upper, o_ref[0])
    grads_q, grads_k, grads_v = ([], [], [])
    for head in range(qr_ref.shape[-1] // head_dim):
        span = slice(head * head_dim, (head + 1) * head_dim)
        query, plain_q, scale_q = head_forward(qr_ref[0, :, span], gq[...], cos_tab, sin_tab)
        key, plain_k, scale_k = head_forward(kr_ref[0, :, span], gk[...], cos_tab, sin_tab)
        query, key, value = (query.astype(LOW), key.astype(LOW), v_ref[0, :, span])
        probs = soft_weights(query, key, length, score_scale)
        grad_out = grad_joined[:, span]
        grads_v.append(dot_tn(probs.astype(LOW), grad_out).astype(LOW))
        grad_probs = dot_nt(grad_out, value)
        inner = jnp.sum(probs * grad_probs, axis=-1, keepdims=True)
        grad_scores = (probs * (grad_probs - inner)).astype(LOW)
        grad_q, head_gain_q = head_backward(
            dot_nn(grad_scores, key) * score_scale, plain_q, scale_q, gq[...], cos_tab, sin_tab
        )
        grad_k, head_gain_k = head_backward(
            dot_tn(grad_scores, query) * score_scale, plain_k, scale_k, gk[...], cos_tab, sin_tab
        )
        gain_q[...] += head_gain_q
        gain_k[...] += head_gain_k
        grads_q.append(grad_q.astype(LOW))
        grads_k.append(grad_k.astype(LOW))
    grads = jnp.concatenate(grads_q + grads_k + grads_v, axis=-1)
    part = (
        dot_nt(grads[:, :wide], wq[...])
        + dot_nt(grads[:, wide : 2 * wide], wk[...])
        + dot_nt(grads[:, 2 * wide :], wv[...])
    )
    normed = pk_ref[0, :rows]
    part_ref[0] = part.astype(LOW)
    gain_n[...] += jnp.sum(part * normed.astype(WIDE), axis=0, keepdims=True)
    gw_sum[:, : 3 * wide] += dot_tn(normed, grads)

    @pl.when(pl.program_id(0) == pl.num_programs(0) - 1)
    def _():
        gw_ref[...] = gw_sum[...].astype(LOW)


def attend_backward(upper, packets, kept, wq, wk, wv, wo, gq, gk, cos_tab, sin_tab):
    count, lines, width = packets.shape
    rows, wide = (lines - LINES, wq.shape[1])
    blocks = (upper, packets) + tuple(kept)
    fixed = (wq, wk, wv, wo, gq, gk, cos_tab, sin_tab)
    sums = tuple(
        jax.ShapeDtypeStruct(shape, kind)
        for shape, kind in (
            ((width, 4 * wide), LOW), (gq.shape, WIDE), (gk.shape, WIDE), ((1, width), WIDE)
        )
    )
    return pl.pallas_call(
        attend_back_kernel,
        grid=(count,),
        in_specs=[first_spec(array) for array in blocks] + [whole_spec(array) for array in fixed],
        out_specs=[first_spec(upper)] + [whole_spec(array) for array in sums],
        out_shape=(jax.ShapeDtypeStruct((count, rows, width), LOW),) + sums,
        scratch_shapes=[pltpu.VMEM((width, 4 * wide), WIDE)],
        compiler_params=pltpu.CompilerParams(vmem_limit_bytes=VMEM_BYTES),
        cost_estimate=COST,
        name="attend_backward",
    )(*blocks, *fixed)


def slot_spots(table, expert):
    row_count = table.shape[1]
    slots = lax.broadcasted_iota(jnp.int32, (CAP, row_count), 0).astype(WIDE) + 1.0
    mine = lax.broadcasted_iota(jnp.int32, table.shape, 0) == expert
    ranks = jnp.sum(jnp.where(mine, table, 0.0), axis=0, keepdims=True)
    return (slots == ranks).astype(LOW)


class Trades:
    def __init__(self, trades):
        self.trades = trades
        self.axes = sorted({(axis, size) for _, axis, size, _ in trades})
        self.arrays = [array for array, _, _, _ in trades]
        self.in_specs = [pl.BlockSpec(memory_space=pltpu.VMEM) for _ in trades]
        self.out_specs = [pl.BlockSpec(memory_space=pl.ANY) for _ in trades]
        self.out_shapes = [
            jax.ShapeDtypeStruct(array.shape if pieces else (size,) + array.shape, array.dtype)
            for array, _, size, pieces in trades
        ]
        self.scratch = [
            pltpu.SemaphoreType.DMA((size,)) for _, _, size, _ in trades for _ in range(2)
        ]

    def bind(self, sources, targets, sems):
        self.sources, self.targets, self.sems = (sources, targets, sems)

    def device(self, axis, size, bits):
        return {axis: lax.rem(lax.axis_index(axis) + bits, size)}

    def copies(self):
        for number, (_, axis, size, pieces) in enumerate(self.trades):
            me = lax.axis_index(axis)
            send, recv = (self.sems[2 * number], self.sems[2 * number + 1])
            target = self.targets[number].at[me]
            for bits in range(size):
                source = self.sources[number]
                source = source.at[lax.rem(me + bits, size)] if pieces else source
                if bits == 0:
                    yield pltpu.make_async_copy(source, target, send.at[0])
                else:
                    yield pltpu.make_async_remote_copy(
                        source, target, send.at[bits], recv.at[bits],
                        device_id=self.device(axis, size, bits),
                        device_id_type=pl.DeviceIdType.MESH,
                    )

    def start(self):
        barrier = pltpu.get_barrier_semaphore()
        for axis, size in self.axes:
            for bits in range(1, size):
                pl.semaphore_signal(
                    barrier, inc=1, device_id=self.device(axis, size, bits),
                    device_id_type=pl.DeviceIdType.MESH,
                )
        pl.semaphore_wait(barrier, sum(size - 1 for _, size in self.axes))
        for copy in self.copies():
            copy.start()

    def finish(self):
        for copy in self.copies():
            copy.wait()


UNIT = 2


def expert_block(expert, rows_in, cots_in, wg, wu, wd, wr, x_ref, y_ref, m_ref, dg_ref, du_ref):
    row_count, hidden = (rows_in[0].shape[0], wg.shape[-1])
    for seq, (rows, cots) in enumerate(zip(rows_in, cots_in)):
        spots = slot_spots(cots[row_count:, :row_count].astype(WIDE), expert)
        span = pl.ds(seq * CAP, CAP)
        x_ref[span] = dot_nn(spots, rows[...]).astype(LOW)
        y_ref[span] = dot_nn(spots, cots[:row_count]).astype(LOW)
    x_all, y_all = (x_ref[...], y_ref[...])
    logits = dot_nn(x_all, wr[...])
    expo = jnp.exp(logits - jnp.max(logits, axis=-1, keepdims=True))
    chosen = lax.broadcasted_iota(jnp.int32, expo.shape, 1) == expert
    gates = jnp.sum(jnp.where(chosen, expo, 0.0), axis=-1, keepdims=True) / jnp.sum(
        expo, axis=-1, keepdims=True
    )
    step = min(256, hidden)
    dgate = jnp.zeros((x_all.shape[0], 1), WIDE)
    for start in range(0, hidden, step):
        span = slice(start, start + step)
        gate_act, up_act = (dot_nn(x_all, wg[:, span]), dot_nn(x_all, wu[:, span]))
        plain_grad = dot_nt(y_all, wd[span, :])
        sig = jax.nn.sigmoid(gate_act)
        silu = gate_act * sig
        joined = silu * up_act
        dgate += jnp.sum(joined * plain_grad, axis=-1, keepdims=True)
        grad = plain_grad * gates
        m_ref[:, span] = (joined * gates).astype(LOW)
        dg_ref[:, span] = (grad * up_act * (sig + silu * (1.0 - sig))).astype(LOW)
        du_ref[:, span] = (grad * silu).astype(LOW)
    return dgate


def expert_kernel(row_spans, cot_spans, batch, trades, ex_ref, wg, wu, wd, wr, *refs):
    first, second = (len(row_spans), len(row_spans) + len(cot_spans))
    rows_in, cots_in = (refs[:first], refs[first:second])
    third, number = (second + len(trades.trades), len(trades.trades))
    x_ref, y_ref, m_ref, dg_ref, du_ref, dgate_ref = refs[third : third + 6]
    rows_buf, cots_buf, sems = refs[third + 6 + number : third + 9 + number]
    trades.bind(refs[second:third], refs[third + 6 : third + 6 + number], refs[third + 9 + number :])
    steps, units = (sum(count for _, count in row_spans) // batch, batch // UNIT)
    turn = pl.program_id(0) * steps + pl.program_id(1)
    slot = lax.rem(turn, 2)
    row_count = rows_buf.shape[2]

    def copy(kind, source, offset, place, part):
        buffer = (rows_buf, cots_buf)[kind]
        return pltpu.make_async_copy(
            source.at[pl.ds(offset, UNIT)],
            buffer.at[place, pl.ds(part * UNIT, UNIT)],
            sems.at[kind, place, part],
        )

    def fetch(step, place):
        for part in range(units):
            unit = step * units + part
            for kind, sources, spans in ((0, rows_in, row_spans), (1, cots_in, cot_spans)):
                begin = 0
                for source, (offset, count) in zip(sources, spans):
                    size = count // UNIT

                    @pl.when((unit >= begin) & (unit < begin + size))
                    def _(source=source, begin=begin, offset=offset):
                        copy(kind, source, offset + (unit - begin) * UNIT, place, part).start()

                    begin += size

    @pl.when(turn == 0)
    def _():
        fetch(turn, slot)
        if number:
            trades.start()

    @pl.when(turn + 1 < pl.num_programs(0) * steps)
    def _():
        fetch(lax.rem(turn + 1, steps), 1 - slot)

    for part in range(units):
        copy(0, rows_in[0], 0, slot, part).wait()
        copy(1, cots_in[0], 0, slot, part).wait()
    dgate = expert_block(
        ex_ref[pl.program_id(0)],
        [rows_buf.at[slot, seq] for seq in range(batch)],
        [cots_buf.at[slot, seq] for seq in range(batch)],
        wg.at[0], wu.at[0], wd.at[0], wr,
        x_ref.at[0], y_ref.at[0], m_ref.at[0], dg_ref.at[0], du_ref.at[0],
    )
    dgate_ref[0] = jnp.broadcast_to(dgate, dgate_ref.shape[1:])
    if number:

        @pl.when(turn == pl.num_programs(0) * steps - 1)
        def _():
            trades.finish()


def expert_acts(ids, rows, cots, wg, wu, wd, wr, batch=4, trades=(), collective=None):
    trades = Trades(trades)
    row_spans, cot_spans = ([span for _, span in items] for items in (rows, cots))
    rows, cots = ([array for array, _ in items] for items in (rows, cots))
    count = sum(size for _, size in row_spans)
    width = rows[0].shape[2]
    own, _, hidden = wg.shape
    out_rows = batch * CAP

    def acts(cols, kind=LOW):
        return jax.ShapeDtypeStruct((own, count * CAP, cols), kind)

    def act_spec(cols):
        return pl.BlockSpec((1, out_rows, cols), lambda e, i: (e, i, 0))

    def weight_spec(array):
        return pl.BlockSpec(
            (1,) + array.shape[1:], lambda e, i: (e, 0, 0), pipeline_mode=pl.Buffered(1)
        )

    any_spec = pl.BlockSpec(memory_space=pl.ANY)
    columns = (width, width, hidden, hidden, hidden, 128)
    return pl.pallas_call(
        functools.partial(expert_kernel, row_spans, cot_spans, batch, trades),
        grid=(own, count // batch),
        in_specs=[
            pl.BlockSpec(memory_space=pltpu.SMEM),
            weight_spec(wg),
            weight_spec(wu),
            weight_spec(wd),
            pl.BlockSpec(wr.shape, lambda e, i: (0, 0)),
        ]
        + [any_spec] * (len(rows) + len(cots))
        + trades.in_specs,
        out_specs=[act_spec(cols) for cols in columns] + trades.out_specs,
        out_shape=[acts(cols) for cols in columns[:5]] + [acts(128, WIDE)] + trades.out_shapes,
        scratch_shapes=[
            pltpu.VMEM((2, batch) + rows[0].shape[1:], LOW),
            pltpu.VMEM((2, batch) + cots[0].shape[1:], LOW),
            pltpu.SemaphoreType.DMA((2, 2, batch // UNIT)),
        ]
        + trades.scratch,
        compiler_params=pltpu.CompilerParams(
            vmem_limit_bytes=VMEM_BYTES,
            collective_id=collective,
            has_side_effects=collective is not None,
        ),
        cost_estimate=COST,
        name="expert_acts",
    )(ids, wg, wu, wd, wr, *rows, *cots, *trades.arrays)


def pull_block(experts, rows, table, backs, dgates, wr):
    logits = dot_nn(rows, wr[...])
    expo = jnp.exp(logits - jnp.max(logits, axis=-1, keepdims=True))
    probs = expo / jnp.sum(expo, axis=-1, keepdims=True)
    columns = lax.broadcasted_iota(jnp.int32, probs.shape, 1)
    grad_logits = jnp.zeros_like(probs)
    total = jnp.zeros(rows.shape, WIDE)
    for expert, back, dgate in zip(experts, backs, dgates):
        spots = slot_spots(table, expert)
        total += dot_tn(spots, back)
        high = dgate.astype(LOW)
        rest = (dgate - high.astype(WIDE)).astype(LOW)
        at_rows = (dot_tn(spots, high) + dot_tn(spots, rest))[:, : probs.shape[1]]
        chosen = (columns == expert).astype(WIDE)
        prob = jnp.sum(probs * chosen, axis=-1, keepdims=True)
        grad_logits += at_rows * prob * (chosen - probs)
    low_logits = grad_logits.astype(LOW)
    return (total + dot_nt(low_logits, wr[...])).astype(LOW), dot_tn(low_logits, rows)


def pull_kernel(ex_ref, rows_ref, cot_ref, dg_ref, du_ref, dgate_ref, wg, wu, wr, part_ref, router):
    batch, row_count, _ = rows_ref.shape
    own = wg.shape[0]

    @pl.when(pl.program_id(0) == 0)
    def _():
        router[...] = jnp.zeros_like(router)

    backs = [
        (dot_nt(dg_ref[e], wg[e]) + dot_nt(du_ref[e], wu[e])).astype(LOW) for e in range(own)
    ]
    for seq in range(batch):
        span = slice(seq * CAP, (seq + 1) * CAP)
        part_ref[seq], router_part = pull_block(
            [ex_ref[e] for e in range(own)],
            rows_ref[seq],
            cot_ref[seq, :, :row_count].astype(WIDE),
            [back[span] for back in backs],
            [dgate_ref[e, span] for e in range(own)],
            wr,
        )
        router[...] += router_part


def mix_kernel(ex_ref, cot_ref, m_ref, wd, part_ref):
    batch, row_count, _ = part_ref.shape
    own = wd.shape[0]
    outs = [dot_nn(m_ref[e], wd[e]).astype(LOW) for e in range(own)]
    for seq in range(batch):
        table = cot_ref[seq, :, :row_count].astype(WIDE)
        span = slice(seq * CAP, (seq + 1) * CAP)
        total = sum(dot_tn(slot_spots(table, ex_ref[e]), outs[e][span]) for e in range(own))
        part_ref[seq] = total.astype(LOW)


def spread_call(kernel, name, ids, by_seq, cots, by_slot, fixed, router_shape, batch=2):
    count, lines, width = cots.shape
    row_count = lines - LINES
    part = jax.ShapeDtypeStruct((count, row_count, width), LOW)

    def seq_spec(array):
        return pl.BlockSpec((batch,) + array.shape[1:], lambda i: (i, 0, 0))

    def slot_spec(array):
        return pl.BlockSpec((array.shape[0], batch * CAP, array.shape[2]), lambda i: (0, i, 0))

    return pl.pallas_call(
        kernel,
        grid=(count // batch,),
        in_specs=[pl.BlockSpec(memory_space=pltpu.SMEM)]
        + [seq_spec(array) for array in by_seq]
        + [pl.BlockSpec((batch, LINES, width), lambda i: (i, row_count // LINES, 0))]
        + [slot_spec(array) for array in by_slot]
        + [whole_spec(array) for array in fixed],
        out_specs=[seq_spec(part)] + [whole_spec(shape) for shape in router_shape],
        out_shape=[part] + list(router_shape),
        compiler_params=pltpu.CompilerParams(vmem_limit_bytes=VMEM_BYTES),
        cost_estimate=COST,
        name=name,
    )(ids, *by_seq, cots, *by_slot, *fixed)


def weight_grad(lefts, rights, starts=None, trades=(), collective=None, in_place=True):
    own, _, left_cols = lefts[0].shape
    right_cols = rights[0][0].shape[-1]
    sets, outs = (len(lefts), len(rights))
    tile = min(512, left_cols)
    trades = Trades(trades)
    number, begun = (len(trades.trades), 0 if starts is None else outs)
    first = sets * (1 + outs)

    def kernel(*refs):
        refs, tail = (refs[: first + begun], refs[first + begun :])
        results = tail[number : number + outs]
        trades.bind(
            tail[:number], tail[number + outs : 2 * number + outs], tail[2 * number + outs :]
        )
        if number:

            @pl.when((pl.program_id(0) == 0) & (pl.program_id(1) == 0))
            def _():
                trades.start()

        for place in range(outs):
            total = sum(
                dot_tn(refs[i][0], refs[sets * (1 + place) + i][0]) for i in range(sets)
            )
            results[place][0] = total + refs[first + place][0] if begun else total
        if number:

            @pl.when((pl.program_id(0) == own - 1) & (pl.program_id(1) == left_cols // tile - 1))
            def _():
                trades.finish()

    out_spec = pl.BlockSpec((1, tile, right_cols), lambda e, l: (e, l, 0))
    flat = [array for group in rights for array in group]
    return pl.pallas_call(
        kernel,
        grid=(own, left_cols // tile),
        in_specs=[
            pl.BlockSpec((1, array.shape[1], tile), lambda e, l: (e, 0, l)) for array in lefts
        ]
        + [pl.BlockSpec((1,) + array.shape[1:], lambda e, l: (e, 0, 0)) for array in flat]
        + [out_spec] * begun
        + trades.in_specs,
        out_specs=[out_spec] * outs + trades.out_specs,
        out_shape=[jax.ShapeDtypeStruct((own, left_cols, right_cols), WIDE)] * outs
        + trades.out_shapes,
        scratch_shapes=trades.scratch,
        input_output_aliases={first + place: place for place in range(begun * in_place)},
        compiler_params=pltpu.CompilerParams(
            vmem_limit_bytes=VMEM_BYTES,
            collective_id=collective,
            has_side_effects=collective is not None,
        ),
        cost_estimate=COST,
        name="weight_grad",
    )(*lefts, *flat, *(starts or []), *trades.arrays)


CHUNKS = 4
NEAR_LINES = 128


def each(size, body):
    def step(i, carry):
        body(i)
        return carry

    lax.fori_loop(0, size, step, 0)


def remote(source, target, send, recv, device):
    return pltpu.make_async_remote_copy(
        source, target, send, recv, device_id=device, device_id_type=pl.DeviceIdType.MESH
    )


class Links:
    def __init__(self, replicas, groups):
        rep, shard = (lax.axis_index("rep"), lax.axis_index("shard"))
        self.rail = groups // 2
        self.last = self.rail - 1
        self.shard, self.place, self.core = (shard, shard // 2, shard % 2)
        self.right, self.left = ((rep, shard + 2), (rep, shard - 2))
        self.partner = (rep, shard + 1 - 2 * self.core)
        self.over_x = (rep + 1 - 2 * (rep % 2), shard)
        self.over_y = ((rep + 2) % replicas, shard)

    def greet(self, others):
        barrier = pltpu.get_barrier_semaphore()

        def signal(device):
            pl.semaphore_signal(
                barrier, inc=1, device_id=device, device_id_type=pl.DeviceIdType.MESH
            )

        for device in others:
            signal(device)
        pl.when(self.place < self.last)(lambda: signal(self.right))
        pl.when(self.place > 0)(lambda: signal(self.left))
        inner = (self.place > 0) & (self.place < self.last)
        pl.when(inner)(lambda: pl.semaphore_wait(barrier, len(others) + 2))
        pl.when(jnp.logical_not(inner))(lambda: pl.semaphore_wait(barrier, len(others) + 1))


class Flood:
    def __init__(self, links, view, send, recv, pair, own):
        self.links, self.view, self.own = (links, view, own)
        self.send, self.recv, self.pair = (send, recv, pair)

    def copy(self, way, q, own=False):
        links = self.links
        slot = 2 * q + links.core
        source = self.own if own else self.view.at[slot]
        recv = self.pair.at[q] if way == 2 else self.recv.at[q]
        device = (links.right, links.left, links.partner)[way]
        return remote(source, self.view.at[slot], self.send.at[way, q], recv, device)

    def start(self):
        place = self.links.place

        @pl.when(place < self.links.last)
        def _():
            self.copy(0, place, True).start()

        @pl.when(place > 0)
        def _():
            self.copy(1, place, True).start()

        self.copy(2, place, True).start()

    def onward(self, d, more=None):
        place, last = (self.links.place, self.links.last)

        @pl.when((d > 0) & (place - d >= 0))
        def _():
            q = place - d
            self.copy(0, q).wait_recv()

            @pl.when(place < last)
            def _():
                self.copy(0, q).start()

            self.copy(2, q).start()
            if more is not None:
                more(q)

        @pl.when((d > 0) & (place + d <= last))
        def _():
            q = place + d
            self.copy(1, q).wait_recv()

            @pl.when(place > 0)
            def _():
                self.copy(1, q).start()

            self.copy(2, q).start()
            if more is not None:
                more(q)

    def wait_pair(self, q):
        slot = self.view.at[2 * q + 1 - self.links.core]
        remote(slot, slot, self.send.at[2, q], self.pair.at[q], self.links.partner).wait_recv()

    def finish(self, q):
        place = self.links.place

        @pl.when((place < self.links.last) & (q <= place))
        def _():
            self.copy(0, q).wait_send()

        @pl.when((place > 0) & (q >= place))
        def _():
            self.copy(1, q).wait_send()

        self.copy(2, q).wait_send()


def front_kernel(
    replicas, groups,
    packet, tokens, wq, wk, wv, wo, gq, gk, cos_ref, sin_ref, gain_ref,
    packets, qr_ref, kr_ref, v_ref, o_ref, hidden, low,
    nb, mine, pair_out, pair_in, line_r, line_l,
    n1_send, n1_recv, n1_pair, po_send, po_recv, lr_send, lr_recv, ll_send, ll_recv, keep_sem, own_sem,
):
    links = Links(replicas, groups)
    rail, last, place, core = (links.rail, links.last, links.place, links.core)
    rows = tokens.shape[0]
    step_rows = rows // CHUNKS
    flood = Flood(links, nb, n1_send, n1_recv, n1_pair, packet)
    links.greet([links.partner])
    flood.start()
    own_block = pltpu.make_async_copy(packet, nb.at[links.shard], own_sem.at[0])
    own_block.start()
    own_block.wait()

    def partial_out(q):
        return remote(pair_out.at[q], pair_in.at[q], po_send.at[q], po_recv.at[q], links.partner)

    def chunk_span(chunk):
        return pl.ds(pl.multiple_of(chunk * step_rows, step_rows), step_rows)

    def line(q, chunk, to_right):
        span = chunk_span(chunk)
        target, send, recv, device = (
            (line_r, lr_send, lr_recv, links.right)
            if to_right
            else (line_l, ll_send, ll_recv, links.left)
        )
        return remote(
            mine.at[q, span], target.at[q, span], send.at[q, chunk], recv.at[q, chunk], device
        )

    def add_up(q, chunk, extras):
        span = chunk_span(chunk)
        total = mine[q, span].astype(WIDE) + pair_in[q, span].astype(WIDE)
        for extra in extras:
            total = total + extra[q, span].astype(WIDE)
        return total

    def forward_line(q, to_right, first):
        partial_out(q).wait_recv()

        def body(chunk):
            extras = []
            if not first:
                line(q, chunk, to_right).wait_recv()
                extras = [line_r if to_right else line_l]
            mine[q, chunk_span(chunk)] = add_up(q, chunk, extras).astype(LOW)
            line(q, chunk, to_right).start()

        each(CHUNKS, body)

    def keep_copy(slot):
        return pltpu.make_async_copy(nb.at[slot], packets.at[slot], keep_sem.at[slot])

    def one_distance(d):
        flood.onward(d)

        def one_block(k):
            side, other = (k % 2, k // 2)
            q = place + (2 * side - 1) * d

            @pl.when((q >= 0) & (q <= last) & ((d > 0) | (side == 0)))
            def _():
                @pl.when(other == 1)
                def _():
                    flood.wait_pair(q)

                slot = 2 * q + core + other * (1 - 2 * core)
                keep_copy(slot).start()
                length = nb[slot, rows:, rows : rows + 128].astype(WIDE)[0:1, 0:1]

                def keep(query_raw, key_raw, value, joined):
                    qr_ref[slot], kr_ref[slot] = (query_raw, key_raw)
                    v_ref[slot], o_ref[slot] = (value, joined)

                part = attend_block(
                    nb[slot, :rows], length, wq, wk, wv, wo, gq[...], gk[...],
                    cos_ref[...], sin_ref[...], keep,
                )

                @pl.when(other == 0)
                def _():
                    mine[q] = part

                @pl.when(other == 1)
                def _():
                    pair_out[q] = part
                    partial_out(q).start()

        each(4, one_block)

        @pl.when((place == 0) & (d > 0))
        def _():
            forward_line(d, True, True)

        @pl.when((place == last) & (d > 0))
        def _():
            forward_line(last - d, False, True)

    each(rail, one_distance)

    def rest_right():
        def body(j):
            @pl.when((place > 0) & (place + j <= last))
            def _():
                forward_line(place + j, True, False)

        each(last, lambda i: body(i + 1))

    def rest_left():
        def body(j):
            @pl.when((place < last) & (place - j >= 0))
            def _():
                forward_line(place - j, False, False)

        each(last, lambda i: body(i + 1))

    near_end = place < rail // 2
    pl.when(near_end)(rest_right)
    pl.when(jnp.logical_not(near_end))(rest_left)
    pl.when(near_end)(rest_left)
    pl.when(jnp.logical_not(near_end))(rest_right)
    partial_out(place).wait_recv()

    def finish_rows(chunk):
        @pl.when(place > 0)
        def _():
            line(place, chunk, True).wait_recv()

        @pl.when(place < last)
        def _():
            line(place, chunk, False).wait_recv()

        span = chunk_span(chunk)
        total = tokens[span].astype(WIDE) + add_up(place, chunk, [])
        from_left = jnp.where(place > 0, line_r[place, span].astype(WIDE), 0.0)
        from_right = jnp.where(place < last, line_l[place, span].astype(WIDE), 0.0)
        total = total + from_left + from_right
        hidden[span] = total
        scale = lax.rsqrt(jnp.mean(total * total, axis=-1, keepdims=True) + EPS_NORM)
        low[span] = (total * scale * gain_ref[...]).astype(LOW)

    each(CHUNKS, finish_rows)

    def settle(q):
        flood.finish(q)
        keep_copy(2 * q).wait()
        keep_copy(2 * q + 1).wait()
        partial_out(q).wait_send()

        def chunk_sends(chunk):
            @pl.when((place < last) & (q > place))
            def _():
                line(q, chunk, True).wait_send()

            @pl.when((place > 0) & (q < place))
            def _():
                line(q, chunk, False).wait_send()

        each(CHUNKS, chunk_sends)

    each(rail, settle)


ANY_SPEC = pl.BlockSpec(memory_space=pl.ANY)
FAST_SPEC = pl.BlockSpec(memory_space=pltpu.VMEM)


def shape(*dims, kind=LOW):
    return jax.ShapeDtypeStruct(dims, kind)


def front(replicas, groups, packet, tokens, wq, wk, wv, wo, gq, gk, cos_tab, sin_tab, gain):
    lines, width = packet.shape
    rows, wide, rail = (tokens.shape[0], wq.shape[1], groups // 2)
    block = pltpu.VMEM((rail, rows, width), LOW)
    dma = pltpu.SemaphoreType.DMA
    return pl.pallas_call(
        functools.partial(front_kernel, replicas, groups),
        in_specs=[ANY_SPEC] + [FAST_SPEC] * 10,
        out_specs=[ANY_SPEC] + [FAST_SPEC] * 6,
        out_shape=[
            shape(groups, lines, width),
            shape(groups, rows, wide, kind=WIDE),
            shape(groups, rows, wide, kind=WIDE),
            shape(groups, rows, wide),
            shape(groups, rows, wide),
            shape(rows, width, kind=WIDE),
            shape(rows, width),
        ],
        scratch_shapes=[pltpu.VMEM((groups, lines, width), LOW), block, block, block, block, block]
        + [dma((3, rail)), dma((rail,)), dma((rail,))]
        + [dma((rail,))] * 2
        + [dma((rail, CHUNKS))] * 4
        + [dma((groups,)), dma((1,))],
        compiler_params=pltpu.CompilerParams(
            vmem_limit_bytes=VMEM_BYTES, collective_id=0, has_side_effects=True
        ),
        cost_estimate=COST,
        name="front",
    )(packet, tokens, wq, wk, wv, wo, gq, gk, cos_tab, sin_tab, gain)


def moe_kernel(
    replicas, groups,
    ex_ref, low, cot, wg_in, wu_in, wd_in, wr,
    rows_all, cots, fx, fy, fd, px, py, pd, x_out, y_out, m_out, dg_out, du_out, part_out, router,
    wg, wu, wd, rows_buf, cots_buf, x_s, y_s, m_s, dg_s, du_s, part_s,
    n2_send, n2_recv, n2_pair, cz_send, cz_recv, cz_pair,
    xy_send, xy_recv, dg_send, dg_recv, fl_send, fl_recv, own_sem, load_sem, out_sem, part_sem,
):
    links = Links(replicas, groups)
    rail, last, place, core = (links.rail, links.last, links.place, links.core)
    own, row_count = (wg.shape[0], low.shape[0])
    flood_n2 = Flood(links, rows_all, n2_send, n2_recv, n2_pair, low)
    flood_cot = Flood(links, cots, cz_send, cz_recv, cz_pair, cot)

    def cross(way, q, own_block=False):
        source = cot if own_block else cots.at[2 * q + core]
        target, device = ((fx, links.over_x), (fy, links.over_y))[way]
        return remote(source, target.at[q], xy_send.at[way, q], xy_recv.at[way, q], device)

    def cross_both(q):
        cross(0, q).start()
        cross(1, q).start()

    def diagonal(way, q):
        source, device = ((fx, links.over_y), (fy, links.over_x))[way]
        span = (pl.ds(0, NEAR_LINES), pl.ds(NEAR_LINES, cot.shape[0] - NEAR_LINES))[way]
        return remote(
            source.at[q, span], fd.at[q, span], dg_send.at[way, q], dg_recv.at[way, q], device
        )

    def flip(which, q):
        source, target = ((fx, px), (fy, py), (fd, pd))[which]
        return remote(
            source.at[q], target.at[q], fl_send.at[which, q], fl_recv.at[which, q], links.partner
        )

    def at_distance(d, body):
        @pl.when((d >= 0) & (place - d >= 0))
        def _():
            body(place - d)

        @pl.when((d > 0) & (place + d <= last))
        def _():
            body(place + d)

    def take_cross(q):
        for way in (0, 1):
            cross(way, q).wait_recv()
            diagonal(way, q).start()
            flip(way, q).start()

    def take_diagonal(q):
        for way in (0, 1):
            diagonal(way, q).wait_recv()
        flip(2, q).start()

    links.greet([links.partner, links.over_x, links.over_y])
    flood_cot.start()
    flood_n2.start()
    cross(0, place, True).start()
    cross(1, place, True).start()
    own_copies = (
        pltpu.make_async_copy(low, rows_all.at[links.shard], own_sem.at[0]),
        pltpu.make_async_copy(cot, cots.at[links.shard], own_sem.at[1]),
        pltpu.make_async_copy(wg_in, wg, own_sem.at[2]),
        pltpu.make_async_copy(wu_in, wu, own_sem.at[3]),
        pltpu.make_async_copy(wd_in, wd, own_sem.at[4]),
    )
    for copy in own_copies:
        copy.start()
    router[...] = jnp.zeros_like(router)
    for copy in own_copies:
        copy.wait()

    def out_copies(q):
        span = pl.ds(2 * q * CAP, 2 * CAP)
        pairs = ((x_s, x_out), (y_s, y_out), (m_s, m_out), (dg_s, dg_out), (du_s, du_out))
        return [
            pltpu.make_async_copy(source.at[e], target.at[e, span], out_sem.at[e, i])
            for e in range(own)
            for i, (source, target) in enumerate(pairs)
        ]

    def part_copy(q):
        return pltpu.make_async_copy(part_s, part_out.at[pl.ds(2 * q, 2)], part_sem.at[0])

    near = jnp.where(place <= last - place, place, last - place)
    far_sign = jnp.where(place <= last - place, 1, -1)

    def one_step(k):
        flood_cot.onward(k, cross_both)
        flood_n2.onward(k)
        at_distance(k - 1, take_cross)
        at_distance(k - 2, take_diagonal)
        within = k <= 2 * near
        sign = jnp.where(within & (k % 2 == 1), -far_sign, far_sign)
        q = place + sign * jnp.where(within, (k + 1) // 2, k - near)
        flood_cot.wait_pair(q)
        flood_n2.wait_pair(q)
        loads = (
            pltpu.make_async_copy(rows_all.at[pl.ds(2 * q, 2)], rows_buf, load_sem.at[0]),
            pltpu.make_async_copy(cots.at[pl.ds(2 * q, 2)], cots_buf, load_sem.at[1]),
        )
        for copy in loads:
            copy.start()

        @pl.when(k > 0)
        def _():
            for copy in out_copies(0):
                copy.wait()
            part_copy(0).wait()

        for copy in loads:
            copy.wait()
        dgates, backs = ([], [])
        for e in range(own):
            dgate = expert_block(
                ex_ref[e],
                [rows_buf.at[seq] for seq in range(2)],
                [cots_buf.at[seq] for seq in range(2)],
                wg.at[e], wu.at[e], wd.at[e], wr,
                x_s.at[e], y_s.at[e], m_s.at[e], dg_s.at[e], du_s.at[e],
            )
            dgates.append(jnp.broadcast_to(dgate, (dgate.shape[0], 128)))
            backs.append((dot_nt(dg_s[e], wg[e]) + dot_nt(du_s[e], wu[e])).astype(LOW))
        for copy in out_copies(q):
            copy.start()
        for seq in range(2):
            span = slice(seq * CAP, (seq + 1) * CAP)
            part_s[seq], router_part = pull_block(
                [ex_ref[e] for e in range(own)],
                rows_buf[seq],
                cots_buf[seq, row_count:, :row_count].astype(WIDE),
                [back[span] for back in backs],
                [dgate[span] for dgate in dgates],
                wr,
            )
            router[...] += router_part
        part_copy(q).start()

    each(rail, one_step)
    at_distance(last, take_cross)
    at_distance(last - 1, take_diagonal)
    at_distance(last, take_diagonal)
    for copy in out_copies(0):
        copy.wait()
    part_copy(0).wait()

    def settle(q):
        flood_n2.finish(q)
        flood_cot.finish(q)
        for way in (0, 1):
            cross(way, q).wait_send()
            diagonal(way, q).wait_send()
        for which in (0, 1, 2):
            flip(which, q).wait_send()
            flip(which, q).wait_recv()

    each(rail, settle)


def moe(replicas, groups, ids, low, cot, wg, wu, wd, wr):
    lines, width = cot.shape
    rows, rail = (low.shape[0], groups // 2)
    own, _, hidden = wg.shape
    pair = 2 * CAP
    dma, vmem = (pltpu.SemaphoreType.DMA, pltpu.VMEM)
    acts = [shape(own, groups * CAP, cols) for cols in (width, width, hidden, hidden, hidden)]
    return pl.pallas_call(
        functools.partial(moe_kernel, replicas, groups),
        in_specs=[pl.BlockSpec(memory_space=pltpu.SMEM)]
        + [FAST_SPEC] * 2
        + [ANY_SPEC] * 3
        + [FAST_SPEC],
        out_specs=[ANY_SPEC] * 14 + [FAST_SPEC],
        out_shape=[shape(groups, rows, width), shape(groups, lines, width)]
        + [shape(rail, lines, width)] * 6
        + acts
        + [shape(groups, rows, width), shape(wr.shape[1], width, kind=WIDE)],
        scratch_shapes=[vmem(array.shape, LOW) for array in (wg, wu, wd)]
        + [vmem((2, rows, width), LOW), vmem((2, lines, width), LOW)]
        + [vmem((own, pair, cols), LOW) for cols in (width, width, hidden, hidden, hidden)]
        + [vmem((2, rows, width), LOW)]
        + [dma((3, rail)), dma((rail,)), dma((rail,))] * 2
        + [dma((2, rail))] * 4
        + [dma((3, rail))] * 2
        + [dma((5,)), dma((2,)), dma((own, 5)), dma((1,))],
        compiler_params=pltpu.CompilerParams(
            vmem_limit_bytes=VMEM_BYTES, collective_id=3, has_side_effects=True
        ),
        cost_estimate=COST,
        name="moe",
    )(ids, low, cot, wg, wu, wd, wr)


def rms_parts(values):
    scale = lax.rsqrt(jnp.mean(values * values, axis=-1, keepdims=True) + EPS_NORM)
    return (values * scale, scale)


def rms_back(plain, scale, gain, grad):
    back = grad * gain
    return scale * (back - plain * jnp.mean(back * plain, axis=-1, keepdims=True))


def local(
    tokens, lengths, routes, gain_attn, gain_query, gain_key,
    w_query, w_key, w_value, w_out, gain_moe, w_router,
    w_gate, w_up, w_down, out_grad,
):
    row_count, width = tokens.shape
    head_dim = gain_query.shape[0]
    groups, replicas = (lax.axis_size("shard"), lax.axis_size("rep"))
    expert_count, own = (w_router.shape[1], w_gate.shape[0])
    wide = w_query.shape[1]
    after = lax.optimization_barrier
    gain_q, gain_k = (gain_query.reshape(1, -1), gain_key.reshape(1, -1))
    cos_tab, sin_tab = rope_tables(row_count, head_dim)
    ids = lax.axis_index("shard") * own + jnp.arange(own, dtype=jnp.int32)

    def flip_replica(values, bits):
        return lax.ppermute(values, "rep", [(i, i ^ bits) for i in range(replicas)])

    def flip_shard(values, bits):
        return lax.ppermute(values, "shard", [(i, i ^ bits) for i in range(groups)])

    def scatter_sum(parts):
        return lax.psum_scatter(
            parts.reshape(-1, width), "shard", scatter_dimension=0, tiled=True
        ).astype(WIDE)

    experts = (w_gate, w_up, w_down, w_router)

    def whole(*arrays):
        return [(array, (0, array.shape[0])) for array in arrays]

    def in_grads(acts, grads=None, **more):
        return weight_grad(
            [act[0] for act in acts], [[act[place] for act in acts] for place in (3, 4)], grads, **more
        )

    def down_grads(acts, grads=None):
        return weight_grad([act[2] for act in acts], [[act[1] for act in acts]], grads)

    inputs = tokens.astype(WIDE)
    row_mask = (jnp.arange(row_count, dtype=jnp.int32) < lengths[0])[:, None]
    named = jnp.any(
        routes[None, :, :] == jnp.arange(expert_count, dtype=jnp.int32)[:, None, None], axis=-1
    )
    upto = (jnp.arange(row_count)[:, None] <= jnp.arange(row_count)[None, :]).astype(LOW)
    ranks = jnp.where(named, dot_nn(named.astype(LOW), upto), 0.0).astype(LOW)
    lines = jnp.concatenate(
        [ranks, jnp.broadcast_to(lengths[0].astype(LOW), (expert_count, width - row_count))], axis=1
    )
    plain_in, scale_in = rms_parts(inputs)
    packet = jnp.concatenate([(plain_in * gain_attn).astype(LOW), lines], axis=0)
    cot_low = jnp.where(row_mask, out_grad, 0.0)
    cot_packet = jnp.concatenate([cot_low, lines], axis=0)
    heads = (w_query, w_key, w_value, w_out, gain_q, gain_k, cos_tab, sin_tab)
    share = replicas == 4 and groups == 8
    if share:
        packets, *kept, hidden, low = front(
            replicas, groups, packet, tokens, *heads, gain_moe.reshape(1, -1)
        )
        rows_all, cots, *found = moe(
            replicas, groups, ids, low, cot_packet, w_gate, w_up, w_down, w_router
        )
        far_cots, acts, (pull_part, grad_router) = (found[:6], [found[6:11]], found[11:])
        gated = acts[0][2]
        pairs = rows_all.reshape((groups // 2, 2) + rows_all.shape[1:])
        core = lax.axis_index("shard") % 2
        near = [
            lax.dynamic_slice(pairs, (start, core, 0, 0), (2, 1) + pairs.shape[2:])[:, 0]
            for start in (0, 2)
        ]
        early, late = ([flip_replica(part, bits) for bits in (1, 2)] for part in near)
    else:
        packets = lax.all_gather(packet, "shard", axis=0)
        cot_packet, packets = after((cot_packet, packets))
        cots = lax.all_gather(cot_packet, "shard", axis=0)
        part, *kept = attend_forward(packets, *heads)
        hidden = inputs + scatter_sum(part)
        plain_mid, scale_mid = rms_parts(hidden)
        rows_all = lax.all_gather((plain_mid * gain_moe).astype(LOW), "shard", axis=0)

        acts = [expert_acts(ids, whole(rows_all), whole(cots), *experts)]
        _, _, gated, grad_gate_act, grad_up_act, dgates = acts[0]
        pull_part, grad_router = spread_call(
            pull_kernel, "expert_pull", ids, (rows_all,), cots,
            (grad_gate_act, grad_up_act, dgates), (w_gate, w_up, w_router),
            (jax.ShapeDtypeStruct(w_router.shape[::-1], WIDE),),
        )
    grad_moe_in = scatter_sum(pull_part)
    gated, pull_part = after((gated, pull_part))
    (mix_part,) = spread_call(mix_kernel, "expert_mix", ids, (), cots, (gated,), (w_down,), ())
    if share:
        acts, mix_part = after((acts, mix_part))
        in_sums = in_grads(acts)
        in_sums, early = after((in_sums, early))
        early_flipped = [flip_shard(values, 1) for values in early]
        down_sums = down_grads(acts)
        down_sums, late, early_flipped = after((down_sums, late, early_flipped))
        grad_moe_in, in_sums, down_sums = after((grad_moe_in, in_sums, down_sums))

    grad_out = cot_low.astype(WIDE)
    if share:
        hidden, grad_moe_in = after((hidden, grad_moe_in))
        plain_mid, scale_mid = rms_parts(hidden)
    grad_hidden = grad_out + rms_back(plain_mid, scale_mid, gain_moe, grad_moe_in)
    gain_moe_sum = jnp.sum(grad_moe_in * plain_mid, axis=0)
    branch_low = grad_hidden.astype(LOW)
    upper = lax.all_gather(branch_low, "shard", axis=0)
    if share:
        late, in_sums, down_sums, branch_low = after((late, in_sums, down_sums, branch_low))
        diagonal = [flip_replica(early[0], 2), flip_replica(late[1], 1)]
        late_flipped = [flip_shard(values, 1) for values in late]
        branch_low, late_flipped = after((branch_low, late_flipped))
        rows = whole(early[0], late[0], early[1], late[1])
        for pair in zip(early_flipped, late_flipped):
            rows = rows + whole(*pair)
        acts = [expert_acts(ids, rows, whole(*far_cots[:2], *far_cots[3:5]), *experts)]
        upper, acts, diagonal = after((upper, acts, diagonal))
        diagonal_flipped = [flip_shard(values, 1) for values in diagonal]
    mix_part, upper = after((mix_part, upper))
    mixture = scatter_sum(mix_part)
    part, gw_low, sum_q, sum_k, sum_n = attend_backward(upper, packets, kept, *heads)

    small = jnp.concatenate(
        [
            grad_router,
            gain_moe_sum[None],
            sum_n / gain_attn,
            jnp.pad(
                jnp.concatenate([sum_q, sum_k], axis=1), ((0, 0), (0, width - 2 * head_dim))
            ),
            jnp.zeros((5, width), WIDE),
        ]
    )
    if share:
        part, gw_low, diagonal_flipped = after((part, gw_low, diagonal_flipped))
        pieces = gw_low.reshape((replicas, -1) + gw_low.shape[1:])
        *act, traded, smalls = expert_acts(
            ids, whole(*diagonal, *diagonal_flipped), whole(far_cots[2], far_cots[5]), *experts,
            trades=((pieces, "rep", replicas, True), (small, "rep", replicas, False)), collective=1,
        )
        act, traded, smalls, part, mixture = after((act, traded, smalls, part, mixture))
        grad_normed = scatter_sum(part)
        low = jnp.sum(traded.astype(WIDE), axis=0).astype(LOW)
        small = jnp.sum(smalls, axis=0)
        *in_sums, found, smalls = in_grads(
            acts, in_sums,
            trades=((low, "rep", replicas, False), (small, "shard", groups, False)), collective=2,
        )
        in_sums, found, smalls, act = after((in_sums, found, smalls, act))
        gw_sum = found.reshape(gw_low.shape)
        small = jnp.sum(smalls, axis=0)
        grad_gate_w, grad_up_w = in_grads([act], in_sums, in_place=False)
        (grad_down,) = down_grads(acts + [act], down_sums)
    else:
        grad_normed = scatter_sum(part)
        over_reps = lax.psum(
            (gw_low,)
            + tuple(values.astype(LOW) for values in in_grads(acts) + down_grads(acts)),
            "rep",
        )
        gw_sum = over_reps[0]
        grad_gate_w, grad_up_w, grad_down = (values.astype(WIDE) for values in over_reps[1:])
        small = lax.psum(small, ("rep", "shard"))
    grads_q, grads_k, grads_v, grads_o = (
        gw_sum[:, i * wide : (i + 1) * wide].astype(WIDE) for i in range(4)
    )
    grad_router = small[:expert_count].T
    grad_gain_moe, grad_gain_attn = (small[expert_count], small[expert_count + 1])
    grad_gain_query, grad_gain_key = (
        small[expert_count + 2, i * head_dim : (i + 1) * head_dim] for i in range(2)
    )
    output = (hidden + mixture).astype(LOW)
    grad_input = grad_hidden + rms_back(plain_in, scale_in, gain_attn, grad_normed)
    return (
        output, grad_input, grad_gain_attn, grad_gain_query, grad_gain_key,
        grads_q, grads_k, grads_v, grads_o.T,
        grad_gain_moe, grad_router, grad_gate_w, grad_up_w, grad_down,
    )


def solution(mesh):
    rows, flat, cols = (P(("rep", "shard"), None), P(), P(None, "shard"))
    lead, experts = (P("shard", None), P("shard", None, None))
    return jax.shard_map(
        local,
        mesh=mesh,
        in_specs=(
            rows, P(("rep", "shard")), rows, flat, flat, flat, cols, cols, cols, lead,
            flat, flat, experts, experts, experts, rows,
        ),
        out_specs=(
            rows, rows, flat, flat, flat, cols, cols, cols, lead,
            flat, flat, experts, experts, experts,
        ),
        check_vma=False,
    )
```

```python
import functools
import math

import jax
import jax.numpy as jnp
from jax import lax
from jax.experimental import pallas as pl
from jax.experimental.pallas import tpu as pltpu
from jax.sharding import PartitionSpec as P

CAP = 144
LINES = 16
EPS_NORM = 1e-06
ROPE_BASE = 50000.0
MASKED = -1e30
VMEM_BYTES = 60 * 1024 * 1024
LOW = jnp.bfloat16
WIDE = jnp.float32
COST = pl.CostEstimate(flops=1 << 20, bytes_accessed=1 << 16, transcendentals=0)


def dot_nn(a, b):
    return lax.dot_general(a, b, (((1,), (0,)), ((), ())), preferred_element_type=WIDE)


def dot_nt(a, b):
    return lax.dot_general(a, b, (((1,), (1,)), ((), ())), preferred_element_type=WIDE)


def dot_tn(a, b):
    return lax.dot_general(a, b, (((0,), (0,)), ((), ())), preferred_element_type=WIDE)


def rope_tables(seq_len, head_dim):
    half_dim = head_dim // 2
    places = jnp.arange(seq_len, dtype=WIDE)
    freqs = ROPE_BASE ** (-jnp.arange(half_dim, dtype=WIDE) * (2.0 / head_dim))
    angles = places[:, None] * freqs[None, :]
    cosine, sine = (jnp.cos(angles), jnp.sin(angles))
    return (
        jnp.concatenate([cosine, cosine], axis=-1),
        jnp.concatenate([-sine, sine], axis=-1),
    )


def head_forward(raw, gain, cos_tab, sin_tab):
    scale = lax.rsqrt(jnp.mean(raw * raw, axis=-1, keepdims=True) + EPS_NORM)
    plain = raw * scale
    scaled = plain * gain
    turned = pltpu.roll(scaled, raw.shape[-1] // 2, axis=1)
    return (scaled * cos_tab + turned * sin_tab, plain, scale)


def head_backward(grad, plain, scale, gain, cos_tab, sin_tab):
    back = grad * cos_tab + pltpu.roll(grad * sin_tab, grad.shape[-1] // 2, axis=1)
    gain_grad = jnp.sum(back * plain, axis=0, keepdims=True)
    back = back * gain
    raw_grad = scale * (back - plain * jnp.mean(back * plain, axis=-1, keepdims=True))
    return (raw_grad, gain_grad)


def soft_weights(query, key, length, score_scale):
    scores = dot_nt(query, key) * score_scale
    places = lax.broadcasted_iota(jnp.int32, scores.shape, 1).astype(WIDE)
    scores = jnp.where(places < length, scores, MASKED)
    expo = jnp.exp(scores - jnp.max(scores, axis=-1, keepdims=True))
    return expo / jnp.sum(expo, axis=-1, keepdims=True)


def attend_block(normed, length, wq, wk, wv, wo, gq, gk, cos_tab, sin_tab, keep):
    head_dim = gq.shape[-1]
    query_raw, key_raw = (dot_nn(normed, wq[...]), dot_nn(normed, wk[...]))
    value = dot_nn(normed, wv[...]).astype(LOW)
    heads = []
    for head in range(query_raw.shape[-1] // head_dim):
        span = slice(head * head_dim, (head + 1) * head_dim)
        query = head_forward(query_raw[:, span], gq, cos_tab, sin_tab)[0].astype(LOW)
        key = head_forward(key_raw[:, span], gk, cos_tab, sin_tab)[0].astype(LOW)
        weights = soft_weights(query, key, length, head_dim**-0.5).astype(LOW)
        heads.append(dot_nn(weights, value[:, span]).astype(LOW))
    joined = heads[0] if len(heads) == 1 else jnp.concatenate(heads, axis=-1)
    keep(query_raw, key_raw, value, joined)
    return dot_nn(joined, wo[...]).astype(LOW)


def attend_kernel(
    pk_ref, wq, wk, wv, wo, gq, gk, cos_ref, sin_ref, part_ref, qr_ref, kr_ref, v_ref, o_ref
):
    rows = pk_ref.shape[1] - LINES
    length = pk_ref[0, rows:, rows : rows + 128].astype(WIDE)[0:1, 0:1]

    def keep(query_raw, key_raw, value, joined):
        qr_ref[0], kr_ref[0], v_ref[0], o_ref[0] = (query_raw, key_raw, value, joined)

    part_ref[0] = attend_block(
        pk_ref[0, :rows], length, wq, wk, wv, wo, gq[...], gk[...], cos_ref[...], sin_ref[...], keep
    )


def whole_spec(array):
    return pl.BlockSpec(array.shape, lambda *_: (0,) * array.ndim, pipeline_mode=pl.Buffered(1))


def first_spec(array):
    return pl.BlockSpec((1,) + array.shape[1:], lambda i: (i,) + (0,) * (array.ndim - 1))


def attend_forward(packets, wq, wk, wv, wo, gq, gk, cos_tab, sin_tab):
    count, lines, width = packets.shape
    rows, wide = (lines - LINES, wq.shape[1])
    fixed = (wq, wk, wv, wo, gq, gk, cos_tab, sin_tab)
    out = (
        jax.ShapeDtypeStruct((count, rows, width), LOW),
        jax.ShapeDtypeStruct((count, rows, wide), WIDE),
        jax.ShapeDtypeStruct((count, rows, wide), WIDE),
        jax.ShapeDtypeStruct((count, rows, wide), LOW),
        jax.ShapeDtypeStruct((count, rows, wide), LOW),
    )
    return pl.pallas_call(
        attend_kernel,
        grid=(count,),
        in_specs=[first_spec(packets)] + [whole_spec(array) for array in fixed],
        out_specs=[first_spec(array) for array in out],
        out_shape=out,
        compiler_params=pltpu.CompilerParams(vmem_limit_bytes=VMEM_BYTES),
        cost_estimate=COST,
        name="attend_forward",
    )(packets, *fixed)


def attend_back_kernel(
    da_ref, pk_ref, qr_ref, kr_ref, v_ref, o_ref,
    wq, wk, wv, wo, gq, gk, cos_ref, sin_ref,
    part_ref, gw_ref, gain_q, gain_k, gain_n, gw_sum,
):
    rows = pk_ref.shape[1] - LINES
    head_dim = gq.shape[-1]
    length = pk_ref[0, rows:, rows : rows + 128].astype(WIDE)[0:1, 0:1]
    cos_tab, sin_tab = (cos_ref[...], sin_ref[...])
    score_scale = head_dim**-0.5

    @pl.when(pl.program_id(0) == 0)
    def _():
        for ref in (gw_sum, gain_q, gain_k, gain_n):
            ref[...] = jnp.zeros_like(ref)

    upper = da_ref[0]
    grad_joined = dot_nt(upper, wo[...]).astype(LOW)
    wide = qr_ref.shape[-1]
    gw_sum[:, 3 * wide :] += dot_tn(upper, o_ref[0])
    grads_q, grads_k, grads_v = ([], [], [])
    for head in range(qr_ref.shape[-1] // head_dim):
        span = slice(head * head_dim, (head + 1) * head_dim)
        query, plain_q, scale_q = head_forward(qr_ref[0, :, span], gq[...], cos_tab, sin_tab)
        key, plain_k, scale_k = head_forward(kr_ref[0, :, span], gk[...], cos_tab, sin_tab)
        query, key, value = (query.astype(LOW), key.astype(LOW), v_ref[0, :, span])
        probs = soft_weights(query, key, length, score_scale)
        grad_out = grad_joined[:, span]
        grads_v.append(dot_tn(probs.astype(LOW), grad_out).astype(LOW))
        grad_probs = dot_nt(grad_out, value)
        inner = jnp.sum(probs * grad_probs, axis=-1, keepdims=True)
        grad_scores = (probs * (grad_probs - inner)).astype(LOW)
        grad_q, head_gain_q = head_backward(
            dot_nn(grad_scores, key) * score_scale, plain_q, scale_q, gq[...], cos_tab, sin_tab
        )
        grad_k, head_gain_k = head_backward(
            dot_tn(grad_scores, query) * score_scale, plain_k, scale_k, gk[...], cos_tab, sin_tab
        )
        gain_q[...] += head_gain_q
        gain_k[...] += head_gain_k
        grads_q.append(grad_q.astype(LOW))
        grads_k.append(grad_k.astype(LOW))
    grads = jnp.concatenate(grads_q + grads_k + grads_v, axis=-1)
    part = (
        dot_nt(grads[:, :wide], wq[...])
        + dot_nt(grads[:, wide : 2 * wide], wk[...])
        + dot_nt(grads[:, 2 * wide :], wv[...])
    )
    normed = pk_ref[0, :rows]
    part_ref[0] = part.astype(LOW)
    gain_n[...] += jnp.sum(part * normed.astype(WIDE), axis=0, keepdims=True)
    gw_sum[:, : 3 * wide] += dot_tn(normed, grads)

    @pl.when(pl.program_id(0) == pl.num_programs(0) - 1)
    def _():
        gw_ref[...] = gw_sum[...].astype(LOW)


def attend_backward(upper, packets, kept, wq, wk, wv, wo, gq, gk, cos_tab, sin_tab):
    count, lines, width = packets.shape
    rows, wide = (lines - LINES, wq.shape[1])
    blocks = (upper, packets) + tuple(kept)
    fixed = (wq, wk, wv, wo, gq, gk, cos_tab, sin_tab)
    sums = tuple(
        jax.ShapeDtypeStruct(shape, kind)
        for shape, kind in (
            ((width, 4 * wide), LOW), (gq.shape, WIDE), (gk.shape, WIDE), ((1, width), WIDE)
        )
    )
    return pl.pallas_call(
        attend_back_kernel,
        grid=(count,),
        in_specs=[first_spec(array) for array in blocks] + [whole_spec(array) for array in fixed],
        out_specs=[first_spec(upper)] + [whole_spec(array) for array in sums],
        out_shape=(jax.ShapeDtypeStruct((count, rows, width), LOW),) + sums,
        scratch_shapes=[pltpu.VMEM((width, 4 * wide), WIDE)],
        compiler_params=pltpu.CompilerParams(vmem_limit_bytes=VMEM_BYTES),
        cost_estimate=COST,
        name="attend_backward",
    )(*blocks, *fixed)


def slot_spots(table, expert):
    row_count = table.shape[1]
    slots = lax.broadcasted_iota(jnp.int32, (CAP, row_count), 0).astype(WIDE) + 1.0
    mine = lax.broadcasted_iota(jnp.int32, table.shape, 0) == expert
    ranks = jnp.sum(jnp.where(mine, table, 0.0), axis=0, keepdims=True)
    return (slots == ranks).astype(LOW)


class Trades:
    def __init__(self, trades):
        self.trades = trades
        self.axes = sorted({(axis, size) for _, axis, size, _ in trades})
        self.arrays = [array for array, _, _, _ in trades]
        self.in_specs = [pl.BlockSpec(memory_space=pltpu.VMEM) for _ in trades]
        self.out_specs = [pl.BlockSpec(memory_space=pl.ANY) for _ in trades]
        self.out_shapes = [
            jax.ShapeDtypeStruct(array.shape if pieces else (size,) + array.shape, array.dtype)
            for array, _, size, pieces in trades
        ]
        self.scratch = [
            pltpu.SemaphoreType.DMA((size,)) for _, _, size, _ in trades for _ in range(2)
        ]

    def bind(self, sources, targets, sems):
        self.sources, self.targets, self.sems = (sources, targets, sems)

    def device(self, axis, size, bits):
        return {axis: lax.rem(lax.axis_index(axis) + bits, size)}

    def copies(self):
        for number, (_, axis, size, pieces) in enumerate(self.trades):
            me = lax.axis_index(axis)
            send, recv = (self.sems[2 * number], self.sems[2 * number + 1])
            target = self.targets[number].at[me]
            for bits in range(size):
                source = self.sources[number]
                source = source.at[lax.rem(me + bits, size)] if pieces else source
                if bits == 0:
                    yield pltpu.make_async_copy(source, target, send.at[0])
                else:
                    yield pltpu.make_async_remote_copy(
                        source, target, send.at[bits], recv.at[bits],
                        device_id=self.device(axis, size, bits),
                        device_id_type=pl.DeviceIdType.MESH,
                    )

    def start(self):
        barrier = pltpu.get_barrier_semaphore()
        for axis, size in self.axes:
            for bits in range(1, size):
                pl.semaphore_signal(
                    barrier, inc=1, device_id=self.device(axis, size, bits),
                    device_id_type=pl.DeviceIdType.MESH,
                )
        pl.semaphore_wait(barrier, sum(size - 1 for _, size in self.axes))
        for copy in self.copies():
            copy.start()

    def finish(self):
        for copy in self.copies():
            copy.wait()


UNIT = 2


def expert_block(
    expert, rows_in, cots_in, wg, wu, wd, wr, x_ref, y_ref, m_ref, dg_ref, du_ref,
    most=256, before=None, behind=None,
):
    row_count, hidden = (rows_in[0].shape[0], wg.shape[-1])
    for seq, (rows, cots) in enumerate(zip(rows_in, cots_in)):
        spots = slot_spots(cots[row_count:, :row_count].astype(WIDE), expert)
        span = pl.ds(seq * CAP, CAP)
        x_ref[span] = dot_nn(spots, rows[...]).astype(LOW)
        y_ref[span] = dot_nn(spots, cots[:row_count]).astype(LOW)
    x_all, y_all = (x_ref[...], y_ref[...])
    logits = dot_nn(x_all, wr[...])
    expo = jnp.exp(logits - jnp.max(logits, axis=-1, keepdims=True))
    chosen = lax.broadcasted_iota(jnp.int32, expo.shape, 1) == expert
    gates = jnp.sum(jnp.where(chosen, expo, 0.0), axis=-1, keepdims=True) / jnp.sum(
        expo, axis=-1, keepdims=True
    )
    step = min(most, hidden)
    dgate = jnp.zeros((x_all.shape[0], 1), WIDE)
    if before is not None:
        before()
    for start in range(0, hidden, step):
        span = slice(start, start + step)
        gate_act, up_act = (dot_nn(x_all, wg[:, span]), dot_nn(x_all, wu[:, span]))
        plain_grad = dot_nt(y_all, wd[span, :])
        sig = jax.nn.sigmoid(gate_act)
        silu = gate_act * sig
        joined = silu * up_act
        dgate += jnp.sum(joined * plain_grad, axis=-1, keepdims=True)
        grad = plain_grad * gates
        m_ref[:, span] = (joined * gates).astype(LOW)
        dg_ref[:, span] = (grad * up_act * (sig + silu * (1.0 - sig))).astype(LOW)
        du_ref[:, span] = (grad * silu).astype(LOW)
    if behind is not None:
        behind()
    return dgate


def expert_kernel(row_spans, cot_spans, batch, trades, ex_ref, wg_in, wu_in, wd_in, wr, *refs):
    first, second = (len(row_spans), len(row_spans) + len(cot_spans))
    rows_in, cots_in = (refs[:first], refs[first:second])
    third, number = (second + len(trades.trades), len(trades.trades))
    x_ref, y_ref, m_ref, dg_ref, du_ref, dgate_ref = refs[third : third + 6]
    scratch = refs[third + 6 + number :]
    rows_buf, cots_buf, sems, wg, wu, wd, weight_sems = scratch[:7]
    trades.bind(refs[second:third], refs[third + 6 : third + 6 + number], scratch[7:])
    steps, units = (sum(count for _, count in row_spans) // batch, batch // UNIT)
    turn = pl.program_id(0) * steps + pl.program_id(1)
    slot = lax.rem(turn, 2)
    row_count = rows_buf.shape[2]

    def copy(kind, source, offset, place, part):
        buffer = (rows_buf, cots_buf)[kind]
        return pltpu.make_async_copy(
            source.at[pl.ds(offset, UNIT)],
            buffer.at[place, pl.ds(part * UNIT, UNIT)],
            sems.at[kind, place, part],
        )

    def fetch(step, place):
        for part in range(units):
            unit = step * units + part
            for kind, sources, spans in ((0, rows_in, row_spans), (1, cots_in, cot_spans)):
                begin = 0
                for source, (offset, count) in zip(sources, spans):
                    size = count // UNIT

                    @pl.when((unit >= begin) & (unit < begin + size))
                    def _(source=source, begin=begin, offset=offset):
                        copy(kind, source, offset + (unit - begin) * UNIT, place, part).start()

                    begin += size

    own = wg_in.shape[0]
    lane, at_step = (pl.program_id(0), pl.program_id(1))

    def weight_copies(expert):
        pairs = ((wg_in, wg), (wu_in, wu), (wd_in, wd))
        return [
            pltpu.make_async_copy(source.at[expert], target, weight_sems.at[i])
            for i, (source, target) in enumerate(pairs)
        ]

    def before():
        @pl.when(at_step == 0)
        def _():
            for item in weight_copies(0):
                item.wait()

    def behind():
        @pl.when((at_step == steps - 1) & (lane < own - 1))
        def _():
            for item in weight_copies(lane + 1):
                item.start()

    @pl.when(turn == 0)
    def _():
        fetch(turn, slot)
        for item in weight_copies(0):
            item.start()
        if number:
            trades.start()

    @pl.when(turn + 1 < pl.num_programs(0) * steps)
    def _():
        fetch(lax.rem(turn + 1, steps), 1 - slot)

    for part in range(units):
        copy(0, rows_in[0], 0, slot, part).wait()
        copy(1, cots_in[0], 0, slot, part).wait()
    dgate = expert_block(
        ex_ref[pl.program_id(0)],
        [rows_buf.at[slot, seq] for seq in range(batch)],
        [cots_buf.at[slot, seq] for seq in range(batch)],
        wg, wu, wd, wr,
        x_ref.at[0], y_ref.at[0], m_ref.at[0], dg_ref.at[0], du_ref.at[0],
        256, before, behind,
    )
    dgate_ref[0] = jnp.broadcast_to(dgate, dgate_ref.shape[1:])
    if number:

        @pl.when(turn == pl.num_programs(0) * steps - 1)
        def _():
            trades.finish()


def expert_acts(ids, rows, cots, wg, wu, wd, wr, batch=4, trades=(), collective=None):
    trades = Trades(trades)
    row_spans, cot_spans = ([span for _, span in items] for items in (rows, cots))
    rows, cots = ([array for array, _ in items] for items in (rows, cots))
    count = sum(size for _, size in row_spans)
    width = rows[0].shape[2]
    own, _, hidden = wg.shape
    out_rows = batch * CAP

    def acts(cols, kind=LOW):
        return jax.ShapeDtypeStruct((own, count * CAP, cols), kind)

    def act_spec(cols):
        return pl.BlockSpec((1, out_rows, cols), lambda e, i: (e, i, 0))

    any_spec = pl.BlockSpec(memory_space=pl.ANY)
    columns = (width, width, hidden, hidden, hidden, 128)
    return pl.pallas_call(
        functools.partial(expert_kernel, row_spans, cot_spans, batch, trades),
        grid=(own, count // batch),
        in_specs=[
            pl.BlockSpec(memory_space=pltpu.SMEM),
            any_spec,
            any_spec,
            any_spec,
            pl.BlockSpec(wr.shape, lambda e, i: (0, 0)),
        ]
        + [any_spec] * (len(rows) + len(cots))
        + trades.in_specs,
        out_specs=[act_spec(cols) for cols in columns] + trades.out_specs,
        out_shape=[acts(cols) for cols in columns[:5]] + [acts(128, WIDE)] + trades.out_shapes,
        scratch_shapes=[
            pltpu.VMEM((2, batch) + rows[0].shape[1:], LOW),
            pltpu.VMEM((2, batch) + cots[0].shape[1:], LOW),
            pltpu.SemaphoreType.DMA((2, 2, batch // UNIT)),
            pltpu.VMEM(wg.shape[1:], LOW),
            pltpu.VMEM(wu.shape[1:], LOW),
            pltpu.VMEM(wd.shape[1:], LOW),
            pltpu.SemaphoreType.DMA((3,)),
        ]
        + trades.scratch,
        compiler_params=pltpu.CompilerParams(
            vmem_limit_bytes=VMEM_BYTES,
            collective_id=collective,
            has_side_effects=collective is not None,
        ),
        cost_estimate=COST,
        name="expert_acts",
    )(ids, wg, wu, wd, wr, *rows, *cots, *trades.arrays)


def pull_block(experts, rows, table, backs, dgates, wr):
    logits = dot_nn(rows, wr[...])
    expo = jnp.exp(logits - jnp.max(logits, axis=-1, keepdims=True))
    probs = expo / jnp.sum(expo, axis=-1, keepdims=True)
    columns = lax.broadcasted_iota(jnp.int32, probs.shape, 1)
    grad_logits = jnp.zeros_like(probs)
    total = jnp.zeros(rows.shape, WIDE)
    for expert, back, dgate in zip(experts, backs, dgates):
        spots = slot_spots(table, expert)
        total += dot_tn(spots, back)
        high = dgate.astype(LOW)
        rest = (dgate - high.astype(WIDE)).astype(LOW)
        at_rows = (dot_tn(spots, high) + dot_tn(spots, rest))[:, : probs.shape[1]]
        chosen = (columns == expert).astype(WIDE)
        prob = jnp.sum(probs * chosen, axis=-1, keepdims=True)
        grad_logits += at_rows * prob * (chosen - probs)
    low_logits = grad_logits.astype(LOW)
    return (total + dot_nt(low_logits, wr[...])).astype(LOW), dot_tn(low_logits, rows)


def pull_kernel(ex_ref, rows_ref, cot_ref, dg_ref, du_ref, dgate_ref, wg, wu, wr, part_ref, router):
    batch, row_count, _ = rows_ref.shape
    own = wg.shape[0]

    @pl.when(pl.program_id(0) == 0)
    def _():
        router[...] = jnp.zeros_like(router)

    backs = [
        (dot_nt(dg_ref[e], wg[e]) + dot_nt(du_ref[e], wu[e])).astype(LOW) for e in range(own)
    ]
    for seq in range(batch):
        span = slice(seq * CAP, (seq + 1) * CAP)
        part_ref[seq], router_part = pull_block(
            [ex_ref[e] for e in range(own)],
            rows_ref[seq],
            cot_ref[seq, :, :row_count].astype(WIDE),
            [back[span] for back in backs],
            [dgate_ref[e, span] for e in range(own)],
            wr,
        )
        router[...] += router_part


def mix_kernel(ex_ref, cot_ref, m_ref, wd, part_ref):
    batch, row_count, _ = part_ref.shape
    own = wd.shape[0]
    outs = [dot_nn(m_ref[e], wd[e]).astype(LOW) for e in range(own)]
    for seq in range(batch):
        table = cot_ref[seq, :, :row_count].astype(WIDE)
        span = slice(seq * CAP, (seq + 1) * CAP)
        total = sum(dot_tn(slot_spots(table, ex_ref[e]), outs[e][span]) for e in range(own))
        part_ref[seq] = total.astype(LOW)


def spread_call(kernel, name, ids, by_seq, cots, by_slot, fixed, router_shape, batch=2):
    count, lines, width = cots.shape
    row_count = lines - LINES
    part = jax.ShapeDtypeStruct((count, row_count, width), LOW)

    def seq_spec(array):
        return pl.BlockSpec((batch,) + array.shape[1:], lambda i: (i, 0, 0))

    def slot_spec(array):
        return pl.BlockSpec((array.shape[0], batch * CAP, array.shape[2]), lambda i: (0, i, 0))

    return pl.pallas_call(
        kernel,
        grid=(count // batch,),
        in_specs=[pl.BlockSpec(memory_space=pltpu.SMEM)]
        + [seq_spec(array) for array in by_seq]
        + [pl.BlockSpec((batch, LINES, width), lambda i: (i, row_count // LINES, 0))]
        + [slot_spec(array) for array in by_slot]
        + [whole_spec(array) for array in fixed],
        out_specs=[seq_spec(part)] + [whole_spec(shape) for shape in router_shape],
        out_shape=[part] + list(router_shape),
        compiler_params=pltpu.CompilerParams(vmem_limit_bytes=VMEM_BYTES),
        cost_estimate=COST,
        name=name,
    )(ids, *by_seq, cots, *by_slot, *fixed)


def weight_grad(lefts, rights, starts=None, trades=(), collective=None, in_place=True):
    own, _, left_cols = lefts[0].shape
    right_cols = rights[0][0].shape[-1]
    sets, outs = (len(lefts), len(rights))
    deep = sum(array.shape[1] for array in lefts)
    tile = min(256 if starts is not None and deep * outs > 4096 else 512, left_cols)
    trades = Trades(trades)
    number, begun = (len(trades.trades), 0 if starts is None else outs)
    first = sets * (1 + outs)

    def kernel(*refs):
        refs, tail = (refs[: first + begun], refs[first + begun :])
        results = tail[number : number + outs]
        trades.bind(
            tail[:number], tail[number + outs : 2 * number + outs], tail[2 * number + outs :]
        )
        if number:

            @pl.when((pl.program_id(0) == 0) & (pl.program_id(1) == 0))
            def _():
                trades.start()

        for place in range(outs):
            total = sum(
                dot_tn(refs[i][0], refs[sets * (1 + place) + i][0]) for i in range(sets)
            )
            results[place][0] = total + refs[first + place][0] if begun else total
        if number:

            @pl.when((pl.program_id(0) == own - 1) & (pl.program_id(1) == left_cols // tile - 1))
            def _():
                trades.finish()

    out_spec = pl.BlockSpec((1, tile, right_cols), lambda e, l: (e, l, 0))
    flat = [array for group in rights for array in group]
    return pl.pallas_call(
        kernel,
        grid=(own, left_cols // tile),
        in_specs=[
            pl.BlockSpec((1, array.shape[1], tile), lambda e, l: (e, 0, l)) for array in lefts
        ]
        + [pl.BlockSpec((1,) + array.shape[1:], lambda e, l: (e, 0, 0)) for array in flat]
        + [out_spec] * begun
        + trades.in_specs,
        out_specs=[out_spec] * outs + trades.out_specs,
        out_shape=[jax.ShapeDtypeStruct((own, left_cols, right_cols), WIDE)] * outs
        + trades.out_shapes,
        scratch_shapes=trades.scratch,
        input_output_aliases={first + place: place for place in range(begun * in_place)},
        compiler_params=pltpu.CompilerParams(
            vmem_limit_bytes=VMEM_BYTES,
            collective_id=collective,
            has_side_effects=collective is not None,
        ),
        cost_estimate=COST,
        name="weight_grad",
    )(*lefts, *flat, *(starts or []), *trades.arrays)


CHUNKS = 4
NEAR_LINES = 128


def each(size, body):
    def step(i, carry):
        body(i)
        return carry

    lax.fori_loop(0, size, step, 0)


def remote(source, target, send, recv, device):
    return pltpu.make_async_remote_copy(
        source, target, send, recv, device_id=device, device_id_type=pl.DeviceIdType.MESH
    )


class Links:
    def __init__(self, replicas, groups):
        rep, shard = (lax.axis_index("rep"), lax.axis_index("shard"))
        self.rail = groups // 2
        self.last = self.rail - 1
        self.shard, self.place, self.core = (shard, shard // 2, shard % 2)
        self.right, self.left = ((rep, shard + 2), (rep, shard - 2))
        self.partner = (rep, shard + 1 - 2 * self.core)
        self.over_x = (rep + 1 - 2 * (rep % 2), shard)
        self.over_y = ((rep + 2) % replicas, shard)

    def greet(self, others):
        barrier = pltpu.get_barrier_semaphore()

        def signal(device):
            pl.semaphore_signal(
                barrier, inc=1, device_id=device, device_id_type=pl.DeviceIdType.MESH
            )

        for device in others:
            signal(device)
        pl.when(self.place < self.last)(lambda: signal(self.right))
        pl.when(self.place > 0)(lambda: signal(self.left))
        inner = (self.place > 0) & (self.place < self.last)
        pl.when(inner)(lambda: pl.semaphore_wait(barrier, len(others) + 2))
        pl.when(jnp.logical_not(inner))(lambda: pl.semaphore_wait(barrier, len(others) + 1))


class Flood:
    def __init__(self, links, view, send, recv, pair, own):
        self.links, self.view, self.own = (links, view, own)
        self.send, self.recv, self.pair = (send, recv, pair)

    def copy(self, way, q, own=False):
        links = self.links
        slot = 2 * q + links.core
        source = self.own if own else self.view.at[slot]
        recv = self.pair.at[q] if way == 2 else self.recv.at[q]
        device = (links.right, links.left, links.partner)[way]
        return remote(source, self.view.at[slot], self.send.at[way, q], recv, device)

    def start(self):
        place = self.links.place

        @pl.when(place < self.links.last)
        def _():
            self.copy(0, place, True).start()

        @pl.when(place > 0)
        def _():
            self.copy(1, place, True).start()

        self.copy(2, place, True).start()

    def onward(self, d, more=None):
        place, last = (self.links.place, self.links.last)

        @pl.when((d > 0) & (place - d >= 0))
        def _():
            q = place - d
            self.copy(0, q).wait_recv()

            @pl.when(place < last)
            def _():
                self.copy(0, q).start()

            self.copy(2, q).start()
            if more is not None:
                more(q)

        @pl.when((d > 0) & (place + d <= last))
        def _():
            q = place + d
            self.copy(1, q).wait_recv()

            @pl.when(place > 0)
            def _():
                self.copy(1, q).start()

            self.copy(2, q).start()
            if more is not None:
                more(q)

    def wait_pair(self, q):
        slot = self.view.at[2 * q + 1 - self.links.core]
        remote(slot, slot, self.send.at[2, q], self.pair.at[q], self.links.partner).wait_recv()

    def finish(self, q):
        place = self.links.place

        @pl.when((place < self.links.last) & (q <= place))
        def _():
            self.copy(0, q).wait_send()

        @pl.when((place > 0) & (q >= place))
        def _():
            self.copy(1, q).wait_send()

        self.copy(2, q).wait_send()


def front_kernel(
    replicas, groups,
    packet, tokens, wq, wk, wv, wo, gq, gk, cos_ref, sin_ref, gain_ref,
    packets, qr_ref, kr_ref, v_ref, o_ref, hidden, low,
    nb, mine, pair_out, pair_in, line_r, line_l,
    n1_send, n1_recv, n1_pair, po_send, po_recv, lr_send, lr_recv, ll_send, ll_recv, keep_sem, own_sem,
):
    links = Links(replicas, groups)
    rail, last, place, core = (links.rail, links.last, links.place, links.core)
    rows = tokens.shape[0]
    step_rows = rows // CHUNKS
    flood = Flood(links, nb, n1_send, n1_recv, n1_pair, packet)
    links.greet([links.partner])
    flood.start()
    own_block = pltpu.make_async_copy(packet, nb.at[links.shard], own_sem.at[0])
    own_block.start()
    own_block.wait()

    def partial_out(q):
        return remote(pair_out.at[q], pair_in.at[q], po_send.at[q], po_recv.at[q], links.partner)

    def chunk_span(chunk):
        return pl.ds(pl.multiple_of(chunk * step_rows, step_rows), step_rows)

    def line(q, chunk, to_right):
        span = chunk_span(chunk)
        target, send, recv, device = (
            (line_r, lr_send, lr_recv, links.right)
            if to_right
            else (line_l, ll_send, ll_recv, links.left)
        )
        return remote(
            mine.at[q, span], target.at[q, span], send.at[q, chunk], recv.at[q, chunk], device
        )

    def add_up(q, chunk, extras):
        span = chunk_span(chunk)
        total = mine[q, span].astype(WIDE) + pair_in[q, span].astype(WIDE)
        for extra in extras:
            total = total + extra[q, span].astype(WIDE)
        return total

    def forward_line(q, to_right, first):
        partial_out(q).wait_recv()

        def body(chunk):
            extras = []
            if not first:
                line(q, chunk, to_right).wait_recv()
                extras = [line_r if to_right else line_l]
            mine[q, chunk_span(chunk)] = add_up(q, chunk, extras).astype(LOW)
            line(q, chunk, to_right).start()

        each(CHUNKS, body)

    def keep_copy(slot):
        return pltpu.make_async_copy(nb.at[slot], packets.at[slot], keep_sem.at[slot])

    def one_distance(d):
        flood.onward(d)

        def one_block(k):
            side, other = (k % 2, k // 2)
            q = place + (2 * side - 1) * d

            @pl.when((q >= 0) & (q <= last) & ((d > 0) | (side == 0)))
            def _():
                @pl.when(other == 1)
                def _():
                    flood.wait_pair(q)

                slot = 2 * q + core + other * (1 - 2 * core)
                keep_copy(slot).start()
                length = nb[slot, rows:, rows : rows + 128].astype(WIDE)[0:1, 0:1]

                def keep(query_raw, key_raw, value, joined):
                    qr_ref[slot], kr_ref[slot] = (query_raw, key_raw)
                    v_ref[slot], o_ref[slot] = (value, joined)

                part = attend_block(
                    nb[slot, :rows], length, wq, wk, wv, wo, gq[...], gk[...],
                    cos_ref[...], sin_ref[...], keep,
                )

                @pl.when(other == 0)
                def _():
                    mine[q] = part

                @pl.when(other == 1)
                def _():
                    pair_out[q] = part
                    partial_out(q).start()

        each(4, one_block)

        @pl.when((place == 0) & (d > 0))
        def _():
            forward_line(d, True, True)

        @pl.when((place == last) & (d > 0))
        def _():
            forward_line(last - d, False, True)

    each(rail, one_distance)

    def rest_right():
        def body(j):
            @pl.when((place > 0) & (place + j <= last))
            def _():
                forward_line(place + j, True, False)

        each(last, lambda i: body(i + 1))

    def rest_left():
        def body(j):
            @pl.when((place < last) & (place - j >= 0))
            def _():
                forward_line(place - j, False, False)

        each(last, lambda i: body(i + 1))

    near_end = place < rail // 2
    pl.when(near_end)(rest_right)
    pl.when(jnp.logical_not(near_end))(rest_left)
    pl.when(near_end)(rest_left)
    pl.when(jnp.logical_not(near_end))(rest_right)
    partial_out(place).wait_recv()

    def finish_rows(chunk):
        @pl.when(place > 0)
        def _():
            line(place, chunk, True).wait_recv()

        @pl.when(place < last)
        def _():
            line(place, chunk, False).wait_recv()

        span = chunk_span(chunk)
        total = tokens[span].astype(WIDE) + add_up(place, chunk, [])
        from_left = jnp.where(place > 0, line_r[place, span].astype(WIDE), 0.0)
        from_right = jnp.where(place < last, line_l[place, span].astype(WIDE), 0.0)
        total = total + from_left + from_right
        hidden[span] = total
        scale = lax.rsqrt(jnp.mean(total * total, axis=-1, keepdims=True) + EPS_NORM)
        low[span] = (total * scale * gain_ref[...]).astype(LOW)

    each(CHUNKS, finish_rows)

    def settle(q):
        flood.finish(q)
        keep_copy(2 * q).wait()
        keep_copy(2 * q + 1).wait()
        partial_out(q).wait_send()

        def chunk_sends(chunk):
            @pl.when((place < last) & (q > place))
            def _():
                line(q, chunk, True).wait_send()

            @pl.when((place > 0) & (q < place))
            def _():
                line(q, chunk, False).wait_send()

        each(CHUNKS, chunk_sends)

    each(rail, settle)


ANY_SPEC = pl.BlockSpec(memory_space=pl.ANY)
FAST_SPEC = pl.BlockSpec(memory_space=pltpu.VMEM)


def shape(*dims, kind=LOW):
    return jax.ShapeDtypeStruct(dims, kind)


def front(replicas, groups, packet, tokens, wq, wk, wv, wo, gq, gk, cos_tab, sin_tab, gain):
    lines, width = packet.shape
    rows, wide, rail = (tokens.shape[0], wq.shape[1], groups // 2)
    block = pltpu.VMEM((rail, rows, width), LOW)
    dma = pltpu.SemaphoreType.DMA
    return pl.pallas_call(
        functools.partial(front_kernel, replicas, groups),
        in_specs=[ANY_SPEC] + [FAST_SPEC] * 10,
        out_specs=[ANY_SPEC] + [FAST_SPEC] * 6,
        out_shape=[
            shape(groups, lines, width),
            shape(groups, rows, wide, kind=WIDE),
            shape(groups, rows, wide, kind=WIDE),
            shape(groups, rows, wide),
            shape(groups, rows, wide),
            shape(rows, width, kind=WIDE),
            shape(rows, width),
        ],
        scratch_shapes=[pltpu.VMEM((groups, lines, width), LOW), block, block, block, block, block]
        + [dma((3, rail)), dma((rail,)), dma((rail,))]
        + [dma((rail,))] * 2
        + [dma((rail, CHUNKS))] * 4
        + [dma((groups,)), dma((1,))],
        compiler_params=pltpu.CompilerParams(
            vmem_limit_bytes=VMEM_BYTES, collective_id=0, has_side_effects=True
        ),
        cost_estimate=COST,
        name="front",
    )(packet, tokens, wq, wk, wv, wo, gq, gk, cos_tab, sin_tab, gain)


def moe_kernel(
    replicas, groups,
    ex_ref, low, cot, wg_in, wu_in, wd_in, wr,
    rows_all, cots, fx, fy, fd, px, py, pd, x_out, y_out, m_out, dg_out, du_out, part_out, router,
    wg, wu, wd, rows_buf, cots_buf, x_s, y_s, m_s, dg_s, du_s, part_s,
    n2_send, n2_recv, n2_pair, cz_send, cz_recv, cz_pair,
    xy_send, xy_recv, dg_send, dg_recv, fl_send, fl_recv, own_sem, load_sem, out_sem, part_sem,
):
    links = Links(replicas, groups)
    rail, last, place, core = (links.rail, links.last, links.place, links.core)
    own, row_count = (wg.shape[0], low.shape[0])
    flood_n2 = Flood(links, rows_all, n2_send, n2_recv, n2_pair, low)
    flood_cot = Flood(links, cots, cz_send, cz_recv, cz_pair, cot)

    def cross(way, q, own_block=False):
        source = cot if own_block else cots.at[2 * q + core]
        target, device = ((fx, links.over_x), (fy, links.over_y))[way]
        return remote(source, target.at[q], xy_send.at[way, q], xy_recv.at[way, q], device)

    def cross_both(q):
        cross(0, q).start()
        cross(1, q).start()

    def diagonal(way, q):
        source, device = ((fx, links.over_y), (fy, links.over_x))[way]
        span = (pl.ds(0, NEAR_LINES), pl.ds(NEAR_LINES, cot.shape[0] - NEAR_LINES))[way]
        return remote(
            source.at[q, span], fd.at[q, span], dg_send.at[way, q], dg_recv.at[way, q], device
        )

    def flip(which, q):
        source, target = ((fx, px), (fy, py), (fd, pd))[which]
        return remote(
            source.at[q], target.at[q], fl_send.at[which, q], fl_recv.at[which, q], links.partner
        )

    def at_distance(d, body):
        @pl.when((d >= 0) & (place - d >= 0))
        def _():
            body(place - d)

        @pl.when((d > 0) & (place + d <= last))
        def _():
            body(place + d)

    def take_cross(q):
        for way in (0, 1):
            cross(way, q).wait_recv()
            diagonal(way, q).start()
            flip(way, q).start()

    def take_diagonal(q):
        for way in (0, 1):
            diagonal(way, q).wait_recv()
        flip(2, q).start()

    links.greet([links.partner, links.over_x, links.over_y])
    flood_cot.start()
    flood_n2.start()
    cross(0, place, True).start()
    cross(1, place, True).start()
    own_copies = (
        pltpu.make_async_copy(low, rows_all.at[links.shard], own_sem.at[0]),
        pltpu.make_async_copy(cot, cots.at[links.shard], own_sem.at[1]),
        pltpu.make_async_copy(wg_in, wg, own_sem.at[2]),
        pltpu.make_async_copy(wu_in, wu, own_sem.at[3]),
        pltpu.make_async_copy(wd_in, wd, own_sem.at[4]),
    )
    for copy in own_copies:
        copy.start()
    router[...] = jnp.zeros_like(router)
    for copy in own_copies:
        copy.wait()

    def out_copies(q):
        span = pl.ds(2 * q * CAP, 2 * CAP)
        pairs = ((x_s, x_out), (y_s, y_out), (m_s, m_out), (dg_s, dg_out), (du_s, du_out))
        return [
            pltpu.make_async_copy(source.at[e], target.at[e, span], out_sem.at[e, i])
            for e in range(own)
            for i, (source, target) in enumerate(pairs)
        ]

    def part_copy(q):
        return pltpu.make_async_copy(part_s, part_out.at[pl.ds(2 * q, 2)], part_sem.at[0])

    near = jnp.where(place <= last - place, place, last - place)
    far_sign = jnp.where(place <= last - place, 1, -1)

    def one_step(k):
        flood_cot.onward(k, cross_both)
        flood_n2.onward(k)
        at_distance(k - 1, take_cross)
        at_distance(k - 2, take_diagonal)
        within = k <= 2 * near
        sign = jnp.where(within & (k % 2 == 1), -far_sign, far_sign)
        q = place + sign * jnp.where(within, (k + 1) // 2, k - near)
        flood_cot.wait_pair(q)
        flood_n2.wait_pair(q)
        loads = (
            pltpu.make_async_copy(rows_all.at[pl.ds(2 * q, 2)], rows_buf, load_sem.at[0]),
            pltpu.make_async_copy(cots.at[pl.ds(2 * q, 2)], cots_buf, load_sem.at[1]),
        )
        for copy in loads:
            copy.start()

        @pl.when(k > 0)
        def _():
            for copy in out_copies(0):
                copy.wait()
            part_copy(0).wait()

        for copy in loads:
            copy.wait()
        dgates, backs = ([], [])
        for e in range(own):
            dgate = expert_block(
                ex_ref[e],
                [rows_buf.at[seq] for seq in range(2)],
                [cots_buf.at[seq] for seq in range(2)],
                wg.at[e], wu.at[e], wd.at[e], wr,
                x_s.at[e], y_s.at[e], m_s.at[e], dg_s.at[e], du_s.at[e],
            )
            dgates.append(jnp.broadcast_to(dgate, (dgate.shape[0], 128)))
            backs.append((dot_nt(dg_s[e], wg[e]) + dot_nt(du_s[e], wu[e])).astype(LOW))
        for copy in out_copies(q):
            copy.start()
        for seq in range(2):
            span = slice(seq * CAP, (seq + 1) * CAP)
            part_s[seq], router_part = pull_block(
                [ex_ref[e] for e in range(own)],
                rows_buf[seq],
                cots_buf[seq, row_count:, :row_count].astype(WIDE),
                [back[span] for back in backs],
                [dgate[span] for dgate in dgates],
                wr,
            )
            router[...] += router_part
        part_copy(q).start()

    each(rail, one_step)
    at_distance(last, take_cross)
    at_distance(last - 1, take_diagonal)
    at_distance(last, take_diagonal)
    for copy in out_copies(0):
        copy.wait()
    part_copy(0).wait()

    def settle(q):
        flood_n2.finish(q)
        flood_cot.finish(q)
        for way in (0, 1):
            cross(way, q).wait_send()
            diagonal(way, q).wait_send()
        for which in (0, 1, 2):
            flip(which, q).wait_send()
            flip(which, q).wait_recv()

    each(rail, settle)


def moe(replicas, groups, ids, low, cot, wg, wu, wd, wr):
    lines, width = cot.shape
    rows, rail = (low.shape[0], groups // 2)
    own, _, hidden = wg.shape
    pair = 2 * CAP
    dma, vmem = (pltpu.SemaphoreType.DMA, pltpu.VMEM)
    acts = [shape(own, groups * CAP, cols) for cols in (width, width, hidden, hidden, hidden)]
    return pl.pallas_call(
        functools.partial(moe_kernel, replicas, groups),
        in_specs=[pl.BlockSpec(memory_space=pltpu.SMEM)]
        + [FAST_SPEC] * 2
        + [ANY_SPEC] * 3
        + [FAST_SPEC],
        out_specs=[ANY_SPEC] * 14 + [FAST_SPEC],
        out_shape=[shape(groups, rows, width), shape(groups, lines, width)]
        + [shape(rail, lines, width)] * 6
        + acts
        + [shape(groups, rows, width), shape(wr.shape[1], width, kind=WIDE)],
        scratch_shapes=[vmem(array.shape, LOW) for array in (wg, wu, wd)]
        + [vmem((2, rows, width), LOW), vmem((2, lines, width), LOW)]
        + [vmem((own, pair, cols), LOW) for cols in (width, width, hidden, hidden, hidden)]
        + [vmem((2, rows, width), LOW)]
        + [dma((3, rail)), dma((rail,)), dma((rail,))] * 2
        + [dma((2, rail))] * 4
        + [dma((3, rail))] * 2
        + [dma((5,)), dma((2,)), dma((own, 5)), dma((1,))],
        compiler_params=pltpu.CompilerParams(
            vmem_limit_bytes=VMEM_BYTES, collective_id=3, has_side_effects=True
        ),
        cost_estimate=COST,
        name="moe",
    )(ids, low, cot, wg, wu, wd, wr)


def rms_parts(values):
    scale = lax.rsqrt(jnp.mean(values * values, axis=-1, keepdims=True) + EPS_NORM)
    return (values * scale, scale)


def rms_back(plain, scale, gain, grad):
    back = grad * gain
    return scale * (back - plain * jnp.mean(back * plain, axis=-1, keepdims=True))


def local(
    tokens, lengths, routes, gain_attn, gain_query, gain_key,
    w_query, w_key, w_value, w_out, gain_moe, w_router,
    w_gate, w_up, w_down, out_grad,
):
    row_count, width = tokens.shape
    head_dim = gain_query.shape[0]
    groups, replicas = (lax.axis_size("shard"), lax.axis_size("rep"))
    expert_count, own = (w_router.shape[1], w_gate.shape[0])
    wide = w_query.shape[1]
    after = lax.optimization_barrier
    gain_q, gain_k = (gain_query.reshape(1, -1), gain_key.reshape(1, -1))
    cos_tab, sin_tab = rope_tables(row_count, head_dim)
    ids = lax.axis_index("shard") * own + jnp.arange(own, dtype=jnp.int32)

    def flip_replica(values, bits):
        return lax.ppermute(values, "rep", [(i, i ^ bits) for i in range(replicas)])

    def flip_shard(values, bits):
        return lax.ppermute(values, "shard", [(i, i ^ bits) for i in range(groups)])

    def scatter_sum(parts):
        return lax.psum_scatter(
            parts.reshape(-1, width), "shard", scatter_dimension=0, tiled=True
        ).astype(WIDE)

    experts = (w_gate, w_up, w_down, w_router)

    def whole(*arrays):
        return [(array, (0, array.shape[0])) for array in arrays]

    def in_grads(acts, grads=None, **more):
        return weight_grad(
            [act[0] for act in acts], [[act[place] for act in acts] for place in (3, 4)], grads, **more
        )

    def down_grads(acts, grads=None):
        return weight_grad([act[2] for act in acts], [[act[1] for act in acts]], grads)

    inputs = tokens.astype(WIDE)
    row_mask = (jnp.arange(row_count, dtype=jnp.int32) < lengths[0])[:, None]
    named = jnp.any(
        routes[None, :, :] == jnp.arange(expert_count, dtype=jnp.int32)[:, None, None], axis=-1
    )
    upto = (jnp.arange(row_count)[:, None] <= jnp.arange(row_count)[None, :]).astype(LOW)
    ranks = jnp.where(named, dot_nn(named.astype(LOW), upto), 0.0).astype(LOW)
    lines = jnp.concatenate(
        [ranks, jnp.broadcast_to(lengths[0].astype(LOW), (expert_count, width - row_count))], axis=1
    )
    plain_in, scale_in = rms_parts(inputs)
    packet = jnp.concatenate([(plain_in * gain_attn).astype(LOW), lines], axis=0)
    cot_low = jnp.where(row_mask, out_grad, 0.0)
    cot_packet = jnp.concatenate([cot_low, lines], axis=0)
    heads = (w_query, w_key, w_value, w_out, gain_q, gain_k, cos_tab, sin_tab)
    share = replicas == 4 and groups == 8
    if share:
        packets, *kept, hidden, low = front(
            replicas, groups, packet, tokens, *heads, gain_moe.reshape(1, -1)
        )
        rows_all, cots, *found = moe(
            replicas, groups, ids, low, cot_packet, w_gate, w_up, w_down, w_router
        )
        far_cots, acts, (pull_part, grad_router) = (found[:6], [found[6:11]], found[11:])
        gated = acts[0][2]
        pairs = rows_all.reshape((groups // 2, 2) + rows_all.shape[1:])
        core = lax.axis_index("shard") % 2
        near = [
            lax.dynamic_slice(pairs, (start, core, 0, 0), (2, 1) + pairs.shape[2:])[:, 0]
            for start in (0, 2)
        ]
        early, late = ([flip_replica(part, bits) for bits in (1, 2)] for part in near)
    else:
        packets = lax.all_gather(packet, "shard", axis=0)
        cot_packet, packets = after((cot_packet, packets))
        cots = lax.all_gather(cot_packet, "shard", axis=0)
        part, *kept = attend_forward(packets, *heads)
        hidden = inputs + scatter_sum(part)
        plain_mid, scale_mid = rms_parts(hidden)
        rows_all = lax.all_gather((plain_mid * gain_moe).astype(LOW), "shard", axis=0)

        acts = [expert_acts(ids, whole(rows_all), whole(cots), *experts)]
        _, _, gated, grad_gate_act, grad_up_act, dgates = acts[0]
        pull_part, grad_router = spread_call(
            pull_kernel, "expert_pull", ids, (rows_all,), cots,
            (grad_gate_act, grad_up_act, dgates), (w_gate, w_up, w_router),
            (jax.ShapeDtypeStruct(w_router.shape[::-1], WIDE),),
        )
    grad_moe_in = scatter_sum(pull_part)
    gated, pull_part = after((gated, pull_part))
    (mix_part,) = spread_call(mix_kernel, "expert_mix", ids, (), cots, (gated,), (w_down,), ())
    if share:
        acts, mix_part = after((acts, mix_part))
        in_sums = in_grads(acts)
        in_sums, early = after((in_sums, early))
        early_flipped = [flip_shard(values, 1) for values in early]
        down_sums = down_grads(acts)
        down_sums, early_flipped = after((down_sums, early_flipped))
        grad_moe_in, in_sums, down_sums = after((grad_moe_in, in_sums, down_sums))

    grad_out = cot_low.astype(WIDE)
    if share:
        hidden, grad_moe_in = after((hidden, grad_moe_in))
        plain_mid, scale_mid = rms_parts(hidden)
    grad_hidden = grad_out + rms_back(plain_mid, scale_mid, gain_moe, grad_moe_in)
    gain_moe_sum = jnp.sum(grad_moe_in * plain_mid, axis=0)
    branch_low = grad_hidden.astype(LOW)
    upper = lax.all_gather(branch_low, "shard", axis=0)
    if share:
        late, in_sums, down_sums, branch_low = after((late, in_sums, down_sums, branch_low))
        diagonal = [flip_replica(early[0], 2), flip_replica(late[1], 1)]
        late_flipped = [flip_shard(values, 1) for values in late]
        rows = whole(early[0], late[0], early[1], late[1], *early_flipped)
        from_pairs = [(array, (0, 2)) for array in far_cots[3:5]]
        acts = [expert_acts(ids, rows, whole(*far_cots[:2]) + from_pairs, *experts)]
        acts, late_flipped = after((acts, late_flipped))
        upper, acts, diagonal = after((upper, acts, diagonal))
        diagonal_flipped = [flip_shard(values, 1) for values in diagonal]
    mix_part, upper = after((mix_part, upper))
    mixture = scatter_sum(mix_part)
    part, gw_low, sum_q, sum_k, sum_n = attend_backward(upper, packets, kept, *heads)

    small = jnp.concatenate(
        [
            grad_router,
            gain_moe_sum[None],
            sum_n / gain_attn,
            jnp.pad(
                jnp.concatenate([sum_q, sum_k], axis=1), ((0, 0), (0, width - 2 * head_dim))
            ),
            jnp.zeros((5, width), WIDE),
        ]
    )
    if share:
        part, gw_low, diagonal_flipped = after((part, gw_low, diagonal_flipped))
        pieces = gw_low.reshape((replicas, -1) + gw_low.shape[1:])
        *act, traded, smalls = expert_acts(
            ids, whole(*late_flipped, *diagonal, *diagonal_flipped),
            [(array, (2, 2)) for array in far_cots[3:5]] + whole(far_cots[2], far_cots[5]), *experts,
            trades=((pieces, "rep", replicas, True), (small, "shard", groups, False)), collective=1,
        )
        act, traded, smalls, part, mixture = after((act, traded, smalls, part, mixture))
        acts.append(act)
        grad_normed = scatter_sum(part)
        low = jnp.sum(traded.astype(WIDE), axis=0).astype(LOW)
        small = jnp.sum(smalls, axis=0)
        found = [low] + [flip_replica(low, bits) for bits in range(1, replicas)]
        other = flip_replica(small, 1)
        grad_gate_w, grad_up_w = in_grads(acts, in_sums)
        grad_gate_w, grad_up_w, found, other, acts = after(
            (grad_gate_w, grad_up_w, found, other, acts)
        )
        small = small + other
        other = flip_replica(small, 2)
        gw_sum = jnp.zeros((replicas,) + low.shape, LOW)
        for bits, piece in enumerate(found):
            gw_sum = lax.dynamic_update_index_in_dim(
                gw_sum, piece, lax.axis_index("rep") ^ bits, axis=0
            )
        gw_sum = gw_sum.reshape(gw_low.shape)
        (grad_down,) = down_grads(acts, down_sums)
        grad_down, other = after((grad_down, other))
        small = small + other
    else:
        grad_normed = scatter_sum(part)
        over_reps = lax.psum(
            (gw_low,)
            + tuple(values.astype(LOW) for values in in_grads(acts) + down_grads(acts)),
            "rep",
        )
        gw_sum = over_reps[0]
        grad_gate_w, grad_up_w, grad_down = (values.astype(WIDE) for values in over_reps[1:])
        small = lax.psum(small, ("rep", "shard"))
    grads_q, grads_k, grads_v, grads_o = (
        gw_sum[:, i * wide : (i + 1) * wide].astype(WIDE) for i in range(4)
    )
    grad_router = small[:expert_count].T
    grad_gain_moe, grad_gain_attn = (small[expert_count], small[expert_count + 1])
    grad_gain_query, grad_gain_key = (
        small[expert_count + 2, i * head_dim : (i + 1) * head_dim] for i in range(2)
    )
    output = (hidden + mixture).astype(LOW)
    grad_input = grad_hidden + rms_back(plain_in, scale_in, gain_attn, grad_normed)
    return (
        output, grad_input, grad_gain_attn, grad_gain_query, grad_gain_key,
        grads_q, grads_k, grads_v, grads_o.T,
        grad_gain_moe, grad_router, grad_gate_w, grad_up_w, grad_down,
    )


def solution(mesh):
    rows, flat, cols = (P(("rep", "shard"), None), P(), P(None, "shard"))
    lead, experts = (P("shard", None), P("shard", None, None))
    return jax.shard_map(
        local,
        mesh=mesh,
        in_specs=(
            rows, P(("rep", "shard")), rows, flat, flat, flat, cols, cols, cols, lead,
            flat, flat, experts, experts, experts, rows,
        ),
        out_specs=(
            rows, rows, flat, flat, flat, cols, cols, cols, lead,
            flat, flat, experts, experts, experts,
        ),
        check_vma=False,
    )
```
